128 devices in a mesh: lon: 32 (over z, y, core), lat: 4 (over x).
Axes of the slice: x: 4, y: 4, z: 4, core: 2. Of those that a mesh axis runs over, the one named last changes fastest.
Arguments:
- forcing: float32 [75, 256, 4096], P(None, 'lat', 'lon'), may hold values from -6 to 6
- obs_values: float32 [75, 1048576], P(None, ('lon', 'lat')), may hold values from -6 to 6
- obs_owner: int32 [1048576], P(('lon', 'lat')), may hold values from 0 to 127, as said below
- obs_cell: int32 [1048576], P(('lon', 'lat')), may hold values from 0 to 8191
- obs_count: int32 [128], P(('lon', 'lat')), may hold values from 1024 to 8192, as said below
- coef_east: float32 [256, 4096], P('lat', 'lon'), may hold values from 0.05 to 0.11
- coef_north: float32 [256, 4096], P('lat', 'lon'), may hold values from 0.05 to 0.11
- area_inv: float32 [256, 4096], P('lat', 'lon'), may hold values from 0.6 to 2
- sea_mask: int32 [256, 4096], P('lat', 'lon'), may hold values 0 or 1
- vert_coef: float32 [74], replicated, may hold values from 0.3 to 0.5
- inv_thick: float32 [75], replicated, may hold values from 0.5 to 0.7
Outputs:
- adjoint_field: float32 [75, 256, 4096], P(None, 'lat', 'lon')
The draws below stay inside these ranges and needn't reach their ends.
Inputs may be any that keep to these rules, and one draw needn't show every extreme that they name: `obs_owner`: owners are numbered lon index times the number of lat devices plus lat index. Among the slots of one device at most 64 go to one owner, and in every draw some owner receives 64 used slots from every device. `obs_count`: slots of a device at or past its count are unused and ignored.
All inputs are finite; a program needn't handle non-finite values. No bound on the sum of `sea_mask` on one device may be relied on, other than what follows from the above.
Results may differ from the reference program's by a relative error of at most 0.0003.
Values sent between devices are 32-bit elements; how exact they have to be, the bound alone decides.
A program may use at most 128 MiB of HBM per device.

```python
import math
import jax
import jax.numpy as jnp
from jax import lax

LEV = 75
CX = 128
CY = 64
STEPS = 4
OBS_DEV = 8192
NX = 4096
NY = 256
CAP = 64
ROWS_ALL = 1048576
N_LAT = 4
DEVICES = 128


def owner_plan(key):
    base = jax.random.fold_in(key, 7)
    shift_key = jax.random.fold_in(base, 1)
    busy_key = jax.random.fold_in(base, 2)
    order_key = jax.random.fold_in(base, 3)
    shifts = jax.random.randint(shift_key, (DEVICES,), 0, 4)
    counts = jnp.right_shift(jnp.full((DEVICES,), OBS_DEV, jnp.int32), shifts.astype(jnp.int32))
    busiest = jax.random.randint(busy_key, (), 0, DEVICES).astype(jnp.int32)
    places = jnp.arange(DEVICES, dtype=jnp.int32)
    counts = jnp.where(places == busiest, OBS_DEV, counts)
    counts = jnp.where(places == (busiest + 1) % DEVICES, OBS_DEV // 8, counts)
    order_keys = jax.random.split(order_key, DEVICES)
    orders = jax.vmap(lambda single: jax.random.permutation(single, OBS_DEV - CAP))(order_keys).astype(jnp.int32)
    others = (busiest + 1 + orders % (DEVICES - 1)) % DEVICES
    owners = jnp.concatenate([jnp.full((DEVICES, CAP), busiest, jnp.int32), others], 1).reshape(-1)
    return (counts.astype(jnp.int32), owners.astype(jnp.int32))


def draw_obs_owner(key, part):
    return owner_plan(key)[1]


def draw_obs_count(key, part):
    return owner_plan(key)[0]


def place_ends(drawn, stream_key, smallest, top_value):
    longest = drawn.shape.index(max(drawn.shape))
    spots = []
    for shift in (0, 1):
        where = [jax.random.randint(jax.random.fold_in(stream_key, axis), (), 0, length) for axis, length in enumerate(drawn.shape)]
        where[longest] = (where[longest] + shift) % drawn.shape[longest]
        spots.append(tuple(where))
    return drawn.at[spots[0]].set(smallest).at[spots[1]].set(top_value)


def level_of(stream_key, shape, cuts, least, top_value):
    level = 1.0
    for position, shards_of in cuts:
        draws = jax.random.uniform(jax.random.fold_in(jax.random.fold_in(stream_key, 6), position), (shards_of,), jnp.float32, least / len(cuts), top_value / len(cuts))
        level = level * jnp.repeat(jnp.exp(draws), shape[position] // shards_of).reshape((-1,) + (1,) * (len(shape) - 1 - position))
    return level


def scatter_about(key, dims, deviation, reach, pieces=(), kind=jnp.bfloat16):
    level = level_of(key, dims, pieces, -0.22, 0.18) if pieces else 1.0
    entries = jax.random.normal(key, dims, jnp.float32) * deviation * level
    return jnp.minimum(jnp.maximum(entries, -reach), reach).astype(kind)


def setup_inputs(seed: int = 0) -> dict:
    keys = jax.random.split(jax.random.key(seed), 12)
    forcing = scatter_about(keys[0], (LEV, NY, NX), 1.0, 6.0, ((1, 4), (2, 32)), jnp.float32)
    obs_values = scatter_about(keys[1], (LEV, ROWS_ALL), 1.0, 6.0, ((1, 128),), jnp.float32)
    obs_owner = draw_obs_owner(jax.random.fold_in(keys[11], 71), 0)
    obs_cell = place_ends(jax.random.randint(keys[3], (ROWS_ALL,), 0, CY * CX), jax.random.fold_in(keys[3], 1), 0, (CY * CX) - 1).astype(jnp.int32)
    obs_count = draw_obs_count(jax.random.fold_in(keys[11], 71), 0)
    coef_east = jnp.clip(jnp.exp(math.log(0.11) - 0.78845734 * jax.random.uniform(keys[5], (NY, NX), jnp.float32) ** level_of(keys[5], (NY, NX), ((0, 4), (1, 32)), -0.2, 0.2)), 0.05, 0.11)
    coef_north = jnp.clip(jnp.exp(math.log(0.11) - 0.78845734 * jax.random.uniform(keys[6], (NY, NX), jnp.float32) ** level_of(keys[6], (NY, NX), ((0, 4), (1, 32)), -0.2, 0.2)), 0.05, 0.11)
    area_inv = jnp.clip(jnp.exp(math.log(2.0) - 1.2039728 * jax.random.uniform(keys[7], (NY, NX), jnp.float32) ** level_of(keys[7], (NY, NX), ((0, 4), (1, 32)), -0.2, 0.2)), 0.6, 2.0)
    sea_mask = place_ends((jax.random.randint(keys[8], (NY, NX), 0, 5) < 4).astype(jnp.int32), jax.random.fold_in(keys[8], 1), 0, 1)
    vert_coef = jnp.clip(jnp.exp(jax.random.uniform(keys[9], (LEV - 1,), jnp.float32, math.log(0.3), math.log(0.5))), 0.3, 0.5)
    inv_thick = jnp.clip(jnp.exp(jax.random.uniform(keys[10], (LEV,), jnp.float32, math.log(0.5), math.log(0.7))), 0.5, 0.7)
    return dict(forcing=forcing, obs_values=obs_values, obs_owner=obs_owner, obs_cell=obs_cell, obs_count=obs_count, coef_east=coef_east, coef_north=coef_north, area_inv=area_inv, sea_mask=sea_mask, vert_coef=vert_coef, inv_thick=inv_thick)


def vertical_inverse(vert_coef, inv_thick):
    empty = jnp.zeros((1,), jnp.float32)
    upper_c = jnp.concatenate([vert_coef, empty])
    lower_c = jnp.concatenate([empty, vert_coef])
    middle = 1.0 + (lower_c + upper_c) * inv_thick
    above = jnp.concatenate([-inv_thick[1:] * vert_coef, empty])
    below = jnp.concatenate([empty, -inv_thick[:-1] * vert_coef])
    ident = jnp.eye(inv_thick.shape[0], dtype=jnp.float32)
    return lax.linalg.tridiagonal_solve(below, middle, above, ident)

def edge_factors(coef_east, coef_north, sea_mask):
    sea = sea_mask.astype(jnp.float32)
    east_sea = jnp.roll(sea, -1, axis=1)
    east_edge = coef_east * sea * east_sea
    west_edge = jnp.roll(east_edge, 1, axis=1)
    zero_row = jnp.zeros_like(sea[:1])
    north_sea = jnp.concatenate([sea[1:], zero_row], 0)
    north_edge = coef_north * sea * north_sea
    south_edge = jnp.concatenate([zero_row, north_edge[:-1]], 0)
    return (east_edge, west_edge, north_edge, south_edge)

def reference(forcing, obs_values, obs_owner, obs_cell, obs_count, coef_east, coef_north, area_inv, sea_mask, vert_coef, inv_thick):
    slot_ids = jnp.arange(OBS_DEV * DEVICES, dtype=jnp.int32)
    source = slot_ids // OBS_DEV
    active = slot_ids % OBS_DEV < obs_count[source]
    lon_block = obs_owner // N_LAT
    lat_block = obs_owner % N_LAT
    grid_row = lat_block * CY + obs_cell // CX
    grid_col = lon_block * CX + obs_cell % CX
    target = (grid_row * NX + grid_col).astype(jnp.int32)
    profiles = jnp.where(active[None, :], obs_values, jnp.zeros_like(obs_values))
    adjoint = forcing.reshape(LEV, NY * NX).at[:, target].add(profiles).reshape(LEV, NY, NX)
    matrix = vertical_inverse(vert_coef, inv_thick)
    east_edge, west_edge, north_edge, south_edge = edge_factors(coef_east, coef_north, sea_mask)
    for repeat in range(STEPS):
        adjoint = jnp.dot(matrix.astype(jnp.float32), adjoint.reshape(LEV, NY * NX).astype(jnp.float32), precision=lax.Precision.HIGHEST, preferred_element_type=jnp.float32).reshape(LEV, NY, NX)
        weighted = area_inv * adjoint
        zero_row = jnp.zeros_like(weighted[:, :1])
        east_g = jnp.roll(weighted, -1, axis=2)
        west_g = jnp.roll(weighted, 1, axis=2)
        north_g = jnp.concatenate([weighted[:, 1:], zero_row], 1)
        south_g = jnp.concatenate([zero_row, weighted[:, :-1]], 1)
        adjoint = adjoint + east_edge * (east_g - weighted) + west_edge * (west_g - weighted) + north_edge * (north_g - weighted) + south_edge * (south_g - weighted)
    return adjoint
```

```python
import jax
import jax.numpy as jnp
from jax import lax
from jax.experimental import pallas as pl
from jax.experimental.pallas import tpu as pltpu
from jax.sharding import PartitionSpec as P

LEV = 75
LP = 80
NX = 128
NY = 64
DEV = 128
CAP = 64
SLOTS = 8192
ROWS = 40
HALO = 4
STRIDE = 53
F32 = jnp.float32
BF16 = jnp.bfloat16
HI = lax.Precision.HIGHEST
MESH = pl.DeviceIdType.MESH


def iota(shape, dim, dtype=jnp.int32):
    return lax.broadcasted_iota(dtype, shape, dim)


def vertical_body(vert_ref, thick_ref, out_ref, cp_ref, dp_ref):
    lane = iota((1, NX), 1)
    dp_ref[...] = jnp.zeros_like(dp_ref)

    def forward(i, carry):
        cp, dp = carry
        up = jnp.where(i < LEV - 1, vert_ref[jnp.minimum(i, LEV - 2)], 0.0)
        low = jnp.where(i > 0, vert_ref[jnp.maximum(i - 1, 0)], 0.0)
        middle = 1.0 + (low + up) * thick_ref[i]
        above = -thick_ref[jnp.minimum(i + 1, LEV - 1)] * up
        below = -thick_ref[jnp.maximum(i - 1, 0)] * low
        inv = 1.0 / (middle - below * cp)
        cp = above * inv
        dp = (jnp.where(lane == i, 1.0, 0.0) - below * dp) * inv
        cp_ref[pl.ds(i, 1), :] = cp
        dp_ref[pl.ds(i, 1), :] = dp
        return cp, dp

    zero = jnp.zeros((1, NX), F32)
    lax.fori_loop(0, LEV, forward, (zero, zero))

    def backward(j, x):
        i = LEV - 1 - j
        x = dp_ref[pl.ds(i, 1), :] - cp_ref[pl.ds(i, 1), :] * x
        dp_ref[pl.ds(i, 1), :] = x
        return x

    lax.fori_loop(0, LEV, backward, zero)
    single = dp_ref[...]
    double = jnp.dot(single, single, precision=HI, preferred_element_type=F32)
    out_ref[...] = jnp.dot(double, double, precision=HI, preferred_element_type=F32)


def vertical_fourth(vert_coef, inv_thick):
    return pl.pallas_call(
        vertical_body,
        out_shape=jax.ShapeDtypeStruct((NX, NX), F32),
        in_specs=[pl.BlockSpec(memory_space=pltpu.SMEM)] * 2,
        out_specs=pl.BlockSpec(memory_space=pltpu.VMEM),
        scratch_shapes=[pltpu.VMEM((NX, NX), F32), pltpu.VMEM((NX, NX), F32)],
        name="vertical",
    )(vert_coef, inv_thick)


def places_body(count_ref, own_ref, idx_ref):
    width = 256
    count = count_ref[0]
    lane = iota((1, width), 1)
    owners = iota((DEV, width), 0)
    tri = (iota((width, width + NX), 0) <= iota((width, width + NX), 1)) | (
        iota((width, width + NX), 1) >= width
    )
    tri = tri.astype(F32).astype(BF16)
    kth = iota((CAP, width), 0).astype(F32)
    number = (iota((CAP, width), 1) + 1).astype(F32)
    acc_lane = iota((DEV, NX), 1)

    def step(b, carry):
        offset, acc = carry
        own = jnp.concatenate([own_ref[pl.ds(2 * b, 1), :], own_ref[pl.ds(2 * b + 1, 1), :]], 1)
        own = jnp.where(lane + b * width < count, own, -1)
        onehot = jnp.where(jnp.broadcast_to(own, (DEV, width)) == owners, 1.0, 0.0)
        ones = onehot.astype(BF16)
        prefix = jnp.dot(ones, tri, preferred_element_type=F32)
        rank = prefix[:, :width] + jnp.concatenate([offset, offset], 1)
        rank = jnp.sum(onehot * rank, axis=0, keepdims=True) - 1.0
        hit = jnp.where(jnp.broadcast_to(rank, (CAP, width)) == kth, 1.0, 0.0)
        both = jnp.concatenate([hit, hit * number], 0).astype(BF16)
        found = lax.dot_general(ones, both, (((1,), (1,)), ((), ())), preferred_element_type=F32)
        scale = jnp.where(acc_lane < CAP, (b * width).astype(F32), 1.0)
        return offset + prefix[:, width:], acc + found * scale

    zero = jnp.zeros((DEV, NX), F32)
    _, acc = lax.fori_loop(0, SLOTS // width, step, (zero, zero), unroll=4)
    total = (acc + pltpu.roll(acc, CAP, 1)).astype(jnp.int32)
    idx_ref[...] = jnp.where(total > 0, total - 1, SLOTS)


def places(owner, count):
    return pl.pallas_call(
        places_body,
        out_shape=jax.ShapeDtypeStruct((DEV, NX), jnp.int32),
        in_specs=[
            pl.BlockSpec(memory_space=pltpu.SMEM),
            pl.BlockSpec(memory_space=pltpu.VMEM),
        ],
        out_specs=pl.BlockSpec(memory_space=pltpu.VMEM),
        name="places",
    )(count, owner.reshape(SLOTS // NX, NX))


def send_body(
    idx_ref, obs_ref, cell_ref, coef_ref,
    recv_ref, row_halo_ref, col_halo_ref, corner_ref,
    table, rows, outbox, colbox, send_sem, recv_sem, side_send, side_recv,
):
    lon = lax.axis_index("lon")
    lat = lax.axis_index("lat")
    z, y, c = lon // 8, (lon // 2) % 4, lon % 2
    me = lon * 4 + lat

    def target(k):
        q = (k * STRIDE) % DEV
        dx, dc, dy, dz = q % 4, (q // 4) % 2, (q // 8) % 4, q // 32
        return (((z + dz) % 4) * 4 + (y + dy) % 4) * 2 + (c + dc) % 2, (lat + dx) % 4

    barrier = pltpu.get_barrier_semaphore()

    def greet(k, _):
        pl.semaphore_signal(barrier, inc=1, device_id=target(k), device_id_type=MESH)
        return 0

    lax.fori_loop(1, DEV, greet, 0)

    def turn(b, _):
        columns = pl.ds(pl.multiple_of(b * NX, NX), NX)
        block = jnp.concatenate(
            [
                obs_ref[:, columns],
                cell_ref[pl.ds(b, 1), :].astype(F32),
                jnp.zeros((NX - LEV - 1, NX), F32),
            ],
            0,
        )
        table[columns, :] = block.T
        return 0

    lax.fori_loop(0, SLOTS // NX, turn, 0)
    table[pl.ds(SLOTS, 8), :] = jnp.zeros((8, NX), F32)

    lane = iota((NY, NX), 1)
    cols = jnp.zeros((NY, NX), F32)
    for i in range(4):
        cols = jnp.where((lane >= 8 * i) & (lane < 8 * i + 4), pltpu.roll(coef_ref[i], 8 * i, 1), cols)
        cols = jnp.where(
            (lane >= 8 * i + 4) & (lane < 8 * i + 8),
            pltpu.roll(coef_ref[i], (8 * i + 4 - 124) % NX, 1),
            cols,
        )
    colbox[...] = cols
    pl.semaphore_wait(barrier, DEV - 1)

    east, west = (lon + 1) % 32, (lon + 31) % 32
    north, south = (lat + 1) % 4, (lat + 3) % 4
    side = []

    def beside(number, src, dst, where):
        copy = pltpu.make_async_remote_copy(
            src_ref=src, dst_ref=dst, send_sem=side_send.at[number], recv_sem=side_recv.at[number],
            device_id=where, device_id_type=MESH,
        )
        copy.start()
        side.append(copy)

    beside(0, coef_ref.at[:, pl.ds(NY - 8, 8), :], row_halo_ref.at[0], (lon, north))
    beside(1, coef_ref.at[:, pl.ds(0, 8), :], row_halo_ref.at[1], (lon, south))
    beside(2, colbox, col_halo_ref.at[0], (east, lat))
    beside(3, colbox, col_halo_ref.at[1], (west, lat))
    beside(4, colbox.at[pl.ds(NY - 8, 8), :], corner_ref.at[0], (east, north))
    beside(5, colbox.at[pl.ds(NY - 8, 8), :], corner_ref.at[1], (west, north))
    beside(6, colbox.at[pl.ds(0, 8), :], corner_ref.at[2], (east, south))
    beside(7, colbox.at[pl.ds(0, 8), :], corner_ref.at[3], (west, south))

    lane8 = iota((8, NX), 1)
    lane32 = iota((32, NX), 1)

    def gather(owner):
        for k in range(CAP):
            rows[pl.ds(k, 1), :] = table[pl.ds(idx_ref[owner, k], 1), :]

    def fold(box):
        box[pl.ds(0, 32), :] = jnp.where(
            lane32 < 64, rows[pl.ds(0, 32), :], pltpu.roll(rows[pl.ds(32, 32), :], 64, 1)
        )
        rest = jnp.zeros((8, NX), F32)
        for g in range(8):
            piece = rows[pl.ds(8 * g, 8), :]
            shift = (16 * g - 64) % NX
            piece = pltpu.roll(piece, shift, 1) if shift else piece
            rest = jnp.where(lane8 // 16 == g, piece, rest)
        box[pl.ds(32, 8), :] = rest

    def send(k, _):
        dlon, dlat = target(k)
        owner = dlon * 4 + dlat
        gather(owner)
        fold(outbox.at[owner])
        pltpu.make_async_remote_copy(
            src_ref=outbox.at[owner], dst_ref=recv_ref.at[me], send_sem=send_sem, recv_sem=recv_sem,
            device_id=(dlon, dlat), device_id_type=MESH,
        ).start()
        return 0

    lax.fori_loop(1, DEV, send, 0)
    gather(me)
    fold(recv_ref.at[me])
    for copy in side:
        copy.wait()
    others = pl.ds(0, DEV - 1)
    pltpu.make_async_copy(outbox.at[others], outbox.at[others], send_sem).wait()
    pltpu.make_async_copy(recv_ref.at[others], recv_ref.at[others], recv_sem).wait()


def send_profiles(idx, obs, cell, coefs):
    vm = pl.BlockSpec(memory_space=pltpu.VMEM)
    return pl.pallas_call(
        send_body,
        out_shape=(
            jax.ShapeDtypeStruct((DEV, ROWS, NX), F32),
            jax.ShapeDtypeStruct((2, 4, 8, NX), F32),
            jax.ShapeDtypeStruct((2, NY, NX), F32),
            jax.ShapeDtypeStruct((4, 8, NX), F32),
        ),
        in_specs=[pl.BlockSpec(memory_space=pltpu.SMEM), vm, vm, vm],
        out_specs=(vm, vm, vm, vm),
        scratch_shapes=[
            pltpu.VMEM((SLOTS + 8, NX), F32),
            pltpu.VMEM((CAP, NX), F32),
            pltpu.VMEM((DEV, ROWS, NX), F32),
            pltpu.VMEM((NY, NX), F32),
            pltpu.SemaphoreType.DMA(()),
            pltpu.SemaphoreType.DMA(()),
            pltpu.SemaphoreType.DMA((8,)),
            pltpu.SemaphoreType.DMA((8,)),
        ],
        compiler_params=pltpu.CompilerParams(
            collective_id=0, has_side_effects=True, vmem_limit_bytes=48 << 20
        ),
        name="send_profiles",
    )(idx, obs, cell.reshape(SLOTS // NX, NX), coefs)


WAYS = 4


def add_body(recv_ref, forcing_ref, out_ref, full, acc0, acc1, acc2, acc3, cell_v, cell_s, sem):
    accs = (acc0, acc1, acc2, acc3)
    pick = jnp.where(
        iota((8, NX), 1) == 16 * iota((8, NX), 0) + (LEV - 64), 1.0, 0.0
    ).astype(F32)

    def cells(b, _):
        part = recv_ref[pl.ds(16 * b, 16), pl.ds(32, 8), :].reshape(NX, NX)
        found = lax.dot_general(
            pick, part, (((1,), (1,)), ((), ())), precision=HI, preferred_element_type=F32
        )
        cell_v[:, pl.ds(pl.multiple_of(b * NX, NX), NX)] = (found + 0.5).astype(jnp.int32)
        return 0

    lax.fori_loop(0, 8, cells, 0, unroll=True)
    copy = pltpu.make_async_copy(cell_v, cell_s, sem)
    copy.start()

    def unfold(s, _):
        rest = recv_ref[s, pl.ds(32, 8), :]
        lane8 = iota((8, NX), 1)
        for g in range(8):
            tail = pltpu.roll(rest, (64 - 16 * g) % NX, 1) if g != 4 else rest
            head = recv_ref[s, pl.ds(8 * (g % 4), 8), :]
            head = pltpu.roll(head, 64, 1) if g >= 4 else head
            full[pl.ds(s * CAP + 8 * g, 8), :] = jnp.where(lane8 < 64, head, tail)
        return 0

    lax.fori_loop(0, DEV, unfold, 0, unroll=2)

    def clear(i, _):
        at = pl.ds(pl.multiple_of(i * 64, 64), 64)
        for acc in accs:
            acc[at, :] = jnp.zeros((64, NX), F32)
        return 0

    lax.fori_loop(0, SLOTS // 64, clear, 0)
    copy.wait()
    per = DEV // WAYS

    def add(s, _):
        for g in range(8):
            for e in range(8):
                for w, acc in enumerate(accs):
                    src = s + w * per
                    cell = cell_s[g, src * 8 + e]
                    at = pl.ds(cell, 1)
                    acc[at, :] = acc[at, :] + full[pl.ds(src * CAP + 8 * g + e, 1), :]
        return 0

    lax.fori_loop(0, per, add, 0)

    def finish(y, _):
        at = pl.ds(pl.multiple_of(y * NX, NX), NX)
        total = (acc0[at, :] + acc1[at, :]) + (acc2[at, :] + acc3[at, :])
        total = total.T
        base = forcing_ref[pl.ds(y, LEV, stride=NY), :]
        out_ref[y, pl.ds(0, LEV), :] = total[:LEV] + base
        out_ref[y, pl.ds(LEV, LP - LEV), :] = jnp.zeros((LP - LEV, NX), F32)
        return 0

    lax.fori_loop(0, NY, finish, 0)


def add_profiles(recv, forcing):
    vm = pl.BlockSpec(memory_space=pltpu.VMEM)
    return pl.pallas_call(
        add_body,
        out_shape=jax.ShapeDtypeStruct((NY, LP, NX), F32),
        in_specs=[vm, vm],
        out_specs=vm,
        scratch_shapes=[pltpu.VMEM((SLOTS, NX), F32)] * 5
        + [
            pltpu.VMEM((8, 8 * DEV), jnp.int32),
            pltpu.SMEM((8, 8 * DEV), jnp.int32),
            pltpu.SemaphoreType.DMA(()),
        ],
        compiler_params=pltpu.CompilerParams(vmem_limit_bytes=56 << 20),
        name="add_profiles",
    )(recv, forcing.reshape(LEV * NY, NX))


YE = NY + 2 * HALO


def spread_body(
    field_ref, coef_ref, row_halo_ref, col_halo_ref, corner_ref,
    out_ref,
    main_a, main_b, side_a, side_b, east_box, west_box, from_west, from_east, corners,
    coef_main, coef_side, fac_main, fac_side, send_sem, recv_sem,
):
    lon = lax.axis_index("lon")
    lat = lax.axis_index("lat")
    east, west = (lon + 1) % 32, (lon + 31) % 32
    north, south = (lat + 1) % 4, (lat + 3) % 4
    peers = [
        (lon, north), (lon, south), (east, lat), (west, lat),
        (east, north), (west, north), (east, south), (west, south),
    ]
    barrier = pltpu.get_barrier_semaphore()
    for peer in peers:
        pl.semaphore_signal(barrier, inc=1, device_id=peer, device_id_type=MESH)

    lane80 = iota((LP, NX), 1)
    for h in range(2):

        def pack(j, carry, h=h):
            e, w = carry
            row = field_ref[32 * h + j]
            here = (lane80 // 4) == j
            e = jnp.where(here, pltpu.roll(row, 4 * j + 4, 1), e)
            w = jnp.where(here, pltpu.roll(row, 4 * j, 1), w)
            return e, w

        zero = jnp.zeros((LP, NX), F32)
        e, w = lax.fori_loop(0, 32, pack, (zero, zero))
        east_box[h] = e
        west_box[h] = w

    pl.semaphore_wait(barrier, 8)
    moves = [
        (field_ref.at[pl.ds(NY - HALO, HALO)], main_a.at[pl.ds(0, HALO)]),
        (field_ref.at[pl.ds(0, HALO)], main_a.at[pl.ds(NY + HALO, HALO)]),
        (east_box, from_west),
        (west_box, from_east),
        (east_box.at[1], corners.at[0]),
        (west_box.at[1], corners.at[1]),
        (east_box.at[0], corners.at[2]),
        (west_box.at[0], corners.at[3]),
    ]
    copies = []
    for number, (src, dst) in enumerate(moves):
        copy = pltpu.make_async_remote_copy(
            src_ref=src, dst_ref=dst, send_sem=send_sem.at[number], recv_sem=recv_sem.at[number],
            device_id=peers[number], device_id_type=MESH,
        )
        copy.start()
        copies.append(copy)

    lane72 = iota((NY, NX), 1)
    lane4 = iota((HALO, NX), 1)
    for i in range(4):
        coef_main[i, pl.ds(HALO, NY), :] = coef_ref[i]
        coef_main[i, pl.ds(0, HALO), :] = row_halo_ref[0, i, pl.ds(4, HALO), :]
        coef_main[i, pl.ds(NY + HALO, HALO), :] = row_halo_ref[1, i, pl.ds(0, HALO), :]

        def sides(lanes, left, right, i=i):
            return jnp.where(
                lanes < 64,
                pltpu.roll(right, (-8 * i) % NX, 1),
                pltpu.roll(left, (124 - 8 * i - 4) % NX, 1),
            )

        coef_side[i, pl.ds(HALO, NY), :] = sides(lane72, col_halo_ref[0], col_halo_ref[1])
        coef_side[i, pl.ds(0, HALO), :] = sides(lane4, corner_ref[0, pl.ds(4, HALO), :], corner_ref[1, pl.ds(4, HALO), :])
        coef_side[i, pl.ds(NY + HALO, HALO), :] = sides(lane4, corner_ref[2, pl.ds(0, HALO), :], corner_ref[3, pl.ds(0, HALO), :])
    outside = jnp.logical_or(
        (iota((YE, NX), 0) < HALO) & (lat == 0), (iota((YE, NX), 0) >= NY + HALO) & (lat == 3)
    )
    coef_main[3] = jnp.where(outside, 0.0, coef_main[3])
    coef_side[3] = jnp.where(outside, 0.0, coef_side[3])

    def shifts(main, side, lanes):
        first, last = lanes == 0, lanes == NX - 1
        main_e = pltpu.roll(jnp.where(first, side, main), NX - 1, 1)
        side_e = pltpu.roll(jnp.where(first, main, side), NX - 1, 1)
        main_w = pltpu.roll(jnp.where(last, side, main), 1, 1)
        side_w = pltpu.roll(jnp.where(last, main, side), 1, 1)
        return main_e, side_e, main_w, side_w

    lanes = iota((YE, NX), 1)
    sea_m, sea_s = coef_main[3], coef_side[3]
    area_m, area_s = coef_main[2], coef_side[2]
    sea_me, sea_se, _, _ = shifts(sea_m, sea_s, lanes)
    east_m = coef_main[0] * sea_m * sea_me
    east_s = coef_side[0] * sea_s * sea_se
    _, _, west_m, west_s = shifts(east_m, east_s, lanes)
    area_me, area_se, area_mw, area_sw = shifts(area_m, area_s, lanes)

    def upward(x):
        return pltpu.roll(x, YE - 1, 0)

    def downward(x):
        return pltpu.roll(x, 1, 0)

    for fac, coef, ee, ww, sea, area, area_e, area_w in (
        (fac_main, coef_main, east_m, west_m, sea_m, area_m, area_me, area_mw),
        (fac_side, coef_side, east_s, west_s, sea_s, area_s, area_se, area_sw),
    ):
        nn = coef[1] * sea * upward(sea)
        ss = downward(nn)
        fac[0] = 1.0 - area * (ee + ww + nn + ss)
        fac[1] = ee * area_e
        fac[2] = ww * area_w
        fac[3] = nn * upward(area)
        fac[4] = ss * downward(area)

    def own(y, _):
        main_a[y + HALO] = field_ref[y]
        return 0

    lax.fori_loop(0, NY, own, 0)
    for copy in copies:
        copy.wait()

    def unpack(j, _):
        for h in range(2):
            side_a[HALO + 32 * h + j] = jnp.where(
                lane80 < 64,
                pltpu.roll(from_east[h], (NX - 4 * j) % NX, 1),
                pltpu.roll(from_west[h], (124 - 4 * j + NX) % NX, 1),
            )
        return 0

    lax.fori_loop(0, 32, unpack, 0)
    for j in range(HALO):
        k = 28 + j
        side_a[j] = jnp.where(
            lane80 < 64,
            pltpu.roll(corners[1], (NX - 4 * k) % NX, 1),
            pltpu.roll(corners[0], (124 - 4 * k) % NX, 1),
        )
        side_a[NY + HALO + j] = jnp.where(
            lane80 < 64,
            pltpu.roll(corners[3], (NX - 4 * j) % NX, 1),
            pltpu.roll(corners[2], (124 - 4 * j) % NX, 1),
        )

    first80, last80 = lane80 == 0, lane80 == NX - 1
    for t in range(4):
        src_m, src_s = (main_a, side_a) if t % 2 == 0 else (main_b, side_b)
        dst_m, dst_s = (main_b, side_b) if t % 2 == 0 else (main_a, side_a)
        final = t == 3

        def row(y, _):
            main, side = src_m[y], src_s[y]

            def fac(ref, i):
                return jnp.broadcast_to(ref[i, pl.ds(y, 1), :], (LP, NX))

            main_e = pltpu.roll(jnp.where(first80, side, main), NX - 1, 1)
            main_w = pltpu.roll(jnp.where(last80, side, main), 1, 1)
            new = (
                fac(fac_main, 0) * main
                + fac(fac_main, 1) * main_e
                + fac(fac_main, 2) * main_w
                + fac(fac_main, 3) * src_m[y + 1]
                + fac(fac_main, 4) * src_m[y - 1]
            )
            if final:
                out_ref[y - HALO] = new
            else:
                dst_m[y] = new
                side_e = pltpu.roll(jnp.where(first80, main, side), NX - 1, 1)
                side_w = pltpu.roll(jnp.where(last80, main, side), 1, 1)
                dst_s[y] = (
                    fac(fac_side, 0) * side
                    + fac(fac_side, 1) * side_e
                    + fac(fac_side, 2) * side_w
                    + fac(fac_side, 3) * src_s[y + 1]
                    + fac(fac_side, 4) * src_s[y - 1]
                )
            return 0

        lax.fori_loop(1 + t, YE - 1 - t, row, 0)


def spread(field, coefs, row_halo, col_halo, corner):
    vm = pl.BlockSpec(memory_space=pltpu.VMEM)
    wide = pltpu.VMEM((YE, LP, NX), F32)
    box = pltpu.VMEM((2, LP, NX), F32)
    return pl.pallas_call(
        spread_body,
        out_shape=jax.ShapeDtypeStruct((NY, LP, NX), F32),
        in_specs=[vm] * 5,
        out_specs=vm,
        scratch_shapes=[
            wide, wide, wide, wide, box, box, box, box,
            pltpu.VMEM((4, LP, NX), F32),
            pltpu.VMEM((4, YE, NX), F32),
            pltpu.VMEM((4, YE, NX), F32),
            pltpu.VMEM((5, YE, NX), F32),
            pltpu.VMEM((5, YE, NX), F32),
            pltpu.SemaphoreType.DMA((8,)),
            pltpu.SemaphoreType.DMA((8,)),
        ],
        compiler_params=pltpu.CompilerParams(
            collective_id=1, has_side_effects=True, vmem_limit_bytes=48 << 20
        ),
        name="spread",
    )(field, coefs, row_halo, col_halo, corner)


def solve_body(matrix_ref, field_ref, out_ref):
    matrix = matrix_ref[pl.ds(0, LP), pl.ds(0, LP)]

    def row(y, _):
        product = jnp.dot(matrix, field_ref[y], precision=HI, preferred_element_type=F32)
        out_ref[pl.ds(y, LEV, stride=NY), :] = product[:LEV]
        return 0

    lax.fori_loop(0, NY, row, 0, unroll=2)


def solve_columns(matrix, field):
    vm = pl.BlockSpec(memory_space=pltpu.VMEM)
    return pl.pallas_call(
        solve_body,
        out_shape=jax.ShapeDtypeStruct((LEV * NY, NX), F32),
        in_specs=[vm, vm],
        out_specs=vm,
        compiler_params=pltpu.CompilerParams(vmem_limit_bytes=32 << 20),
        name="solve_columns",
    )(matrix, field)


def local(
    forcing, obs_values, obs_owner, obs_cell, obs_count,
    coef_east, coef_north, area_inv, sea_mask, vert_coef, inv_thick,
):
    matrix = vertical_fourth(vert_coef, inv_thick)
    coefs = jnp.stack([coef_east, coef_north, area_inv, sea_mask.astype(F32)])
    idx = places(obs_owner, obs_count)
    recv, row_halo, col_halo, corner = send_profiles(idx, obs_values, obs_cell, coefs)
    field = add_profiles(recv, forcing)
    field = spread(field, coefs, row_halo, col_halo, corner)
    return solve_columns(matrix, field).reshape(LEV, NY, NX)


def solution(mesh):
    lead = P(("lon", "lat"))
    flat = P("lat", "lon")
    in_specs = (
        P(None, "lat", "lon"), P(None, ("lon", "lat")), lead, lead, lead,
        flat, flat, flat, flat, P(), P(),
    )
    return jax.shard_map(
        local, mesh=mesh, in_specs=in_specs, out_specs=P(None, "lat", "lon"), check_vma=False
    )
```

```python
import jax
import jax.numpy as jnp
from jax import lax
from jax.experimental import pallas as pl
from jax.experimental.pallas import tpu as pltpu
from jax.sharding import PartitionSpec as P

LEV = 75
LP = 80
NX = 128
NY = 64
DEV = 128
CAP = 64
SLOTS = 8192
ROWS = 40
HALO = 4
YE = NY + 2 * HALO
Q = 18
STRIDE = 27
F32 = jnp.float32
BF16 = jnp.bfloat16
HI = lax.Precision.HIGHEST
MESH = pl.DeviceIdType.MESH


def iota(shape, dim, dtype=jnp.int32):
    return lax.broadcasted_iota(dtype, shape, dim)


def vertical_fourth(vert_ref, thick_ref, out_ref, cp_ref, dp_ref):
    lane = iota((1, NX), 1)
    dp_ref[...] = jnp.zeros_like(dp_ref)

    def forward(i, carry):
        cp, dp = carry
        up = jnp.where(i < LEV - 1, vert_ref[jnp.minimum(i, LEV - 2)], 0.0)
        low = jnp.where(i > 0, vert_ref[jnp.maximum(i - 1, 0)], 0.0)
        middle = 1.0 + (low + up) * thick_ref[i]
        above = -thick_ref[jnp.minimum(i + 1, LEV - 1)] * up
        below = -thick_ref[jnp.maximum(i - 1, 0)] * low
        inv = 1.0 / (middle - below * cp)
        cp = above * inv
        dp = (jnp.where(lane == i, 1.0, 0.0) - below * dp) * inv
        cp_ref[pl.ds(i, 1), :] = cp
        dp_ref[pl.ds(i, 1), :] = dp
        return cp, dp

    zero = jnp.zeros((1, NX), F32)
    lax.fori_loop(0, LEV, forward, (zero, zero))

    def backward(j, x):
        i = LEV - 1 - j
        x = dp_ref[pl.ds(i, 1), :] - cp_ref[pl.ds(i, 1), :] * x
        dp_ref[pl.ds(i, 1), :] = x
        return x

    lax.fori_loop(0, LEV, backward, zero)
    single = dp_ref[...]
    double = jnp.dot(single, single, precision=HI, preferred_element_type=F32)
    out_ref[...] = jnp.dot(double, double, precision=HI, preferred_element_type=F32)


def places(count, own_ref, idx_ref):
    width = 256
    lane = iota((1, width), 1)
    owners = iota((DEV, width), 0)
    tri = (iota((width, width + NX), 0) <= iota((width, width + NX), 1)) | (
        iota((width, width + NX), 1) >= width
    )
    tri = tri.astype(F32).astype(BF16)
    kth = iota((CAP, width), 0).astype(F32)
    number = (iota((CAP, width), 1) + 1).astype(F32)
    acc_lane = iota((DEV, NX), 1)

    def step(b, carry):
        offset, acc = carry
        own = jnp.concatenate([own_ref[pl.ds(2 * b, 1), :], own_ref[pl.ds(2 * b + 1, 1), :]], 1)
        own = jnp.where(lane + b * width < count, own, -1)
        onehot = jnp.where(jnp.broadcast_to(own, (DEV, width)) == owners, 1.0, 0.0)
        ones = onehot.astype(BF16)
        prefix = jnp.dot(ones, tri, preferred_element_type=F32)
        rank = prefix[:, :width] + jnp.concatenate([offset, offset], 1)
        rank = jnp.sum(onehot * rank, axis=0, keepdims=True) - 1.0
        hit = jnp.where(jnp.broadcast_to(rank, (CAP, width)) == kth, 1.0, 0.0)
        both = jnp.concatenate([hit, hit * number], 0).astype(BF16)
        found = lax.dot_general(ones, both, (((1,), (1,)), ((), ())), preferred_element_type=F32)
        scale = jnp.where(acc_lane < CAP, (b * width).astype(F32), 1.0)
        return offset + prefix[:, width:], acc + found * scale

    zero = jnp.zeros((DEV, NX), F32)
    _, acc = lax.fori_loop(0, SLOTS // width, step, (zero, zero), unroll=4)
    total = (acc + pltpu.roll(acc, CAP, 1)).astype(jnp.int32)
    idx_ref[...] = jnp.clip(jnp.where(total > 0, total - 1, SLOTS), 0, SLOTS)


def factors(coef_refs, row_halo_ref, col_halo_ref, corner_ref, coef_main, coef_side, fac_main_ref, fac_strip_ref):
    lat = lax.axis_index("lat")
    lane64 = iota((NY, NX), 1)
    lane4 = iota((HALO, NX), 1)
    for i in range(4):
        coef_main[i, pl.ds(HALO, NY), :] = coef_refs[i][...].astype(F32)
        coef_main[i, pl.ds(0, HALO), :] = row_halo_ref[0, i, pl.ds(4, HALO), :]
        coef_main[i, pl.ds(NY + HALO, HALO), :] = row_halo_ref[1, i, pl.ds(0, HALO), :]

        def sides(lanes, left, right, i=i):
            return jnp.where(
                lanes < 64,
                pltpu.roll(right, (-8 * i) % NX, 1),
                pltpu.roll(left, (124 - 8 * i - 4) % NX, 1),
            )

        coef_side[i, pl.ds(HALO, NY), :] = sides(lane64, col_halo_ref[0], col_halo_ref[1])
        coef_side[i, pl.ds(0, HALO), :] = sides(
            lane4, corner_ref[0, pl.ds(4, HALO), :], corner_ref[1, pl.ds(4, HALO), :]
        )
        coef_side[i, pl.ds(NY + HALO, HALO), :] = sides(
            lane4, corner_ref[2, pl.ds(0, HALO), :], corner_ref[3, pl.ds(0, HALO), :]
        )
    row = iota((YE, NX), 0)
    first_row = jnp.where(lat == 0, HALO, 0)
    last_row = jnp.where(lat == 3, NY + HALO, YE)
    inside = (row >= first_row) & (row < last_row)
    lanes = iota((YE, NX), 1)

    def shifts(main, side):
        first, last = lanes == 0, lanes == NX - 1
        main_e = pltpu.roll(jnp.where(first, side, main), NX - 1, 1)
        side_e = pltpu.roll(jnp.where(first, main, side), NX - 1, 1)
        main_w = pltpu.roll(jnp.where(last, side, main), 1, 1)
        side_w = pltpu.roll(jnp.where(last, main, side), 1, 1)
        return main_e, side_e, main_w, side_w

    sea_m = jnp.where(inside, coef_main[3], 0.0)
    sea_s = jnp.where(inside, coef_side[3], 0.0)
    area_m, area_s = coef_main[2], coef_side[2]
    sea_me, sea_se, _, _ = shifts(sea_m, sea_s)
    east_m = coef_main[0] * sea_m * sea_me
    east_s = coef_side[0] * sea_s * sea_se
    _, _, west_m, west_s = shifts(east_m, east_s)
    area_me, area_se, area_mw, area_sw = shifts(area_m, area_s)

    def five(north_coef, ee, ww, sea, area, area_e, area_w):
        nn = north_coef * sea * pltpu.roll(sea, YE - 1, 0)
        ss = pltpu.roll(nn, 1, 0)
        return (
            1.0 - area * (ee + ww + nn + ss),
            ee * area_e,
            ww * area_w,
            nn * pltpu.roll(area, YE - 1, 0),
            ss * pltpu.roll(area, 1, 0),
        )

    mains = five(coef_main[1], east_m, west_m, sea_m, area_m, area_me, area_mw)
    sides = five(coef_side[1], east_s, west_s, sea_s, area_s, area_se, area_sw)
    laneq = iota((Q, NX), 1)
    group, place = laneq // 32, laneq % 32
    gap = ((place >= 12) & (place < 16)) | (place >= 28)
    for i in range(5):
        fac_main_ref[i] = mains[i]
        coef_main[0] = jnp.where(lanes < 64, sides[i], mains[i])
        coef_main[1] = jnp.where(lanes < 64, mains[i], sides[i])
        strip = jnp.zeros((Q, NX), F32)
        for j in range(4):
            own = pl.ds(Q * j, Q)
            near = pltpu.roll(coef_main[0, own, :], (32 * j + 8) % NX, 1)
            far = pltpu.roll(coef_main[1, own, :], (32 * j + 20) % NX, 1)
            strip = jnp.where(group == j, jnp.where(place < 14, near, far), strip)
        fac_strip_ref[i, pl.ds(0, Q), :] = jnp.where(gap, 0.0, strip)


def send_body(
    count_ref, vert_ref, thick_ref, own_ref, obs_ref, cell_ref, east_ref, north_ref, area_ref, sea_ref,
    recv_ref, fac_main_ref, fac_strip_ref, matrix_ref,
    table, rows, outbox, coef_box, colbox, row_halo, col_halo, corner, coef_main, coef_side,
    cp_ref, dp_ref, idx_v, idx_ref, idx_sem, send_sem, recv_sem, side_send, side_recv,
):
    lon = lax.axis_index("lon")
    lat = lax.axis_index("lat")
    z, y, c = lax.div(lon, 8), lax.rem(lax.div(lon, 2), 4), lax.rem(lon, 2)
    me = lon * 4 + lat

    def target(k):
        q = lax.rem(k * STRIDE, DEV)
        dx, dc = lax.rem(q, 4), lax.rem(lax.div(q, 4), 2)
        dy, dz = lax.rem(lax.div(q, 8), 4), lax.div(q, 32)
        there = (lax.rem(z + dz, 4) * 4 + lax.rem(y + dy, 4)) * 2 + lax.rem(c + dc, 2)
        return there, lax.rem(lat + dx, 4)

    barrier = pltpu.get_barrier_semaphore()

    def greet(k, _):
        pl.semaphore_signal(barrier, inc=1, device_id=target(k), device_id_type=MESH)
        return 0

    lax.fori_loop(1, DEV, greet, 0)

    places(count_ref[0], own_ref, idx_v)
    idx_copy = pltpu.make_async_copy(idx_v, idx_ref, idx_sem)
    idx_copy.start()

    def turn(b, _):
        columns = pl.ds(pl.multiple_of(b * NX, NX), NX)
        block = jnp.concatenate(
            [
                obs_ref[:, columns],
                cell_ref[pl.ds(b, 1), :].astype(F32),
                jnp.zeros((NX - LEV - 1, NX), F32),
            ],
            0,
        )
        table[columns, :] = block.T
        return 0

    lax.fori_loop(0, SLOTS // NX, turn, 0, unroll=4)
    table[pl.ds(SLOTS, 8), :] = jnp.zeros((8, NX), F32)

    lane = iota((NY, NX), 1)
    cols = jnp.zeros((NY, NX), F32)
    coef_refs = (east_ref, north_ref, area_ref, sea_ref)
    for i in range(4):
        whole = coef_refs[i][...].astype(F32)
        coef_box[i, pl.ds(0, 8), :] = whole[:8]
        coef_box[i, pl.ds(8, 8), :] = whole[NY - 8:]
        cols = jnp.where((lane >= 8 * i) & (lane < 8 * i + 4), pltpu.roll(whole, 8 * i, 1), cols)
        cols = jnp.where(
            (lane >= 8 * i + 4) & (lane < 8 * i + 8),
            pltpu.roll(whole, (8 * i + 4 - 124) % NX, 1),
            cols,
        )
    colbox[...] = cols
    idx_copy.wait()
    pl.semaphore_wait(barrier, DEV - 1)

    east, west = lax.rem(lon + 1, 32), lax.rem(lon + 31, 32)
    north, south = lax.rem(lat + 1, 4), lax.rem(lat + 3, 4)
    side = []

    def beside(number, src, dst, where):
        copy = pltpu.make_async_remote_copy(
            src_ref=src, dst_ref=dst, send_sem=side_send.at[number], recv_sem=side_recv.at[number],
            device_id=where, device_id_type=MESH,
        )
        copy.start()
        side.append(copy)

    beside(0, coef_box.at[:, pl.ds(8, 8), :], row_halo.at[0], (lon, north))
    beside(1, coef_box.at[:, pl.ds(0, 8), :], row_halo.at[1], (lon, south))
    beside(2, colbox, col_halo.at[0], (east, lat))
    beside(3, colbox, col_halo.at[1], (west, lat))
    beside(4, colbox.at[pl.ds(NY - 8, 8), :], corner.at[0], (east, north))
    beside(5, colbox.at[pl.ds(NY - 8, 8), :], corner.at[1], (west, north))
    beside(6, colbox.at[pl.ds(0, 8), :], corner.at[2], (east, south))
    beside(7, colbox.at[pl.ds(0, 8), :], corner.at[3], (west, south))

    lane8 = iota((8, NX), 1)
    lane32 = iota((32, NX), 1)

    def gather(owner):
        for k in range(CAP):
            at = jnp.minimum(jnp.maximum(idx_ref[owner, k], 0), SLOTS)
            rows[pl.ds(k, 1), :] = table[pl.ds(at, 1), :]

    def fold(box):
        box[pl.ds(0, 32), :] = jnp.where(
            lane32 < 64, rows[pl.ds(0, 32), :], pltpu.roll(rows[pl.ds(32, 32), :], 64, 1)
        )
        rest = jnp.zeros((8, NX), F32)
        for g in range(8):
            piece = rows[pl.ds(8 * g, 8), :]
            shift = (16 * g - 64) % NX
            piece = pltpu.roll(piece, shift, 1) if shift else piece
            rest = jnp.where(lane8 // 16 == g, piece, rest)
        box[pl.ds(32, 8), :] = rest

    def send(k, _):
        dlon, dlat = target(k)
        owner = dlon * 4 + dlat
        gather(owner)
        fold(outbox.at[owner])
        pltpu.make_async_remote_copy(
            src_ref=outbox.at[owner], dst_ref=recv_ref.at[me], send_sem=send_sem, recv_sem=recv_sem,
            device_id=(dlon, dlat), device_id_type=MESH,
        ).start()
        return 0

    lax.fori_loop(1, DEV, send, 0)
    gather(me)
    fold(recv_ref.at[me])
    vertical_fourth(vert_ref, thick_ref, matrix_ref, cp_ref, dp_ref)
    for copy in side:
        copy.wait()
    factors(coef_refs, row_halo, col_halo, corner, coef_main, coef_side, fac_main_ref, fac_strip_ref)
    others = pl.ds(0, DEV - 1)
    pltpu.make_async_copy(outbox.at[others], outbox.at[others], send_sem).wait()
    pltpu.make_async_copy(recv_ref.at[others], recv_ref.at[others], recv_sem).wait()


def send_profiles(count, vert_coef, inv_thick, owner, obs, cell, coefs):
    vm = pl.BlockSpec(memory_space=pltpu.VMEM)
    sm = pl.BlockSpec(memory_space=pltpu.SMEM)
    plane = pltpu.VMEM((4, YE, NX), F32)
    return pl.pallas_call(
        send_body,
        out_shape=(
            jax.ShapeDtypeStruct((DEV, ROWS, NX), F32),
            jax.ShapeDtypeStruct((5, YE, NX), F32),
            jax.ShapeDtypeStruct((5, 24, NX), F32),
            jax.ShapeDtypeStruct((NX, NX), F32),
        ),
        in_specs=[sm] * 3 + [vm] * 7,
        out_specs=(vm,) * 4,
        scratch_shapes=[
            pltpu.VMEM((SLOTS + 8, NX), F32),
            pltpu.VMEM((CAP, NX), F32),
            pltpu.VMEM((DEV, ROWS, NX), F32),
            pltpu.VMEM((4, 16, NX), F32),
            pltpu.VMEM((NY, NX), F32),
            pltpu.VMEM((2, 4, 8, NX), F32),
            pltpu.VMEM((2, NY, NX), F32),
            pltpu.VMEM((4, 8, NX), F32),
            plane,
            plane,
            pltpu.VMEM((NX, NX), F32),
            pltpu.VMEM((NX, NX), F32),
            pltpu.VMEM((DEV, NX), jnp.int32),
            pltpu.SMEM((DEV, NX), jnp.int32),
            pltpu.SemaphoreType.DMA(()),
            pltpu.SemaphoreType.DMA(()),
            pltpu.SemaphoreType.DMA(()),
            pltpu.SemaphoreType.DMA((8,)),
            pltpu.SemaphoreType.DMA((8,)),
        ],
        compiler_params=pltpu.CompilerParams(
            collective_id=0, has_side_effects=True, vmem_limit_bytes=48 << 20
        ),
        name="send_profiles",
    )(
        count, vert_coef, inv_thick, owner.reshape(SLOTS // NX, NX), obs,
        cell.reshape(SLOTS // NX, NX), *coefs,
    )


WAYS = 4


def add_body(recv_ref, forcing_ref, matrix_ref, out_ref, full, acc0, acc1, acc2, acc3, cell_v, cell_s, sem):
    accs = (acc0, acc1, acc2, acc3)
    pick = jnp.where(
        iota((8, NX), 1) == 16 * iota((8, NX), 0) + (LEV - 64), 1.0, 0.0
    ).astype(F32)

    def cells(b, _):
        part = recv_ref[pl.ds(16 * b, 16), pl.ds(32, 8), :].reshape(NX, NX)
        found = lax.dot_general(
            pick, part, (((1,), (1,)), ((), ())), precision=HI, preferred_element_type=F32
        )
        cell_v[:, pl.ds(pl.multiple_of(b * NX, NX), NX)] = (found + 0.5).astype(jnp.int32)
        return 0

    lax.fori_loop(0, 8, cells, 0, unroll=True)
    copy = pltpu.make_async_copy(cell_v, cell_s, sem)
    copy.start()

    def unfold(s, _):
        rest = recv_ref[s, pl.ds(32, 8), :]
        lane8 = iota((8, NX), 1)
        for g in range(8):
            tail = pltpu.roll(rest, (64 - 16 * g) % NX, 1) if g != 4 else rest
            head = recv_ref[s, pl.ds(8 * (g % 4), 8), :]
            head = pltpu.roll(head, 64, 1) if g >= 4 else head
            full[pl.ds(s * CAP + 8 * g, 8), :] = jnp.where(lane8 < 64, head, tail)
        return 0

    lax.fori_loop(0, DEV, unfold, 0, unroll=4)

    def clear(i, _):
        at = pl.ds(pl.multiple_of(i * 64, 64), 64)
        for acc in accs:
            acc[at, :] = jnp.zeros((64, NX), F32)
        return 0

    lax.fori_loop(0, SLOTS // 64, clear, 0, unroll=2)
    copy.wait()
    per = DEV // WAYS

    def add(s, _):
        for g in range(8):
            for e in range(8):
                for w, acc in enumerate(accs):
                    src = s + w * per
                    cell = cell_s[g, src * 8 + e]
                    at = pl.ds(cell, 1)
                    acc[at, :] = acc[at, :] + full[pl.ds(src * CAP + 8 * g + e, 1), :]
        return 0

    lax.fori_loop(0, per, add, 0)

    matrix = matrix_ref[pl.ds(0, LP), pl.ds(0, LEV)]

    def finish(b, _):
        loaded = []
        for h in range(2):
            y = 2 * b + h
            at = pl.ds(pl.multiple_of(y * NX, NX), NX)
            total = (acc0[at, :] + acc1[at, :]) + (acc2[at, :] + acc3[at, :])
            loaded.append(total.T[:LEV] + forcing_ref[pl.ds(y, LEV, stride=NY), :])
        product = jnp.dot(
            matrix, jnp.concatenate(loaded, 1), precision=HI, preferred_element_type=F32
        )
        out_ref[2 * b] = product[:, :NX]
        out_ref[2 * b + 1] = product[:, NX:]
        return 0

    lax.fori_loop(0, NY // 2, finish, 0, unroll=4)


def add_profiles(recv, forcing, matrix):
    vm = pl.BlockSpec(memory_space=pltpu.VMEM)
    return pl.pallas_call(
        add_body,
        out_shape=jax.ShapeDtypeStruct((NY, LP, NX), F32),
        in_specs=[vm, vm, vm],
        out_specs=vm,
        scratch_shapes=[pltpu.VMEM((SLOTS, NX), F32)] * 5
        + [
            pltpu.VMEM((8, 8 * DEV), jnp.int32),
            pltpu.SMEM((8, 8 * DEV), jnp.int32),
            pltpu.SemaphoreType.DMA(()),
        ],
        compiler_params=pltpu.CompilerParams(vmem_limit_bytes=56 << 20),
        name="add_profiles",
    )(recv, forcing.reshape(LEV * NY, NX), matrix)


def spread_body(
    field_ref, fac_ref, strip_ref,
    out_ref,
    wide_a, wide_b, tips, strip_a, strip_b, east_box, west_box, from_west, from_east, corners,
    own_sem, send_sem, recv_sem,
):
    lon = lax.axis_index("lon")
    lat = lax.axis_index("lat")
    east, west = lax.rem(lon + 1, 32), lax.rem(lon + 31, 32)
    north, south = lax.rem(lat + 1, 4), lax.rem(lat + 3, 4)
    peers = [
        (lon, north), (lon, south), (east, lat), (west, lat),
        (east, north), (west, north), (east, south), (west, south),
    ]
    barrier = pltpu.get_barrier_semaphore()
    for peer in peers:
        pl.semaphore_signal(barrier, inc=1, device_id=peer, device_id_type=MESH)
    own = pltpu.make_async_copy(field_ref, wide_a.at[pl.ds(HALO, NY)], own_sem)
    own.start()
    own.wait()

    lane = iota((LP, NX), 1)
    group, place = lane // 32, lane % 32

    def tip(low, high, parts):
        def one(q, _):
            total = jnp.zeros((LP, NX), F32)
            for j in parts:
                piece = pltpu.roll(wide_a[q + Q * j], (32 * j + 8) % NX, 1)
                total = jnp.where((group == j) & (place < 16), piece, total)
            tips[q] = total
            return 0

        lax.fori_loop(low, high, one, 0, unroll=2)

    tip(0, HALO, (1, 2, 3))
    tip(HALO, Q - HALO, (0, 1, 2, 3))
    tip(Q - HALO, Q, (0, 1, 2))
    for b in range(3):
        e = jnp.zeros((LP, NX), F32)
        w = jnp.zeros((LP, NX), F32)
        for q in range(8 * b, min(8 * b + 8, Q)):
            here = place // 4 == q % 8
            row = tips[q]
            e = jnp.where(here, pltpu.roll(row, (4 * (q % 8) - 4) % NX, 1), e)
            w = jnp.where(here, pltpu.roll(row, (4 * (q % 8) - 8) % NX, 1), w)
        east_box[b] = e
        west_box[b] = w

    pl.semaphore_wait(barrier, 8)
    moves = [
        (field_ref.at[pl.ds(NY - HALO, HALO)], wide_a.at[pl.ds(0, HALO)]),
        (field_ref.at[pl.ds(0, HALO)], wide_a.at[pl.ds(NY + HALO, HALO)]),
        (east_box, from_west),
        (west_box, from_east),
        (east_box.at[1], corners.at[0]),
        (west_box.at[1], corners.at[1]),
        (east_box.at[0], corners.at[2]),
        (west_box.at[0], corners.at[3]),
    ]
    copies = []
    for number, (src, dst) in enumerate(moves):
        copy = pltpu.make_async_remote_copy(
            src_ref=src, dst_ref=dst, send_sem=send_sem.at[number], recv_sem=recv_sem.at[number],
            device_id=peers[number], device_id_type=MESH,
        )
        copy.start()
        copies.append(copy)

    def stencil(facs, y, src, at):
        centre = src[at]

        def fac(i):
            return jnp.broadcast_to(facs[i, pl.ds(y, 1), :], (LP, NX))

        return (
            fac(0) * centre
            + fac(1) * pltpu.roll(centre, NX - 1, 1)
            + fac(2) * pltpu.roll(centre, 1, 1)
            + fac(3) * src[at + 1]
            + fac(4) * src[at - 1]
        )

    def rows(t, low, high, unroll):
        src, dst = (wide_a, wide_b) if t % 2 else (wide_b, wide_a)

        def row(y, _):
            dst[y] = stencil(fac_ref, y, src, y)
            return 0

        lax.fori_loop(low, high, row, 0, unroll=unroll)

    for t in range(1, 5):
        rows(t, HALO + t, NY + HALO - t, 8)

    for copy in copies:
        copy.wait()

    for near, from_side in ((0, from_west), (1, from_east)):
        below, above = corners[near], corners[near + 2]
        from_side[0] = jnp.where(lane < 16, pltpu.roll(below, 24, 1), from_side[0])
        from_side[1] = jnp.where(lane >= 120, pltpu.roll(above, 104, 1), from_side[1])
        from_side[2] = jnp.where((lane >= 96) & (lane < 104), pltpu.roll(above, 72, 1), from_side[2])
    for h in range(HALO):
        q = Q - HALO + h
        tips[h] = jnp.where((group == 0) & (place < 16), pltpu.roll(wide_a[h], 8, 1), tips[h])
        tips[q] = jnp.where((group == 3) & (place < 16), pltpu.roll(wide_a[q + 3 * Q], 104, 1), tips[q])
    for q in range(Q):
        row = tips[q]
        right = pltpu.roll(from_east[q // 8], (8 - 4 * (q % 8)) % NX, 1)
        left = pltpu.roll(from_west[q // 8], (16 - 4 * (q % 8)) % NX, 1)
        far = jnp.where((place >= 16) & (place < 20), left, pltpu.roll(row, 12, 1))
        strip_a[q + 1] = jnp.where(place < 8, row, jnp.where(place < 12, right, far))

    for t in range(1, 5):
        rows(t, t, HALO + t, 4)
        rows(t, NY + HALO - t, NY + 2 * HALO - t, 4)
    for t in range(4):
        src, dst = (strip_a, strip_b) if t % 2 == 0 else (strip_b, strip_a)
        src[0] = pltpu.roll(src[Q], 32, 1)
        src[Q + 1] = pltpu.roll(src[1], NX - 32, 1)

        def strip(q, _):
            dst[q + 1] = stencil(strip_ref, q, src, q + 1)
            return 0

        lax.fori_loop(0, Q, strip, 0, unroll=6)

    edge = (lane < HALO) | (lane >= NX - HALO)

    def write(low, high, parts):
        def one(q, _):
            row = strip_a[q + 1]
            row = jnp.where(place < 8, row, pltpu.roll(row, NX - 12, 1))
            for j in parts:
                y = q + Q * j
                whole = jnp.where(edge, pltpu.roll(row, (120 - 32 * j) % NX, 1), wide_a[y])
                out_ref[pl.ds(y - HALO, LEV, stride=NY), :] = whole[:LEV]
            return 0

        lax.fori_loop(low, high, one, 0, unroll=2)

    write(0, HALO, (1, 2, 3))
    write(HALO, Q - HALO, (0, 1, 2, 3))
    write(Q - HALO, Q, (0, 1, 2))


def spread(field, fac_main, fac_strip):
    vm = pl.BlockSpec(memory_space=pltpu.VMEM)
    wide = pltpu.VMEM((YE, LP, NX), F32)
    strip = pltpu.VMEM((Q + 2, LP, NX), F32)
    box = pltpu.VMEM((3, LP, NX), F32)
    return pl.pallas_call(
        spread_body,
        out_shape=jax.ShapeDtypeStruct((LEV * NY, NX), F32),
        in_specs=[pl.BlockSpec(memory_space=pl.ANY), vm, vm],
        out_specs=vm,
        scratch_shapes=[
            wide, wide, pltpu.VMEM((Q, LP, NX), F32), strip, strip, box, box, box, box,
            pltpu.VMEM((4, LP, NX), F32),
            pltpu.SemaphoreType.DMA(()),
            pltpu.SemaphoreType.DMA((8,)),
            pltpu.SemaphoreType.DMA((8,)),
        ],
        compiler_params=pltpu.CompilerParams(
            collective_id=1, has_side_effects=True, vmem_limit_bytes=40 << 20
        ),
        name="spread",
    )(field, fac_main, fac_strip)


def local(
    forcing, obs_values, obs_owner, obs_cell, obs_count,
    coef_east, coef_north, area_inv, sea_mask, vert_coef, inv_thick,
):
    coefs = (coef_east, coef_north, area_inv, sea_mask)
    recv, fac_main, fac_strip, matrix = send_profiles(
        obs_count, vert_coef, inv_thick, obs_owner, obs_values, obs_cell, coefs
    )
    field = add_profiles(recv, forcing, matrix)
    return spread(field, fac_main, fac_strip).reshape(LEV, NY, NX)


def solution(mesh):
    lead = P(("lon", "lat"))
    flat = P("lat", "lon")
    in_specs = (
        P(None, "lat", "lon"), P(None, ("lon", "lat")), lead, lead, lead,
        flat, flat, flat, flat, P(), P(),
    )
    return jax.shard_map(
        local, mesh=mesh, in_specs=in_specs, out_specs=P(None, "lat", "lon"), check_vma=False
    )
```

```python
import jax
import jax.numpy as jnp
from jax import lax
from jax.experimental import pallas as pl
from jax.experimental.pallas import tpu as pltpu
from jax.sharding import PartitionSpec as P

LEV = 75
LP = 80
NX = 128
NY = 64
DEV = 128
CAP = 64
SLOTS = 8192
ROWS = 40
HALO = 4
YE = NY + 2 * HALO
Q = 18
STRIDE = 27
F32 = jnp.float32
BF16 = jnp.bfloat16
HI = lax.Precision.HIGHEST
MESH = pl.DeviceIdType.MESH


def in_hbm(x):
    return pltpu.with_memory_space_constraint(x, pltpu.HBM)


def iota(shape, dim, dtype=jnp.int32):
    return lax.broadcasted_iota(dtype, shape, dim)


def vertical_fourth(vert_ref, thick_ref, out_ref, cp_ref, dp_ref):
    lane = iota((1, NX), 1)
    dp_ref[...] = jnp.zeros_like(dp_ref)

    def forward(i, carry):
        cp, dp = carry
        up = jnp.where(i < LEV - 1, vert_ref[jnp.minimum(i, LEV - 2)], 0.0)
        low = jnp.where(i > 0, vert_ref[jnp.maximum(i - 1, 0)], 0.0)
        middle = 1.0 + (low + up) * thick_ref[i]
        above = -thick_ref[jnp.minimum(i + 1, LEV - 1)] * up
        below = -thick_ref[jnp.maximum(i - 1, 0)] * low
        inv = 1.0 / (middle - below * cp)
        cp = above * inv
        dp = (jnp.where(lane == i, 1.0, 0.0) - below * dp) * inv
        cp_ref[pl.ds(i, 1), :] = cp
        dp_ref[pl.ds(i, 1), :] = dp
        return cp, dp

    zero = jnp.zeros((1, NX), F32)
    lax.fori_loop(0, LEV, forward, (zero, zero))

    def backward(j, x):
        i = LEV - 1 - j
        x = dp_ref[pl.ds(i, 1), :] - cp_ref[pl.ds(i, 1), :] * x
        dp_ref[pl.ds(i, 1), :] = x
        return x

    lax.fori_loop(0, LEV, backward, zero)
    single = dp_ref[...]
    double = jnp.dot(single, single, precision=HI, preferred_element_type=F32)
    out_ref[...] = jnp.dot(double, double, precision=HI, preferred_element_type=F32)


def places(count, own_ref, idx_ref):
    width = 256
    lane = iota((1, width), 1)
    owners = iota((DEV, width), 0)
    tri = (iota((width, width + NX), 0) <= iota((width, width + NX), 1)) | (
        iota((width, width + NX), 1) >= width
    )
    tri = tri.astype(F32).astype(BF16)
    kth = iota((CAP, width), 0).astype(F32)
    number = (iota((CAP, width), 1) + 1).astype(F32)
    acc_lane = iota((DEV, NX), 1)

    def step(b, carry):
        offset, acc = carry
        own = jnp.concatenate([own_ref[pl.ds(2 * b, 1), :], own_ref[pl.ds(2 * b + 1, 1), :]], 1)
        own = jnp.where(lane + b * width < count, own, -1)
        onehot = jnp.where(jnp.broadcast_to(own, (DEV, width)) == owners, 1.0, 0.0)
        ones = onehot.astype(BF16)
        prefix = jnp.dot(ones, tri, preferred_element_type=F32)
        rank = prefix[:, :width] + jnp.concatenate([offset, offset], 1)
        rank = jnp.sum(onehot * rank, axis=0, keepdims=True) - 1.0
        hit = jnp.where(jnp.broadcast_to(rank, (CAP, width)) == kth, 1.0, 0.0)
        both = jnp.concatenate([hit, hit * number], 0).astype(BF16)
        found = lax.dot_general(ones, both, (((1,), (1,)), ((), ())), preferred_element_type=F32)
        scale = jnp.where(acc_lane < CAP, (b * width).astype(F32), 1.0)
        return offset + prefix[:, width:], acc + found * scale

    zero = jnp.zeros((DEV, NX), F32)
    _, acc = lax.fori_loop(0, SLOTS // width, step, (zero, zero), unroll=4)
    total = (acc + pltpu.roll(acc, CAP, 1)).astype(jnp.int32)
    idx_ref[...] = jnp.clip(jnp.where(total > 0, total - 1, SLOTS), 0, SLOTS)


def factors(coef_refs, row_halo_ref, col_halo_ref, corner_ref, coef_main, coef_side, fac_main_ref, fac_strip_ref):
    lat = lax.axis_index("lat")
    lane64 = iota((NY, NX), 1)
    lane4 = iota((HALO, NX), 1)
    for i in range(4):
        coef_main[i, pl.ds(HALO, NY), :] = coef_refs[i][...].astype(F32)
        coef_main[i, pl.ds(0, HALO), :] = row_halo_ref[0, i, pl.ds(4, HALO), :]
        coef_main[i, pl.ds(NY + HALO, HALO), :] = row_halo_ref[1, i, pl.ds(0, HALO), :]

        def sides(lanes, left, right, i=i):
            return jnp.where(
                lanes < 64,
                pltpu.roll(right, (-8 * i) % NX, 1),
                pltpu.roll(left, (124 - 8 * i - 4) % NX, 1),
            )

        coef_side[i, pl.ds(HALO, NY), :] = sides(lane64, col_halo_ref[0], col_halo_ref[1])
        coef_side[i, pl.ds(0, HALO), :] = sides(
            lane4, corner_ref[0, pl.ds(4, HALO), :], corner_ref[1, pl.ds(4, HALO), :]
        )
        coef_side[i, pl.ds(NY + HALO, HALO), :] = sides(
            lane4, corner_ref[2, pl.ds(0, HALO), :], corner_ref[3, pl.ds(0, HALO), :]
        )
    row = iota((YE, NX), 0)
    first_row = jnp.where(lat == 0, HALO, 0)
    last_row = jnp.where(lat == 3, NY + HALO, YE)
    inside = (row >= first_row) & (row < last_row)
    lanes = iota((YE, NX), 1)

    def shifts(main, side):
        first, last = lanes == 0, lanes == NX - 1
        main_e = pltpu.roll(jnp.where(first, side, main), NX - 1, 1)
        side_e = pltpu.roll(jnp.where(first, main, side), NX - 1, 1)
        main_w = pltpu.roll(jnp.where(last, side, main), 1, 1)
        side_w = pltpu.roll(jnp.where(last, main, side), 1, 1)
        return main_e, side_e, main_w, side_w

    sea_m = jnp.where(inside, coef_main[3], 0.0)
    sea_s = jnp.where(inside, coef_side[3], 0.0)
    area_m, area_s = coef_main[2], coef_side[2]
    sea_me, sea_se, _, _ = shifts(sea_m, sea_s)
    east_m = coef_main[0] * sea_m * sea_me
    east_s = coef_side[0] * sea_s * sea_se
    _, _, west_m, west_s = shifts(east_m, east_s)
    area_me, area_se, area_mw, area_sw = shifts(area_m, area_s)

    def five(north_coef, ee, ww, sea, area, area_e, area_w):
        nn = north_coef * sea * pltpu.roll(sea, YE - 1, 0)
        ss = pltpu.roll(nn, 1, 0)
        return (
            1.0 - area * (ee + ww + nn + ss),
            ee * area_e,
            ww * area_w,
            nn * pltpu.roll(area, YE - 1, 0),
            ss * pltpu.roll(area, 1, 0),
        )

    mains = five(coef_main[1], east_m, west_m, sea_m, area_m, area_me, area_mw)
    sides = five(coef_side[1], east_s, west_s, sea_s, area_s, area_se, area_sw)
    laneq = iota((Q, NX), 1)
    group, place = laneq // 32, laneq % 32
    gap = ((place >= 12) & (place < 16)) | (place >= 28)
    for i in range(5):
        fac_main_ref[i] = mains[i]
        coef_main[0] = jnp.where(lanes < 64, sides[i], mains[i])
        coef_main[1] = jnp.where(lanes < 64, mains[i], sides[i])
        strip = jnp.zeros((Q, NX), F32)
        for j in range(4):
            own = pl.ds(Q * j, Q)
            near = pltpu.roll(coef_main[0, own, :], (32 * j + 8) % NX, 1)
            far = pltpu.roll(coef_main[1, own, :], (32 * j + 20) % NX, 1)
            strip = jnp.where(group == j, jnp.where(place < 14, near, far), strip)
        fac_strip_ref[i, pl.ds(0, Q), :] = jnp.where(gap, 0.0, strip)


def send_body(
    count_ref, vert_hbm, thick_hbm, own_hbm, obs_hbm, cell_hbm, east_hbm, north_hbm, area_hbm, sea_hbm,
    full_ref, cells_ref, fac_main_ref, fac_strip_ref, matrix_ref,
    vert_ref, thick_ref, own_ref, obs_ref, cell_ref, east_ref, north_ref, area_ref, sea_ref,
    recv, load_sem, table, rows, outbox, coef_box, colbox, row_halo, col_halo, corner, coef_main, coef_side,
    cp_ref, dp_ref, idx_v, idx_ref, idx_sem, send_sem, recv_sem, side_send, side_recv,
):
    lon = lax.axis_index("lon")
    lat = lax.axis_index("lat")
    z, y, c = lax.div(lon, 8), lax.rem(lax.div(lon, 2), 4), lax.rem(lon, 2)
    me = lon * 4 + lat

    def target(k):
        q = lax.rem(k * STRIDE, DEV)
        dx, dc = lax.rem(q, 4), lax.rem(lax.div(q, 4), 2)
        dy, dz = lax.rem(lax.div(q, 8), 4), lax.div(q, 32)
        there = (lax.rem(z + dz, 4) * 4 + lax.rem(y + dy, 4)) * 2 + lax.rem(c + dc, 2)
        return there, lax.rem(lat + dx, 4)

    loads = []
    for number, (src, dst) in enumerate((
        (own_hbm, own_ref), (obs_hbm, obs_ref), (cell_hbm, cell_ref), (east_hbm, east_ref),
        (north_hbm, north_ref), (area_hbm, area_ref), (sea_hbm, sea_ref),
        (vert_hbm, vert_ref), (thick_hbm, thick_ref),
    )):
        load = pltpu.make_async_copy(src, dst, load_sem.at[number])
        load.start()
        loads.append(load)

    barrier = pltpu.get_barrier_semaphore()

    def greet(k, _):
        pl.semaphore_signal(barrier, inc=1, device_id=target(k), device_id_type=MESH)
        return 0

    lax.fori_loop(1, DEV, greet, 0)

    loads[0].wait()
    places(count_ref[0], own_ref, idx_v)
    idx_copy = pltpu.make_async_copy(idx_v, idx_ref, idx_sem)
    idx_copy.start()
    for load in loads[1:]:
        load.wait()

    def turn(b, _):
        columns = pl.ds(pl.multiple_of(b * NX, NX), NX)
        block = jnp.concatenate(
            [
                obs_ref[:, columns],
                cell_ref[pl.ds(b, 1), :].astype(F32),
                jnp.zeros((NX - LEV - 1, NX), F32),
            ],
            0,
        )
        table[columns, :] = block.T
        return 0

    lax.fori_loop(0, SLOTS // NX, turn, 0, unroll=4)
    table[pl.ds(SLOTS, 8), :] = jnp.zeros((8, NX), F32)

    lane = iota((NY, NX), 1)
    cols = jnp.zeros((NY, NX), F32)
    coef_refs = (east_ref, north_ref, area_ref, sea_ref)
    for i in range(4):
        whole = coef_refs[i][...].astype(F32)
        coef_box[i, pl.ds(0, 8), :] = whole[:8]
        coef_box[i, pl.ds(8, 8), :] = whole[NY - 8:]
        cols = jnp.where((lane >= 8 * i) & (lane < 8 * i + 4), pltpu.roll(whole, 8 * i, 1), cols)
        cols = jnp.where(
            (lane >= 8 * i + 4) & (lane < 8 * i + 8),
            pltpu.roll(whole, (8 * i + 4 - 124) % NX, 1),
            cols,
        )
    colbox[...] = cols
    idx_copy.wait()
    pl.semaphore_wait(barrier, DEV - 1)

    east, west = lax.rem(lon + 1, 32), lax.rem(lon + 31, 32)
    north, south = lax.rem(lat + 1, 4), lax.rem(lat + 3, 4)
    side = []

    def beside(number, src, dst, where):
        copy = pltpu.make_async_remote_copy(
            src_ref=src, dst_ref=dst, send_sem=side_send.at[number], recv_sem=side_recv.at[number],
            device_id=where, device_id_type=MESH,
        )
        copy.start()
        side.append(copy)

    beside(0, coef_box.at[:, pl.ds(8, 8), :], row_halo.at[0], (lon, north))
    beside(1, coef_box.at[:, pl.ds(0, 8), :], row_halo.at[1], (lon, south))
    beside(2, colbox, col_halo.at[0], (east, lat))
    beside(3, colbox, col_halo.at[1], (west, lat))
    beside(4, colbox.at[pl.ds(NY - 8, 8), :], corner.at[0], (east, north))
    beside(5, colbox.at[pl.ds(NY - 8, 8), :], corner.at[1], (west, north))
    beside(6, colbox.at[pl.ds(0, 8), :], corner.at[2], (east, south))
    beside(7, colbox.at[pl.ds(0, 8), :], corner.at[3], (west, south))

    lane8 = iota((8, NX), 1)
    lane32 = iota((32, NX), 1)

    def gather(owner):
        for k in range(CAP):
            at = jnp.minimum(jnp.maximum(idx_ref[owner, k], 0), SLOTS)
            rows[pl.ds(k, 1), :] = table[pl.ds(at, 1), :]

    def fold(box):
        box[pl.ds(0, 32), :] = jnp.where(
            lane32 < 64, rows[pl.ds(0, 32), :], pltpu.roll(rows[pl.ds(32, 32), :], 64, 1)
        )
        rest = jnp.zeros((8, NX), F32)
        for g in range(8):
            piece = rows[pl.ds(8 * g, 8), :]
            shift = (16 * g - 64) % NX
            piece = pltpu.roll(piece, shift, 1) if shift else piece
            rest = jnp.where(lane8 // 16 == g, piece, rest)
        box[pl.ds(32, 8), :] = rest

    def send(k, _):
        dlon, dlat = target(k)
        owner = dlon * 4 + dlat
        gather(owner)
        fold(outbox.at[owner])
        pltpu.make_async_remote_copy(
            src_ref=outbox.at[owner], dst_ref=recv.at[k], send_sem=send_sem, recv_sem=recv_sem.at[k],
            device_id=(dlon, dlat), device_id_type=MESH,
        ).start()
        return 0

    lax.fori_loop(1, DEV, send, 0)
    gather(me)
    fold(recv.at[0])
    vertical_fourth(vert_ref, thick_ref, matrix_ref, cp_ref, dp_ref)
    for copy in side:
        copy.wait()
    factors(coef_refs, row_halo, col_halo, corner, coef_main, coef_side, fac_main_ref, fac_strip_ref)
    pick = jnp.where(
        iota((8, NX), 1) == 16 * iota((8, NX), 0) + (LEV - 64), 1.0, 0.0
    ).astype(F32)

    def unfold(k):
        rest = recv[k, pl.ds(32, 8), :]
        for g in range(8):
            tail = pltpu.roll(rest, (64 - 16 * g) % NX, 1) if g != 4 else rest
            head = recv[k, pl.ds(8 * (g % 4), 8), :]
            head = pltpu.roll(head, 64, 1) if g >= 4 else head
            full_ref[pl.ds(k * CAP + 8 * g, 8), :] = jnp.where(lane8 < 64, head, tail)

    def arrive(k, _):
        pltpu.make_async_copy(recv.at[k], recv.at[k], recv_sem.at[k]).wait()
        return 0

    def spread_out(k, _):
        unfold(k)
        return 0

    for b in range(8):
        lax.fori_loop(max(16 * b, 1), 16 * b + 16, arrive, 0)
        lax.fori_loop(16 * b, 16 * b + 16, spread_out, 0, unroll=4)
        part = recv[pl.ds(16 * b, 16), pl.ds(32, 8), :].reshape(NX, NX)
        found = lax.dot_general(
            pick, part, (((1,), (1,)), ((), ())), precision=HI, preferred_element_type=F32
        )
        cells_ref[:, pl.ds(NX * b, NX)] = (found + 0.5).astype(jnp.int32)
    others = pl.ds(0, DEV - 1)
    pltpu.make_async_copy(outbox.at[others], outbox.at[others], send_sem).wait()


def send_profiles(count, vert_coef, inv_thick, owner, obs, cell, coefs):
    vm = pl.BlockSpec(memory_space=pltpu.VMEM)
    sm = pl.BlockSpec(memory_space=pltpu.SMEM)
    plane = pltpu.VMEM((4, YE, NX), F32)
    return pl.pallas_call(
        send_body,
        out_shape=(
            jax.ShapeDtypeStruct((SLOTS, NX), F32),
            jax.ShapeDtypeStruct((8, 8 * DEV), jnp.int32),
            jax.ShapeDtypeStruct((5, YE, NX), F32),
            jax.ShapeDtypeStruct((5, 24, NX), F32),
            jax.ShapeDtypeStruct((NX, NX), F32),
        ),
        in_specs=[sm] + [pl.BlockSpec(memory_space=pltpu.HBM)] * 9,
        out_specs=(vm,) * 5,
        scratch_shapes=[
            pltpu.SMEM((LEV - 1,), F32),
            pltpu.SMEM((LEV,), F32),
            pltpu.VMEM((SLOTS // NX, NX), jnp.int32),
            pltpu.VMEM((LEV, SLOTS), F32),
            pltpu.VMEM((SLOTS // NX, NX), jnp.int32),
            pltpu.VMEM((NY, NX), F32),
            pltpu.VMEM((NY, NX), F32),
            pltpu.VMEM((NY, NX), F32),
            pltpu.VMEM((NY, NX), jnp.int32),
            pltpu.VMEM((DEV, ROWS, NX), F32),
            pltpu.SemaphoreType.DMA((9,)),
            pltpu.VMEM((SLOTS + 8, NX), F32),
            pltpu.VMEM((CAP, NX), F32),
            pltpu.VMEM((DEV, ROWS, NX), F32),
            pltpu.VMEM((4, 16, NX), F32),
            pltpu.VMEM((NY, NX), F32),
            pltpu.VMEM((2, 4, 8, NX), F32),
            pltpu.VMEM((2, NY, NX), F32),
            pltpu.VMEM((4, 8, NX), F32),
            plane,
            plane,
            pltpu.VMEM((NX, NX), F32),
            pltpu.VMEM((NX, NX), F32),
            pltpu.VMEM((DEV, NX), jnp.int32),
            pltpu.SMEM((DEV, NX), jnp.int32),
            pltpu.SemaphoreType.DMA(()),
            pltpu.SemaphoreType.DMA(()),
            pltpu.SemaphoreType.DMA((DEV,)),
            pltpu.SemaphoreType.DMA((8,)),
            pltpu.SemaphoreType.DMA((8,)),
        ],
        compiler_params=pltpu.CompilerParams(
            collective_id=0, has_side_effects=True, vmem_limit_bytes=24 << 20
        ),
        name="send_profiles",
    )(count, *map(in_hbm, (
        vert_coef, inv_thick, owner.reshape(SLOTS // NX, NX), obs,
        cell.reshape(SLOTS // NX, NX), *coefs,
    )))


WAYS = 4


def add_body(full, cell_v, forcing_ref, matrix_ref, out_ref, acc0, acc1, acc2, acc3, cell_s, sem):
    accs = (acc0, acc1, acc2, acc3)
    copy = pltpu.make_async_copy(cell_v, cell_s, sem)
    copy.start()

    def clear(i, _):
        at = pl.ds(pl.multiple_of(i * 64, 64), 64)
        for acc in accs:
            acc[at, :] = jnp.zeros((64, NX), F32)
        return 0

    lax.fori_loop(0, SLOTS // 64, clear, 0, unroll=2)
    copy.wait()
    per = DEV // WAYS

    def add(s, _):
        for g in range(8):
            for e in range(8):
                for w, acc in enumerate(accs):
                    src = s + w * per
                    at = pl.ds(cell_s[g, src * 8 + e], 1)
                    acc[at, :] = acc[at, :] + full[pl.ds(src * CAP + 8 * g + e, 1), :]
        return 0

    lax.fori_loop(0, per, add, 0)
    matrix = matrix_ref[pl.ds(0, LP), pl.ds(0, LEV)]

    def finish(b, _):
        loaded = []
        for h in range(2):
            y = 2 * b + h
            at = pl.ds(pl.multiple_of(y * NX, NX), NX)
            total = (acc0[at, :] + acc1[at, :]) + (acc2[at, :] + acc3[at, :])
            loaded.append(total.T[:LEV] + forcing_ref[pl.ds(y, LEV, stride=NY), :])
        product = jnp.dot(
            matrix, jnp.concatenate(loaded, 1), precision=HI, preferred_element_type=F32
        )
        out_ref[2 * b] = product[:, :NX]
        out_ref[2 * b + 1] = product[:, NX:]
        return 0

    lax.fori_loop(0, NY // 2, finish, 0, unroll=4)


def add_profiles(full, cells, forcing, matrix):
    vm = pl.BlockSpec(memory_space=pltpu.VMEM)
    return pl.pallas_call(
        add_body,
        out_shape=jax.ShapeDtypeStruct((NY, LP, NX), F32),
        in_specs=[vm, vm, vm, vm],
        out_specs=vm,
        scratch_shapes=[pltpu.VMEM((SLOTS, NX), F32)] * 4
        + [
            pltpu.SMEM((8, 8 * DEV), jnp.int32),
            pltpu.SemaphoreType.DMA(()),
        ],
        compiler_params=pltpu.CompilerParams(vmem_limit_bytes=30 << 20),
        name="add_profiles",
    )(full, cells, forcing.reshape(LEV * NY, NX), matrix)


def spread_body(
    field_ref, fac_ref, strip_ref,
    out_ref,
    wide_a, wide_b, tips, strip_a, strip_b, east_box, west_box, from_west, from_east, corners,
    own_sem, send_sem, recv_sem,
):
    lon = lax.axis_index("lon")
    lat = lax.axis_index("lat")
    east, west = lax.rem(lon + 1, 32), lax.rem(lon + 31, 32)
    north, south = lax.rem(lat + 1, 4), lax.rem(lat + 3, 4)
    peers = [
        (lon, north), (lon, south), (east, lat), (west, lat),
        (east, north), (west, north), (east, south), (west, south),
    ]
    barrier = pltpu.get_barrier_semaphore()
    for peer in peers:
        pl.semaphore_signal(barrier, inc=1, device_id=peer, device_id_type=MESH)
    own = pltpu.make_async_copy(field_ref, wide_a.at[pl.ds(HALO, NY)], own_sem)
    own.start()
    own.wait()

    lane = iota((LP, NX), 1)
    group, place = lane // 32, lane % 32

    def tip(low, high, parts):
        def one(q, _):
            total = jnp.zeros((LP, NX), F32)
            for j in parts:
                piece = pltpu.roll(wide_a[q + Q * j], (32 * j + 8) % NX, 1)
                total = jnp.where((group == j) & (place < 16), piece, total)
            tips[q] = total
            return 0

        lax.fori_loop(low, high, one, 0, unroll=2)

    tip(0, HALO, (1, 2, 3))
    tip(HALO, Q - HALO, (0, 1, 2, 3))
    tip(Q - HALO, Q, (0, 1, 2))
    for b in range(3):
        e = jnp.zeros((LP, NX), F32)
        w = jnp.zeros((LP, NX), F32)
        for q in range(8 * b, min(8 * b + 8, Q)):
            here = place // 4 == q % 8
            row = tips[q]
            e = jnp.where(here, pltpu.roll(row, (4 * (q % 8) - 4) % NX, 1), e)
            w = jnp.where(here, pltpu.roll(row, (4 * (q % 8) - 8) % NX, 1), w)
        east_box[b] = e
        west_box[b] = w

    pl.semaphore_wait(barrier, 8)
    moves = [
        (field_ref.at[pl.ds(NY - HALO, HALO)], wide_a.at[pl.ds(0, HALO)]),
        (field_ref.at[pl.ds(0, HALO)], wide_a.at[pl.ds(NY + HALO, HALO)]),
        (east_box, from_west),
        (west_box, from_east),
        (east_box.at[1], corners.at[0]),
        (west_box.at[1], corners.at[1]),
        (east_box.at[0], corners.at[2]),
        (west_box.at[0], corners.at[3]),
    ]
    copies = []
    for number, (src, dst) in enumerate(moves):
        copy = pltpu.make_async_remote_copy(
            src_ref=src, dst_ref=dst, send_sem=send_sem.at[number], recv_sem=recv_sem.at[number],
            device_id=peers[number], device_id_type=MESH,
        )
        copy.start()
        copies.append(copy)

    def stencil(facs, y, src, at):
        centre = src[at]

        def fac(i):
            return jnp.broadcast_to(facs[i, pl.ds(y, 1), :], (LP, NX))

        return (
            fac(0) * centre
            + fac(1) * pltpu.roll(centre, NX - 1, 1)
            + fac(2) * pltpu.roll(centre, 1, 1)
            + fac(3) * src[at + 1]
            + fac(4) * src[at - 1]
        )

    def rows(t, low, high, unroll):
        src, dst = (wide_a, wide_b) if t % 2 else (wide_b, wide_a)

        def row(y, _):
            dst[y] = stencil(fac_ref, y, src, y)
            return 0

        lax.fori_loop(low, high, row, 0, unroll=unroll)

    for t in range(1, 5):
        rows(t, HALO + t, NY + HALO - t, 8)

    for copy in copies:
        copy.wait()

    for near, from_side in ((0, from_west), (1, from_east)):
        below, above = corners[near], corners[near + 2]
        from_side[0] = jnp.where(lane < 16, pltpu.roll(below, 24, 1), from_side[0])
        from_side[1] = jnp.where(lane >= 120, pltpu.roll(above, 104, 1), from_side[1])
        from_side[2] = jnp.where((lane >= 96) & (lane < 104), pltpu.roll(above, 72, 1), from_side[2])
    for h in range(HALO):
        q = Q - HALO + h
        tips[h] = jnp.where((group == 0) & (place < 16), pltpu.roll(wide_a[h], 8, 1), tips[h])
        tips[q] = jnp.where((group == 3) & (place < 16), pltpu.roll(wide_a[q + 3 * Q], 104, 1), tips[q])
    for q in range(Q):
        row = tips[q]
        right = pltpu.roll(from_east[q // 8], (8 - 4 * (q % 8)) % NX, 1)
        left = pltpu.roll(from_west[q // 8], (16 - 4 * (q % 8)) % NX, 1)
        far = jnp.where((place >= 16) & (place < 20), left, pltpu.roll(row, 12, 1))
        strip_a[q + 1] = jnp.where(place < 8, row, jnp.where(place < 12, right, far))

    for t in range(1, 5):
        rows(t, t, HALO + t, 4)
        rows(t, NY + HALO - t, NY + 2 * HALO - t, 4)
    for t in range(4):
        src, dst = (strip_a, strip_b) if t % 2 == 0 else (strip_b, strip_a)
        src[0] = pltpu.roll(src[Q], 32, 1)
        src[Q + 1] = pltpu.roll(src[1], NX - 32, 1)

        def strip(q, _):
            dst[q + 1] = stencil(strip_ref, q, src, q + 1)
            return 0

        lax.fori_loop(0, Q, strip, 0, unroll=6)

    edge = (lane < HALO) | (lane >= NX - HALO)

    def write(low, high, parts):
        def one(q, _):
            row = strip_a[q + 1]
            row = jnp.where(place < 8, row, pltpu.roll(row, NX - 12, 1))
            for j in parts:
                y = q + Q * j
                whole = jnp.where(edge, pltpu.roll(row, (120 - 32 * j) % NX, 1), wide_a[y])
                out_ref[pl.ds(y - HALO, LEV, stride=NY), :] = whole[:LEV]
            return 0

        lax.fori_loop(low, high, one, 0, unroll=2)

    write(0, HALO, (1, 2, 3))
    write(HALO, Q - HALO, (0, 1, 2, 3))
    write(Q - HALO, Q, (0, 1, 2))


def spread(field, fac_main, fac_strip):
    vm = pl.BlockSpec(memory_space=pltpu.VMEM)
    wide = pltpu.VMEM((YE, LP, NX), F32)
    strip = pltpu.VMEM((Q + 2, LP, NX), F32)
    box = pltpu.VMEM((3, LP, NX), F32)
    return pl.pallas_call(
        spread_body,
        out_shape=jax.ShapeDtypeStruct((LEV * NY, NX), F32),
        in_specs=[pl.BlockSpec(memory_space=pl.ANY), vm, vm],
        out_specs=vm,
        scratch_shapes=[
            wide, wide, pltpu.VMEM((Q, LP, NX), F32), strip, strip, box, box, box, box,
            pltpu.VMEM((4, LP, NX), F32),
            pltpu.SemaphoreType.DMA(()),
            pltpu.SemaphoreType.DMA((8,)),
            pltpu.SemaphoreType.DMA((8,)),
        ],
        compiler_params=pltpu.CompilerParams(
            collective_id=1, has_side_effects=True, vmem_limit_bytes=24 << 20
        ),
        name="spread",
    )(field, fac_main, fac_strip)


def local(
    forcing, obs_values, obs_owner, obs_cell, obs_count,
    coef_east, coef_north, area_inv, sea_mask, vert_coef, inv_thick,
):
    coefs = (coef_east, coef_north, area_inv, sea_mask)
    full, cells, fac_main, fac_strip, matrix = send_profiles(
        obs_count, vert_coef, inv_thick, obs_owner, obs_values, obs_cell, coefs
    )
    field = add_profiles(full, cells, forcing, matrix)
    return spread(field, fac_main, fac_strip).reshape(LEV, NY, NX)


def solution(mesh):
    lead = P(("lon", "lat"))
    flat = P("lat", "lon")
    in_specs = (
        P(None, "lat", "lon"), P(None, ("lon", "lat")), lead, lead, lead,
        flat, flat, flat, flat, P(), P(),
    )
    return jax.shard_map(
        local, mesh=mesh, in_specs=in_specs, out_specs=P(None, "lat", "lon"), check_vma=False
    )
```

```python
import jax
import jax.numpy as jnp
from jax import lax
from jax.experimental import pallas as pl
from jax.experimental.pallas import tpu as pltpu
from jax.sharding import PartitionSpec as P

LEV = 75
LP = 80
NX = 128
NY = 64
DEV = 128
CAP = 64
SLOTS = 8192
ROWS = 40
HALO = 4
YE = NY + 2 * HALO
Q = 18
STRIDE = 27
F32 = jnp.float32
BF16 = jnp.bfloat16
HI = lax.Precision.HIGHEST
MESH = pl.DeviceIdType.MESH


def in_hbm(x):
    return pltpu.with_memory_space_constraint(x, pltpu.HBM)


def iota(shape, dim, dtype=jnp.int32):
    return lax.broadcasted_iota(dtype, shape, dim)


def vertical_fourth(vert_ref, thick_ref, out_ref, cp_ref, dp_ref):
    lane = iota((1, NX), 1)
    dp_ref[...] = jnp.zeros_like(dp_ref)

    def forward(i, carry):
        cp, dp = carry
        up = jnp.where(i < LEV - 1, vert_ref[jnp.minimum(i, LEV - 2)], 0.0)
        low = jnp.where(i > 0, vert_ref[jnp.maximum(i - 1, 0)], 0.0)
        middle = 1.0 + (low + up) * thick_ref[i]
        above = -thick_ref[jnp.minimum(i + 1, LEV - 1)] * up
        below = -thick_ref[jnp.maximum(i - 1, 0)] * low
        inv = 1.0 / (middle - below * cp)
        cp = above * inv
        dp = (jnp.where(lane == i, 1.0, 0.0) - below * dp) * inv
        cp_ref[pl.ds(i, 1), :] = cp
        dp_ref[pl.ds(i, 1), :] = dp
        return cp, dp

    zero = jnp.zeros((1, NX), F32)
    lax.fori_loop(0, LEV, forward, (zero, zero))

    def backward(j, x):
        i = LEV - 1 - j
        x = dp_ref[pl.ds(i, 1), :] - cp_ref[pl.ds(i, 1), :] * x
        dp_ref[pl.ds(i, 1), :] = x
        return x

    lax.fori_loop(0, LEV, backward, zero)
    single = dp_ref[...]
    double = jnp.dot(single, single, precision=HI, preferred_element_type=F32)
    out_ref[...] = jnp.dot(double, double, precision=HI, preferred_element_type=F32)


def places(count, own_ref, idx_ref):
    width = 256
    lane = iota((1, width), 1)
    owners = iota((DEV, width), 0)
    tri = (iota((width, width + NX), 0) <= iota((width, width + NX), 1)) | (
        iota((width, width + NX), 1) >= width
    )
    tri = tri.astype(F32).astype(BF16)
    kth = iota((CAP, width), 0).astype(F32)
    number = (iota((CAP, width), 1) + 1).astype(F32)
    acc_lane = iota((DEV, NX), 1)

    def step(b, carry):
        offset, acc = carry
        own = jnp.concatenate([own_ref[pl.ds(2 * b, 1), :], own_ref[pl.ds(2 * b + 1, 1), :]], 1)
        own = jnp.where(lane + b * width < count, own, -1)
        onehot = jnp.where(jnp.broadcast_to(own, (DEV, width)) == owners, 1.0, 0.0)
        ones = onehot.astype(BF16)
        prefix = jnp.dot(ones, tri, preferred_element_type=F32)
        rank = prefix[:, :width] + jnp.concatenate([offset, offset], 1)
        rank = jnp.sum(onehot * rank, axis=0, keepdims=True) - 1.0
        hit = jnp.where(jnp.broadcast_to(rank, (CAP, width)) == kth, 1.0, 0.0)
        both = jnp.concatenate([hit, hit * number], 0).astype(BF16)
        found = lax.dot_general(ones, both, (((1,), (1,)), ((), ())), preferred_element_type=F32)
        scale = jnp.where(acc_lane < CAP, (b * width).astype(F32), 1.0)
        return offset + prefix[:, width:], acc + found * scale

    zero = jnp.zeros((DEV, NX), F32)
    _, acc = lax.fori_loop(0, SLOTS // width, step, (zero, zero), unroll=16)
    total = (acc + pltpu.roll(acc, CAP, 1)).astype(jnp.int32)
    idx_ref[...] = jnp.clip(jnp.where(total > 0, total - 1, SLOTS + acc_lane % 8), 0, SLOTS + 7)


def factors(coef_refs, row_halo_ref, col_halo_ref, corner_ref, coef_main, coef_side, fac_main_ref, fac_strip_ref):
    lat = lax.axis_index("lat")
    lane64 = iota((NY, NX), 1)
    lane4 = iota((HALO, NX), 1)
    for i in range(4):
        coef_main[i, pl.ds(HALO, NY), :] = coef_refs[i][...].astype(F32)
        coef_main[i, pl.ds(0, HALO), :] = row_halo_ref[0, i, pl.ds(4, HALO), :]
        coef_main[i, pl.ds(NY + HALO, HALO), :] = row_halo_ref[1, i, pl.ds(0, HALO), :]

        def sides(lanes, left, right, i=i):
            return jnp.where(
                lanes < 64,
                pltpu.roll(right, (-8 * i) % NX, 1),
                pltpu.roll(left, (124 - 8 * i - 4) % NX, 1),
            )

        coef_side[i, pl.ds(HALO, NY), :] = sides(lane64, col_halo_ref[0], col_halo_ref[1])
        coef_side[i, pl.ds(0, HALO), :] = sides(
            lane4, corner_ref[0, pl.ds(4, HALO), :], corner_ref[1, pl.ds(4, HALO), :]
        )
        coef_side[i, pl.ds(NY + HALO, HALO), :] = sides(
            lane4, corner_ref[2, pl.ds(0, HALO), :], corner_ref[3, pl.ds(0, HALO), :]
        )
    row = iota((YE, NX), 0)
    first_row = jnp.where(lat == 0, HALO, 0)
    last_row = jnp.where(lat == 3, NY + HALO, YE)
    inside = (row >= first_row) & (row < last_row)
    lanes = iota((YE, NX), 1)

    def shifts(main, side):
        first, last = lanes == 0, lanes == NX - 1
        main_e = pltpu.roll(jnp.where(first, side, main), NX - 1, 1)
        side_e = pltpu.roll(jnp.where(first, main, side), NX - 1, 1)
        main_w = pltpu.roll(jnp.where(last, side, main), 1, 1)
        side_w = pltpu.roll(jnp.where(last, main, side), 1, 1)
        return main_e, side_e, main_w, side_w

    sea_m = jnp.where(inside, coef_main[3], 0.0)
    sea_s = jnp.where(inside, coef_side[3], 0.0)
    area_m, area_s = coef_main[2], coef_side[2]
    sea_me, sea_se, _, _ = shifts(sea_m, sea_s)
    east_m = coef_main[0] * sea_m * sea_me
    east_s = coef_side[0] * sea_s * sea_se
    _, _, west_m, west_s = shifts(east_m, east_s)
    area_me, area_se, area_mw, area_sw = shifts(area_m, area_s)

    def five(north_coef, ee, ww, sea, area, area_e, area_w):
        nn = north_coef * sea * pltpu.roll(sea, YE - 1, 0)
        ss = pltpu.roll(nn, 1, 0)
        return (
            1.0 - area * (ee + ww + nn + ss),
            ee * area_e,
            ww * area_w,
            nn * pltpu.roll(area, YE - 1, 0),
            ss * pltpu.roll(area, 1, 0),
        )

    mains = five(coef_main[1], east_m, west_m, sea_m, area_m, area_me, area_mw)
    sides = five(coef_side[1], east_s, west_s, sea_s, area_s, area_se, area_sw)
    laneq = iota((Q, NX), 1)
    group, place = laneq // 32, laneq % 32
    gap = ((place >= 12) & (place < 16)) | (place >= 28)
    for i in range(5):
        fac_main_ref[i] = mains[i]
        coef_main[0] = jnp.where(lanes < 64, sides[i], mains[i])
        coef_main[1] = jnp.where(lanes < 64, mains[i], sides[i])
        strip = jnp.zeros((Q, NX), F32)
        for j in range(4):
            own = pl.ds(Q * j, Q)
            near = pltpu.roll(coef_main[0, own, :], (32 * j + 8) % NX, 1)
            far = pltpu.roll(coef_main[1, own, :], (32 * j + 20) % NX, 1)
            strip = jnp.where(group == j, jnp.where(place < 14, near, far), strip)
        fac_strip_ref[i, pl.ds(0, Q), :] = jnp.where(gap, 0.0, strip)


def send_body(
    count_ref, vert_hbm, thick_hbm, own_hbm, obs_hbm, cell_hbm, east_hbm, north_hbm, area_hbm, sea_hbm,
    full_ref, cells_ref, fac_main_ref, fac_strip_ref, matrix_ref,
    vert_ref, thick_ref, own_ref, obs_ref, cell_ref, east_ref, north_ref, area_ref, sea_ref,
    recv, load_sem, table, rows, outbox, coef_box, colbox, row_halo, col_halo, corner, coef_main, coef_side,
    cp_ref, dp_ref, idx_v, idx_ref, idx_sem, send_sem, recv_sem, side_send, side_recv,
):
    lon = lax.axis_index("lon")
    lat = lax.axis_index("lat")
    z, y, c = lax.div(lon, 8), lax.rem(lax.div(lon, 2), 4), lax.rem(lon, 2)
    me = lon * 4 + lat

    def target(k):
        q = lax.rem(k * STRIDE, DEV)
        dx, dc = lax.rem(q, 4), lax.rem(lax.div(q, 4), 2)
        dy, dz = lax.rem(lax.div(q, 8), 4), lax.div(q, 32)
        there = (lax.rem(z + dz, 4) * 4 + lax.rem(y + dy, 4)) * 2 + lax.rem(c + dc, 2)
        return there, lax.rem(lat + dx, 4)

    loads = []
    for number, (src, dst) in enumerate((
        (own_hbm, own_ref), (obs_hbm, obs_ref), (cell_hbm, cell_ref), (east_hbm, east_ref),
        (north_hbm, north_ref), (area_hbm, area_ref), (sea_hbm, sea_ref),
        (vert_hbm, vert_ref), (thick_hbm, thick_ref),
    )):
        load = pltpu.make_async_copy(src, dst, load_sem.at[number])
        load.start()
        loads.append(load)

    barrier = pltpu.get_barrier_semaphore()

    def greet(k, _):
        pl.semaphore_signal(barrier, inc=1, device_id=target(k), device_id_type=MESH)
        return 0

    lax.fori_loop(1, DEV, greet, 0)

    loads[0].wait()
    places(count_ref[0], own_ref, idx_v)
    idx_copy = pltpu.make_async_copy(idx_v, idx_ref, idx_sem)
    idx_copy.start()
    for load in loads[1:]:
        load.wait()

    def turn(b, _):
        columns = pl.ds(pl.multiple_of(b * NX, NX), NX)
        block = jnp.concatenate(
            [
                obs_ref[:, columns],
                cell_ref[pl.ds(b, 1), :].astype(F32),
                jnp.zeros((NX - LEV - 1, NX), F32),
            ],
            0,
        )
        table[columns, :] = block.T
        return 0

    lax.fori_loop(0, SLOTS // NX, turn, 0, unroll=4)
    spare = (iota((8, NX), 0) * 1024).astype(F32)
    table[pl.ds(SLOTS, 8), :] = jnp.where(iota((8, NX), 1) == LEV, spare, 0.0)

    lane = iota((NY, NX), 1)
    cols = jnp.zeros((NY, NX), F32)
    coef_refs = (east_ref, north_ref, area_ref, sea_ref)
    for i in range(4):
        whole = coef_refs[i][...].astype(F32)
        coef_box[i, pl.ds(0, 8), :] = whole[:8]
        coef_box[i, pl.ds(8, 8), :] = whole[NY - 8:]
        cols = jnp.where((lane >= 8 * i) & (lane < 8 * i + 4), pltpu.roll(whole, 8 * i, 1), cols)
        cols = jnp.where(
            (lane >= 8 * i + 4) & (lane < 8 * i + 8),
            pltpu.roll(whole, (8 * i + 4 - 124) % NX, 1),
            cols,
        )
    colbox[...] = cols
    idx_copy.wait()
    pl.semaphore_wait(barrier, DEV - 1)

    east, west = lax.rem(lon + 1, 32), lax.rem(lon + 31, 32)
    north, south = lax.rem(lat + 1, 4), lax.rem(lat + 3, 4)
    side = []

    def beside(number, src, dst, where):
        copy = pltpu.make_async_remote_copy(
            src_ref=src, dst_ref=dst, send_sem=side_send.at[number], recv_sem=side_recv.at[number],
            device_id=where, device_id_type=MESH,
        )
        copy.start()
        side.append(copy)

    beside(0, coef_box.at[:, pl.ds(8, 8), :], row_halo.at[0], (lon, north))
    beside(1, coef_box.at[:, pl.ds(0, 8), :], row_halo.at[1], (lon, south))
    beside(2, colbox, col_halo.at[0], (east, lat))
    beside(3, colbox, col_halo.at[1], (west, lat))
    beside(4, colbox.at[pl.ds(NY - 8, 8), :], corner.at[0], (east, north))
    beside(5, colbox.at[pl.ds(NY - 8, 8), :], corner.at[1], (west, north))
    beside(6, colbox.at[pl.ds(0, 8), :], corner.at[2], (east, south))
    beside(7, colbox.at[pl.ds(0, 8), :], corner.at[3], (west, south))

    lane8 = iota((8, NX), 1)
    lane32 = iota((32, NX), 1)

    def gather(owner):
        for k in range(CAP):
            at = jnp.minimum(jnp.maximum(idx_ref[owner, k], 0), SLOTS + 7)
            rows[pl.ds(k, 1), :] = table[pl.ds(at, 1), :]

    def fold(box):
        box[pl.ds(0, 32), :] = jnp.where(
            lane32 < 64, rows[pl.ds(0, 32), :], pltpu.roll(rows[pl.ds(32, 32), :], 64, 1)
        )
        rest = jnp.zeros((8, NX), F32)
        for g in range(8):
            piece = rows[pl.ds(8 * g, 8), :]
            shift = (16 * g - 64) % NX
            piece = pltpu.roll(piece, shift, 1) if shift else piece
            rest = jnp.where(lane8 // 16 == g, piece, rest)
        box[pl.ds(32, 8), :] = rest

    def send(k, _):
        dlon, dlat = target(k)
        owner = dlon * 4 + dlat
        gather(owner)
        fold(outbox.at[owner])
        pltpu.make_async_remote_copy(
            src_ref=outbox.at[owner], dst_ref=recv.at[k], send_sem=send_sem, recv_sem=recv_sem.at[k],
            device_id=(dlon, dlat), device_id_type=MESH,
        ).start()
        return 0

    lax.fori_loop(1, DEV, send, 0)
    gather(me)
    fold(recv.at[0])
    vertical_fourth(vert_ref, thick_ref, matrix_ref, cp_ref, dp_ref)
    for copy in side:
        copy.wait()
    factors(coef_refs, row_halo, col_halo, corner, coef_main, coef_side, fac_main_ref, fac_strip_ref)
    pick = jnp.where(
        iota((8, NX), 1) == 16 * iota((8, NX), 0) + (LEV - 64), 1.0, 0.0
    ).astype(F32)

    def unfold(k):
        rest = recv[k, pl.ds(32, 8), :]
        for g in range(8):
            tail = pltpu.roll(rest, (64 - 16 * g) % NX, 1) if g != 4 else rest
            head = recv[k, pl.ds(8 * (g % 4), 8), :]
            head = pltpu.roll(head, 64, 1) if g >= 4 else head
            full_ref[pl.ds(k * CAP + 8 * g, 8), :] = jnp.where(lane8 < 64, head, tail)

    def arrive(k, _):
        pltpu.make_async_copy(recv.at[k], recv.at[k], recv_sem.at[k]).wait()
        return 0

    def spread_out(k, _):
        unfold(k)
        return 0

    for b in range(8):
        lax.fori_loop(max(16 * b, 1), 16 * b + 16, arrive, 0)
        lax.fori_loop(16 * b, 16 * b + 16, spread_out, 0, unroll=4)
        part = recv[pl.ds(16 * b, 16), pl.ds(32, 8), :].reshape(NX, NX)
        found = lax.dot_general(
            pick, part, (((1,), (1,)), ((), ())), precision=HI, preferred_element_type=F32
        )
        cells_ref[pl.ds(8 * b, 8), :] = (found + 0.5).astype(jnp.int32)
    others = pl.ds(0, DEV - 1)
    pltpu.make_async_copy(outbox.at[others], outbox.at[others], send_sem).wait()


def send_profiles(count, vert_coef, inv_thick, owner, obs, cell, coefs):
    vm = pl.BlockSpec(memory_space=pltpu.VMEM)
    sm = pl.BlockSpec(memory_space=pltpu.SMEM)
    plane = pltpu.VMEM((4, YE, NX), F32)
    return pl.pallas_call(
        send_body,
        out_shape=(
            jax.ShapeDtypeStruct((SLOTS, NX), F32),
            jax.ShapeDtypeStruct((SLOTS // NX, NX), jnp.int32),
            jax.ShapeDtypeStruct((5, YE, NX), F32),
            jax.ShapeDtypeStruct((5, 24, NX), F32),
            jax.ShapeDtypeStruct((NX, NX), F32),
        ),
        in_specs=[sm] + [pl.BlockSpec(memory_space=pltpu.HBM)] * 9,
        out_specs=(vm,) * 5,
        scratch_shapes=[
            pltpu.SMEM((LEV - 1,), F32),
            pltpu.SMEM((LEV,), F32),
            pltpu.VMEM((SLOTS // NX, NX), jnp.int32),
            pltpu.VMEM((LEV, SLOTS), F32),
            pltpu.VMEM((SLOTS // NX, NX), jnp.int32),
            pltpu.VMEM((NY, NX), F32),
            pltpu.VMEM((NY, NX), F32),
            pltpu.VMEM((NY, NX), F32),
            pltpu.VMEM((NY, NX), jnp.int32),
            pltpu.VMEM((DEV, ROWS, NX), F32),
            pltpu.SemaphoreType.DMA((9,)),
            pltpu.VMEM((SLOTS + 8, NX), F32),
            pltpu.VMEM((CAP, NX), F32),
            pltpu.VMEM((DEV, ROWS, NX), F32),
            pltpu.VMEM((4, 16, NX), F32),
            pltpu.VMEM((NY, NX), F32),
            pltpu.VMEM((2, 4, 8, NX), F32),
            pltpu.VMEM((2, NY, NX), F32),
            pltpu.VMEM((4, 8, NX), F32),
            plane,
            plane,
            pltpu.VMEM((NX, NX), F32),
            pltpu.VMEM((NX, NX), F32),
            pltpu.VMEM((DEV, NX), jnp.int32),
            pltpu.SMEM((DEV, NX), jnp.int32),
            pltpu.SemaphoreType.DMA(()),
            pltpu.SemaphoreType.DMA(()),
            pltpu.SemaphoreType.DMA((DEV,)),
            pltpu.SemaphoreType.DMA((8,)),
            pltpu.SemaphoreType.DMA((8,)),
        ],
        compiler_params=pltpu.CompilerParams(
            collective_id=0, has_side_effects=True, vmem_limit_bytes=24 << 20
        ),
        name="send_profiles",
    )(count, *map(in_hbm, (
        vert_coef, inv_thick, owner.reshape(SLOTS // NX, NX), obs,
        cell.reshape(SLOTS // NX, NX), *coefs,
    )))


WAYS = 8


def add_body(full, cell_v, forcing_ref, matrix_ref, out_ref, acc0, acc1, acc2, acc3, acc4, acc5, acc6, acc7, cell_s, sem):
    accs = (acc0, acc1, acc2, acc3, acc4, acc5, acc6, acc7)
    copy = pltpu.make_async_copy(cell_v, cell_s, sem)
    copy.start()

    def clear(i, _):
        at = pl.ds(pl.multiple_of(i * 64, 64), 64)
        for acc in accs:
            acc[at, :] = jnp.zeros((64, NX), F32)
        return 0

    lax.fori_loop(0, SLOTS // 64, clear, 0, unroll=2)
    copy.wait()
    per = DEV // WAYS

    def add(s, _):
        starts = [pl.multiple_of((s + w * per) * CAP, CAP) for w in range(WAYS)]
        firsts = [(s + w * per) // 16 * 1024 + (s + w * per) % 16 * 8 for w in range(WAYS)]
        blocks = [full.at[pl.ds(start, CAP), :] for start in starts]
        for g in range(8):
            for e in range(8):
                places_of = [pl.ds(cell_s[first + (128 * g + e)], 1) for first in firsts]
                sums = [
                    acc[at, :] + block[pl.ds(8 * g + e, 1), :]
                    for acc, at, block in zip(accs, places_of, blocks)
                ]
                for acc, at, total in zip(accs, places_of, sums):
                    acc[at, :] = total
        return 0

    lax.fori_loop(0, per, add, 0)
    matrix = matrix_ref[pl.ds(0, LP), pl.ds(0, LEV)]

    def finish(b, _):
        loaded = []
        for h in range(2):
            y = 2 * b + h
            at = pl.ds(pl.multiple_of(y * NX, NX), NX)
            parts = [acc[at, :] for acc in accs]
            while len(parts) > 1:
                parts = [p + q for p, q in zip(parts[::2], parts[1::2])]
            total = parts[0]
            loaded.append(total.T[:LEV] + forcing_ref[pl.ds(y, LEV, stride=NY), :])
        product = jnp.dot(
            matrix, jnp.concatenate(loaded, 1), precision=HI, preferred_element_type=F32
        )
        out_ref[2 * b] = product[:, :NX]
        out_ref[2 * b + 1] = product[:, NX:]
        return 0

    lax.fori_loop(0, NY // 2, finish, 0, unroll=8)


def add_profiles(full, cells, forcing, matrix):
    vm = pl.BlockSpec(memory_space=pltpu.VMEM)
    return pl.pallas_call(
        add_body,
        out_shape=jax.ShapeDtypeStruct((NY, LP, NX), F32),
        in_specs=[vm, vm, vm, vm],
        out_specs=vm,
        scratch_shapes=[pltpu.VMEM((SLOTS, NX), F32)] * 8
        + [
            pltpu.SMEM((SLOTS,), jnp.int32),
            pltpu.SemaphoreType.DMA(()),
        ],
        compiler_params=pltpu.CompilerParams(vmem_limit_bytes=44 << 20),
        name="add_profiles",
    )(full, cells.reshape(SLOTS), forcing.reshape(LEV * NY, NX), matrix)


def spread_body(
    field_ref, fac_ref, strip_ref,
    out_ref,
    wide_a, wide_b, tips, strip_a, strip_b, east_box, west_box, from_west, from_east, corners,
    own_sem, send_sem, recv_sem,
):
    lon = lax.axis_index("lon")
    lat = lax.axis_index("lat")
    east, west = lax.rem(lon + 1, 32), lax.rem(lon + 31, 32)
    north, south = lax.rem(lat + 1, 4), lax.rem(lat + 3, 4)
    peers = [
        (lon, north), (lon, south), (east, lat), (west, lat),
        (east, north), (west, north), (east, south), (west, south),
    ]
    barrier = pltpu.get_barrier_semaphore()
    for peer in peers:
        pl.semaphore_signal(barrier, inc=1, device_id=peer, device_id_type=MESH)
    own = pltpu.make_async_copy(field_ref, wide_a.at[pl.ds(HALO, NY)], own_sem)
    own.start()
    own.wait()

    lane = iota((LP, NX), 1)
    group, place = lane // 32, lane % 32

    def tip(low, high, parts):
        def one(q, _):
            total = jnp.zeros((LP, NX), F32)
            for j in parts:
                piece = pltpu.roll(wide_a[q + Q * j], (32 * j + 8) % NX, 1)
                total = jnp.where((group == j) & (place < 16), piece, total)
            tips[q] = total
            return 0

        lax.fori_loop(low, high, one, 0, unroll=2)

    tip(0, HALO, (1, 2, 3))
    tip(HALO, Q - HALO, (0, 1, 2, 3))
    tip(Q - HALO, Q, (0, 1, 2))
    for b in range(3):
        e = jnp.zeros((LP, NX), F32)
        w = jnp.zeros((LP, NX), F32)
        for q in range(8 * b, min(8 * b + 8, Q)):
            here = place // 4 == q % 8
            row = tips[q]
            e = jnp.where(here, pltpu.roll(row, (4 * (q % 8) - 4) % NX, 1), e)
            w = jnp.where(here, pltpu.roll(row, (4 * (q % 8) - 8) % NX, 1), w)
        east_box[b] = e
        west_box[b] = w

    pl.semaphore_wait(barrier, 8)
    moves = [
        (field_ref.at[pl.ds(NY - HALO, HALO)], wide_a.at[pl.ds(0, HALO)]),
        (field_ref.at[pl.ds(0, HALO)], wide_a.at[pl.ds(NY + HALO, HALO)]),
        (east_box, from_west),
        (west_box, from_east),
        (east_box.at[1], corners.at[0]),
        (west_box.at[1], corners.at[1]),
        (east_box.at[0], corners.at[2]),
        (west_box.at[0], corners.at[3]),
    ]
    copies = []
    for number, (src, dst) in enumerate(moves):
        copy = pltpu.make_async_remote_copy(
            src_ref=src, dst_ref=dst, send_sem=send_sem.at[number], recv_sem=recv_sem.at[number],
            device_id=peers[number], device_id_type=MESH,
        )
        copy.start()
        copies.append(copy)

    def stencil(facs, y, src, at):
        centre = src[at]

        def fac(i):
            return jnp.broadcast_to(facs[i, pl.ds(y, 1), :], (LP, NX))

        return (
            fac(0) * centre
            + fac(1) * pltpu.roll(centre, NX - 1, 1)
            + fac(2) * pltpu.roll(centre, 1, 1)
            + fac(3) * src[at + 1]
            + fac(4) * src[at - 1]
        )

    def rows(t, low, high, unroll):
        src, dst = (wide_a, wide_b) if t % 2 else (wide_b, wide_a)

        def row(y, _):
            dst[y] = stencil(fac_ref, y, src, y)
            return 0

        lax.fori_loop(low, high, row, 0, unroll=unroll)

    for t in range(1, 5):
        rows(t, HALO + t, NY + HALO - t, 8)

    for copy in copies:
        copy.wait()

    for near, from_side in ((0, from_west), (1, from_east)):
        below, above = corners[near], corners[near + 2]
        from_side[0] = jnp.where(lane < 16, pltpu.roll(below, 24, 1), from_side[0])
        from_side[1] = jnp.where(lane >= 120, pltpu.roll(above, 104, 1), from_side[1])
        from_side[2] = jnp.where((lane >= 96) & (lane < 104), pltpu.roll(above, 72, 1), from_side[2])
    for h in range(HALO):
        q = Q - HALO + h
        tips[h] = jnp.where((group == 0) & (place < 16), pltpu.roll(wide_a[h], 8, 1), tips[h])
        tips[q] = jnp.where((group == 3) & (place < 16), pltpu.roll(wide_a[q + 3 * Q], 104, 1), tips[q])
    for q in range(Q):
        row = tips[q]
        right = pltpu.roll(from_east[q // 8], (8 - 4 * (q % 8)) % NX, 1)
        left = pltpu.roll(from_west[q // 8], (16 - 4 * (q % 8)) % NX, 1)
        far = jnp.where((place >= 16) & (place < 20), left, pltpu.roll(row, 12, 1))
        strip_a[q + 1] = jnp.where(place < 8, row, jnp.where(place < 12, right, far))

    for t in range(1, 5):
        rows(t, t, HALO + t, 4)
        rows(t, NY + HALO - t, NY + 2 * HALO - t, 4)
    for t in range(4):
        src, dst = (strip_a, strip_b) if t % 2 == 0 else (strip_b, strip_a)
        src[0] = pltpu.roll(src[Q], 32, 1)
        src[Q + 1] = pltpu.roll(src[1], NX - 32, 1)

        def strip(q, _):
            dst[q + 1] = stencil(strip_ref, q, src, q + 1)
            return 0

        lax.fori_loop(0, Q, strip, 0, unroll=6)

    edge = (lane < HALO) | (lane >= NX - HALO)

    def write(low, high, parts):
        def one(q, _):
            row = strip_a[q + 1]
            row = jnp.where(place < 8, row, pltpu.roll(row, NX - 12, 1))
            for j in parts:
                y = q + Q * j
                whole = jnp.where(edge, pltpu.roll(row, (120 - 32 * j) % NX, 1), wide_a[y])
                out_ref[pl.ds(y - HALO, LEV, stride=NY), :] = whole[:LEV]
            return 0

        lax.fori_loop(low, high, one, 0, unroll=2)

    write(0, HALO, (1, 2, 3))
    write(HALO, Q - HALO, (0, 1, 2, 3))
    write(Q - HALO, Q, (0, 1, 2))


def spread(field, fac_main, fac_strip):
    vm = pl.BlockSpec(memory_space=pltpu.VMEM)
    wide = pltpu.VMEM((YE, LP, NX), F32)
    strip = pltpu.VMEM((Q + 2, LP, NX), F32)
    box = pltpu.VMEM((3, LP, NX), F32)
    return pl.pallas_call(
        spread_body,
        out_shape=jax.ShapeDtypeStruct((LEV * NY, NX), F32),
        in_specs=[pl.BlockSpec(memory_space=pl.ANY), vm, vm],
        out_specs=vm,
        scratch_shapes=[
            wide, wide, pltpu.VMEM((Q, LP, NX), F32), strip, strip, box, box, box, box,
            pltpu.VMEM((4, LP, NX), F32),
            pltpu.SemaphoreType.DMA(()),
            pltpu.SemaphoreType.DMA((8,)),
            pltpu.SemaphoreType.DMA((8,)),
        ],
        compiler_params=pltpu.CompilerParams(
            collective_id=1, has_side_effects=True, vmem_limit_bytes=24 << 20
        ),
        name="spread",
    )(field, fac_main, fac_strip)


def local(
    forcing, obs_values, obs_owner, obs_cell, obs_count,
    coef_east, coef_north, area_inv, sea_mask, vert_coef, inv_thick,
):
    coefs = (coef_east, coef_north, area_inv, sea_mask)
    full, cells, fac_main, fac_strip, matrix = send_profiles(
        obs_count, vert_coef, inv_thick, obs_owner, obs_values, obs_cell, coefs
    )
    field = add_profiles(full, cells, forcing, matrix)
    return spread(field, fac_main, fac_strip).reshape(LEV, NY, NX)


def solution(mesh):
    lead = P(("lon", "lat"))
    flat = P("lat", "lon")
    in_specs = (
        P(None, "lat", "lon"), P(None, ("lon", "lat")), lead, lead, lead,
        flat, flat, flat, flat, P(), P(),
    )
    return jax.shard_map(
        local, mesh=mesh, in_specs=in_specs, out_specs=P(None, "lat", "lon"), check_vma=False
    )
```

```python
import jax
import jax.numpy as jnp
from jax import lax
from jax.experimental import pallas as pl
from jax.experimental.pallas import tpu as pltpu
from jax.sharding import PartitionSpec as P

LEV = 75
LP = 80
NX = 128
NY = 64
DEV = 128
CAP = 64
SLOTS = 8192
ROWS = 40
HALO = 4
YE = NY + 2 * HALO
Q = 18
STRIDE = 27
F32 = jnp.float32
BF16 = jnp.bfloat16
HI = lax.Precision.HIGHEST
MESH = pl.DeviceIdType.MESH


def in_hbm(x):
    return pltpu.with_memory_space_constraint(x, pltpu.HBM)


def iota(shape, dim, dtype=jnp.int32):
    return lax.broadcasted_iota(dtype, shape, dim)


def vertical_fourth(vert_ref, thick_ref, out_ref, cp_ref, dp_ref):
    lane = iota((1, NX), 1)
    dp_ref[...] = jnp.zeros_like(dp_ref)

    def forward(i, carry):
        cp, dp = carry
        up = jnp.where(i < LEV - 1, vert_ref[jnp.minimum(i, LEV - 2)], 0.0)
        low = jnp.where(i > 0, vert_ref[jnp.maximum(i - 1, 0)], 0.0)
        middle = 1.0 + (low + up) * thick_ref[i]
        above = -thick_ref[jnp.minimum(i + 1, LEV - 1)] * up
        below = -thick_ref[jnp.maximum(i - 1, 0)] * low
        inv = 1.0 / (middle - below * cp)
        cp = above * inv
        dp = (jnp.where(lane == i, 1.0, 0.0) - below * dp) * inv
        cp_ref[pl.ds(i, 1), :] = cp
        dp_ref[pl.ds(i, 1), :] = dp
        return cp, dp

    zero = jnp.zeros((1, NX), F32)
    lax.fori_loop(0, LEV, forward, (zero, zero))

    def backward(j, x):
        i = LEV - 1 - j
        x = dp_ref[pl.ds(i, 1), :] - cp_ref[pl.ds(i, 1), :] * x
        dp_ref[pl.ds(i, 1), :] = x
        return x

    lax.fori_loop(0, LEV, backward, zero)
    single = dp_ref[...]
    double = jnp.dot(single, single, precision=HI, preferred_element_type=F32)
    out_ref[...] = jnp.dot(double, double, precision=HI, preferred_element_type=F32)


def places(count, own_ref, idx_ref):
    width = 256
    lane = iota((1, width), 1)
    owners = iota((DEV, width), 0)
    tri = (iota((width, width + NX), 0) <= iota((width, width + NX), 1)) | (
        iota((width, width + NX), 1) >= width
    )
    tri = tri.astype(F32).astype(BF16)
    kth = iota((CAP, width), 0).astype(F32)
    number = (iota((CAP, width), 1) + 1).astype(F32)
    acc_lane = iota((DEV, NX), 1)

    def step(b, carry):
        offset, acc = carry
        own = jnp.concatenate([own_ref[pl.ds(2 * b, 1), :], own_ref[pl.ds(2 * b + 1, 1), :]], 1)
        own = jnp.where(lane + b * width < count, own, -1)
        onehot = jnp.where(jnp.broadcast_to(own, (DEV, width)) == owners, 1.0, 0.0)
        ones = onehot.astype(BF16)
        prefix = jnp.dot(ones, tri, preferred_element_type=F32)
        rank = prefix[:, :width] + jnp.concatenate([offset, offset], 1)
        rank = jnp.sum(onehot * rank, axis=0, keepdims=True) - 1.0
        hit = jnp.where(jnp.broadcast_to(rank, (CAP, width)) == kth, 1.0, 0.0)
        both = jnp.concatenate([hit, hit * number], 0).astype(BF16)
        found = lax.dot_general(ones, both, (((1,), (1,)), ((), ())), preferred_element_type=F32)
        scale = jnp.where(acc_lane < CAP, (b * width).astype(F32), 1.0)
        return offset + prefix[:, width:], acc + found * scale

    zero = jnp.zeros((DEV, NX), F32)
    _, acc = lax.fori_loop(0, SLOTS // width, step, (zero, zero), unroll=16)
    total = (acc + pltpu.roll(acc, CAP, 1)).astype(jnp.int32)
    idx_ref[...] = jnp.clip(jnp.where(total > 0, total - 1, SLOTS + acc_lane % 8), 0, SLOTS + 7)


def factors(coef_refs, row_halo_ref, col_halo_ref, corner_ref, coef_main, coef_side, fac_main_ref, fac_strip_ref):
    lat = lax.axis_index("lat")
    lane64 = iota((NY, NX), 1)
    lane4 = iota((HALO, NX), 1)
    for i in range(4):
        coef_main[i, pl.ds(HALO, NY), :] = coef_refs[i][...].astype(F32)
        coef_main[i, pl.ds(0, HALO), :] = row_halo_ref[0, i, pl.ds(4, HALO), :]
        coef_main[i, pl.ds(NY + HALO, HALO), :] = row_halo_ref[1, i, pl.ds(0, HALO), :]

        def sides(lanes, left, right, i=i):
            return jnp.where(
                lanes < 64,
                pltpu.roll(right, (-8 * i) % NX, 1),
                pltpu.roll(left, (124 - 8 * i - 4) % NX, 1),
            )

        coef_side[i, pl.ds(HALO, NY), :] = sides(lane64, col_halo_ref[0], col_halo_ref[1])
        coef_side[i, pl.ds(0, HALO), :] = sides(
            lane4, corner_ref[0, pl.ds(4, HALO), :], corner_ref[1, pl.ds(4, HALO), :]
        )
        coef_side[i, pl.ds(NY + HALO, HALO), :] = sides(
            lane4, corner_ref[2, pl.ds(0, HALO), :], corner_ref[3, pl.ds(0, HALO), :]
        )
    row = iota((YE, NX), 0)
    first_row = jnp.where(lat == 0, HALO, 0)
    last_row = jnp.where(lat == 3, NY + HALO, YE)
    inside = (row >= first_row) & (row < last_row)
    lanes = iota((YE, NX), 1)

    def shifts(main, side):
        first, last = lanes == 0, lanes == NX - 1
        main_e = pltpu.roll(jnp.where(first, side, main), NX - 1, 1)
        side_e = pltpu.roll(jnp.where(first, main, side), NX - 1, 1)
        main_w = pltpu.roll(jnp.where(last, side, main), 1, 1)
        side_w = pltpu.roll(jnp.where(last, main, side), 1, 1)
        return main_e, side_e, main_w, side_w

    sea_m = jnp.where(inside, coef_main[3], 0.0)
    sea_s = jnp.where(inside, coef_side[3], 0.0)
    area_m, area_s = coef_main[2], coef_side[2]
    sea_me, sea_se, _, _ = shifts(sea_m, sea_s)
    east_m = coef_main[0] * sea_m * sea_me
    east_s = coef_side[0] * sea_s * sea_se
    _, _, west_m, west_s = shifts(east_m, east_s)
    area_me, area_se, area_mw, area_sw = shifts(area_m, area_s)

    def five(north_coef, ee, ww, sea, area, area_e, area_w):
        nn = north_coef * sea * pltpu.roll(sea, YE - 1, 0)
        ss = pltpu.roll(nn, 1, 0)
        return (
            1.0 - area * (ee + ww + nn + ss),
            ee * area_e,
            ww * area_w,
            nn * pltpu.roll(area, YE - 1, 0),
            ss * pltpu.roll(area, 1, 0),
        )

    mains = five(coef_main[1], east_m, west_m, sea_m, area_m, area_me, area_mw)
    sides = five(coef_side[1], east_s, west_s, sea_s, area_s, area_se, area_sw)
    laneq = iota((Q, NX), 1)
    group, place = laneq // 32, laneq % 32
    gap = ((place >= 12) & (place < 16)) | (place >= 28)
    for i in range(5):
        fac_main_ref[i] = mains[i]
        coef_main[0] = jnp.where(lanes < 64, sides[i], mains[i])
        coef_main[1] = jnp.where(lanes < 64, mains[i], sides[i])
        strip = jnp.zeros((Q, NX), F32)
        for j in range(4):
            own = pl.ds(Q * j, Q)
            near = pltpu.roll(coef_main[0, own, :], (32 * j + 8) % NX, 1)
            far = pltpu.roll(coef_main[1, own, :], (32 * j + 20) % NX, 1)
            strip = jnp.where(group == j, jnp.where(place < 14, near, far), strip)
        fac_strip_ref[i, pl.ds(0, Q), :] = jnp.where(gap, 0.0, strip)


def clear(refs):
    def some(i, _):
        at = pl.ds(pl.multiple_of(i * 64, 64), 64)
        for ref in refs:
            ref[at, :] = jnp.zeros((64, NX), F32)
        return 0

    lax.fori_loop(0, SLOTS // 64, some, 0, unroll=2)


def send_body(
    count_ref, vert_hbm, thick_hbm, own_hbm, obs_hbm, cell_hbm, east_hbm, north_hbm, area_hbm, sea_hbm,
    full_ref, cells_ref, fac_main_ref, fac_strip_ref, matrix_ref, sum0, sum1, sum2, sum3,
    vert_ref, thick_ref, own_ref, obs_ref, cell_ref, east_ref, north_ref, area_ref, sea_ref,
    recv, load_sem, table, rows, outbox, coef_box, colbox, row_halo, col_halo, corner, coef_main, coef_side,
    cp_ref, dp_ref, idx_v, idx_ref, idx_sem, send_sem, recv_sem, side_send, side_recv,
):
    lon = lax.axis_index("lon")
    lat = lax.axis_index("lat")
    z, y, c = lax.div(lon, 8), lax.rem(lax.div(lon, 2), 4), lax.rem(lon, 2)
    me = lon * 4 + lat

    def target(k):
        q = lax.rem(k * STRIDE, DEV)
        dx, dc = lax.rem(q, 4), lax.rem(lax.div(q, 4), 2)
        dy, dz = lax.rem(lax.div(q, 8), 4), lax.div(q, 32)
        there = (lax.rem(z + dz, 4) * 4 + lax.rem(y + dy, 4)) * 2 + lax.rem(c + dc, 2)
        return there, lax.rem(lat + dx, 4)

    loads = []
    for number, (src, dst) in enumerate((
        (own_hbm, own_ref), (obs_hbm, obs_ref), (cell_hbm, cell_ref), (east_hbm, east_ref),
        (north_hbm, north_ref), (area_hbm, area_ref), (sea_hbm, sea_ref),
        (vert_hbm, vert_ref), (thick_hbm, thick_ref),
    )):
        load = pltpu.make_async_copy(src, dst, load_sem.at[number])
        load.start()
        loads.append(load)

    barrier = pltpu.get_barrier_semaphore()

    def greet(k, _):
        pl.semaphore_signal(barrier, inc=1, device_id=target(k), device_id_type=MESH)
        return 0

    lax.fori_loop(1, DEV, greet, 0)

    loads[0].wait()
    places(count_ref[0], own_ref, idx_v)
    idx_copy = pltpu.make_async_copy(idx_v, idx_ref, idx_sem)
    idx_copy.start()
    for load in loads[1:]:
        load.wait()

    def turn(b, _):
        columns = pl.ds(pl.multiple_of(b * NX, NX), NX)
        block = jnp.concatenate(
            [
                obs_ref[:, columns],
                cell_ref[pl.ds(b, 1), :].astype(F32),
                jnp.zeros((NX - LEV - 1, NX), F32),
            ],
            0,
        )
        table[columns, :] = block.T
        return 0

    lax.fori_loop(0, SLOTS // NX, turn, 0, unroll=4)
    spare = (iota((8, NX), 0) * 1024).astype(F32)
    table[pl.ds(SLOTS, 8), :] = jnp.where(iota((8, NX), 1) == LEV, spare, 0.0)

    lane = iota((NY, NX), 1)
    cols = jnp.zeros((NY, NX), F32)
    coef_refs = (east_ref, north_ref, area_ref, sea_ref)
    for i in range(4):
        whole = coef_refs[i][...].astype(F32)
        coef_box[i, pl.ds(0, 8), :] = whole[:8]
        coef_box[i, pl.ds(8, 8), :] = whole[NY - 8:]
        cols = jnp.where((lane >= 8 * i) & (lane < 8 * i + 4), pltpu.roll(whole, 8 * i, 1), cols)
        cols = jnp.where(
            (lane >= 8 * i + 4) & (lane < 8 * i + 8),
            pltpu.roll(whole, (8 * i + 4 - 124) % NX, 1),
            cols,
        )
    colbox[...] = cols
    idx_copy.wait()
    pl.semaphore_wait(barrier, DEV - 1)

    east, west = lax.rem(lon + 1, 32), lax.rem(lon + 31, 32)
    north, south = lax.rem(lat + 1, 4), lax.rem(lat + 3, 4)
    side = []

    def beside(number, src, dst, where):
        copy = pltpu.make_async_remote_copy(
            src_ref=src, dst_ref=dst, send_sem=side_send.at[number], recv_sem=side_recv.at[number],
            device_id=where, device_id_type=MESH,
        )
        copy.start()
        side.append(copy)

    beside(0, coef_box.at[:, pl.ds(8, 8), :], row_halo.at[0], (lon, north))
    beside(1, coef_box.at[:, pl.ds(0, 8), :], row_halo.at[1], (lon, south))
    beside(2, colbox, col_halo.at[0], (east, lat))
    beside(3, colbox, col_halo.at[1], (west, lat))
    beside(4, colbox.at[pl.ds(NY - 8, 8), :], corner.at[0], (east, north))
    beside(5, colbox.at[pl.ds(NY - 8, 8), :], corner.at[1], (west, north))
    beside(6, colbox.at[pl.ds(0, 8), :], corner.at[2], (east, south))
    beside(7, colbox.at[pl.ds(0, 8), :], corner.at[3], (west, south))

    lane8 = iota((8, NX), 1)
    lane32 = iota((32, NX), 1)

    def gather(owner):
        for k in range(CAP):
            at = jnp.minimum(jnp.maximum(idx_ref[owner, k], 0), SLOTS + 7)
            rows[pl.ds(k, 1), :] = table[pl.ds(at, 1), :]

    def fold(box):
        box[pl.ds(0, 32), :] = jnp.where(
            lane32 < 64, rows[pl.ds(0, 32), :], pltpu.roll(rows[pl.ds(32, 32), :], 64, 1)
        )
        rest = jnp.zeros((8, NX), F32)
        for g in range(8):
            piece = rows[pl.ds(8 * g, 8), :]
            shift = (16 * g - 64) % NX
            piece = pltpu.roll(piece, shift, 1) if shift else piece
            rest = jnp.where(lane8 // 16 == g, piece, rest)
        box[pl.ds(32, 8), :] = rest

    def send(k, _):
        dlon, dlat = target(k)
        owner = dlon * 4 + dlat
        gather(owner)
        fold(outbox.at[owner])
        pltpu.make_async_remote_copy(
            src_ref=outbox.at[owner], dst_ref=recv.at[k], send_sem=send_sem, recv_sem=recv_sem.at[k],
            device_id=(dlon, dlat), device_id_type=MESH,
        ).start()
        return 0

    lax.fori_loop(1, DEV, send, 0)
    gather(me)
    fold(recv.at[0])
    vertical_fourth(vert_ref, thick_ref, matrix_ref, cp_ref, dp_ref)
    for copy in side:
        copy.wait()
    factors(coef_refs, row_halo, col_halo, corner, coef_main, coef_side, fac_main_ref, fac_strip_ref)
    clear((sum0, sum1, sum2, sum3))

    pick = jnp.where(
        iota((8, NX), 1) == 16 * iota((8, NX), 0) + (LEV - 64), 1.0, 0.0
    ).astype(F32)

    def unfold(k):
        rest = recv[k, pl.ds(32, 8), :]
        for g in range(8):
            tail = pltpu.roll(rest, (64 - 16 * g) % NX, 1) if g != 4 else rest
            head = recv[k, pl.ds(8 * (g % 4), 8), :]
            head = pltpu.roll(head, 64, 1) if g >= 4 else head
            full_ref[pl.ds(k * CAP + 8 * g, 8), :] = jnp.where(lane8 < 64, head, tail)

    def arrive(k, _):
        pltpu.make_async_copy(recv.at[k], recv.at[k], recv_sem.at[k]).wait()
        return 0

    def spread_out(k, _):
        unfold(k)
        return 0

    for b in range(8):
        lax.fori_loop(max(16 * b, 1), 16 * b + 16, arrive, 0)
        lax.fori_loop(16 * b, 16 * b + 16, spread_out, 0, unroll=4)
        part = recv[pl.ds(16 * b, 16), pl.ds(32, 8), :].reshape(NX, NX)
        found = lax.dot_general(
            pick, part, (((1,), (1,)), ((), ())), precision=HI, preferred_element_type=F32
        )
        cells_ref[pl.ds(8 * b, 8), :] = (found + 0.5).astype(jnp.int32)
    others = pl.ds(0, DEV - 1)
    pltpu.make_async_copy(outbox.at[others], outbox.at[others], send_sem).wait()


def send_profiles(count, vert_coef, inv_thick, owner, obs, cell, coefs):
    vm = pl.BlockSpec(memory_space=pltpu.VMEM)
    sm = pl.BlockSpec(memory_space=pltpu.SMEM)
    plane = pltpu.VMEM((4, YE, NX), F32)
    return pl.pallas_call(
        send_body,
        out_shape=(
            jax.ShapeDtypeStruct((SLOTS, NX), F32),
            jax.ShapeDtypeStruct((SLOTS // NX, NX), jnp.int32),
            jax.ShapeDtypeStruct((5, YE, NX), F32),
            jax.ShapeDtypeStruct((5, 24, NX), F32),
            jax.ShapeDtypeStruct((NX, NX), F32),
        ) + (jax.ShapeDtypeStruct((SLOTS, NX), F32),) * EARLY,
        in_specs=[sm] + [pl.BlockSpec(memory_space=pltpu.HBM)] * 9,
        out_specs=(vm,) * (5 + EARLY),
        scratch_shapes=[
            pltpu.SMEM((LEV - 1,), F32),
            pltpu.SMEM((LEV,), F32),
            pltpu.VMEM((SLOTS // NX, NX), jnp.int32),
            pltpu.VMEM((LEV, SLOTS), F32),
            pltpu.VMEM((SLOTS // NX, NX), jnp.int32),
            pltpu.VMEM((NY, NX), F32),
            pltpu.VMEM((NY, NX), F32),
            pltpu.VMEM((NY, NX), F32),
            pltpu.VMEM((NY, NX), jnp.int32),
            pltpu.VMEM((DEV, ROWS, NX), F32),
            pltpu.SemaphoreType.DMA((9,)),
            pltpu.VMEM((SLOTS + 8, NX), F32),
            pltpu.VMEM((CAP, NX), F32),
            pltpu.VMEM((DEV, ROWS, NX), F32),
            pltpu.VMEM((4, 16, NX), F32),
            pltpu.VMEM((NY, NX), F32),
            pltpu.VMEM((2, 4, 8, NX), F32),
            pltpu.VMEM((2, NY, NX), F32),
            pltpu.VMEM((4, 8, NX), F32),
            plane,
            plane,
            pltpu.VMEM((NX, NX), F32),
            pltpu.VMEM((NX, NX), F32),
            pltpu.VMEM((DEV, NX), jnp.int32),
            pltpu.SMEM((DEV, NX), jnp.int32),
            pltpu.SemaphoreType.DMA(()),
            pltpu.SemaphoreType.DMA(()),
            pltpu.SemaphoreType.DMA((DEV,)),
            pltpu.SemaphoreType.DMA((8,)),
            pltpu.SemaphoreType.DMA((8,)),
        ],
        compiler_params=pltpu.CompilerParams(
            collective_id=0, has_side_effects=True, vmem_limit_bytes=18 << 20
        ),
        name="send_profiles",
    )(count, *map(in_hbm, (
        vert_coef, inv_thick, owner.reshape(SLOTS // NX, NX), obs,
        cell.reshape(SLOTS // NX, NX), *coefs,
    )))


WAYS = 8
EARLY = 4


def add_body(
    full, cell_v, forcing_ref, matrix_ref, in0, in1, in2, in3, out_ref,
    acc0, acc1, acc2, acc3, acc4, acc5, acc6, acc7, cell_s, sem,
):
    accs = (acc0, acc1, acc2, acc3, acc4, acc5, acc6, acc7)
    copy = pltpu.make_async_copy(cell_v, cell_s, sem)
    copy.start()

    clear(accs[EARLY:])
    copy.wait()
    per = DEV // WAYS

    def add(s, _):
        starts = [pl.multiple_of((s + w * per) * CAP, CAP) for w in range(WAYS)]
        firsts = [(s + w * per) // 16 * 1024 + (s + w * per) % 16 * 8 for w in range(WAYS)]
        blocks = [full.at[pl.ds(start, CAP), :] for start in starts]
        for g in range(8):
            for e in range(8):
                places_of = [pl.ds(cell_s[first + (128 * g + e)], 1) for first in firsts]
                sums = [
                    acc[at, :] + block[pl.ds(8 * g + e, 1), :]
                    for acc, at, block in zip(accs, places_of, blocks)
                ]
                for acc, at, total in zip(accs, places_of, sums):
                    acc[at, :] = total
        return 0

    lax.fori_loop(0, per, add, 0)
    whole = matrix_ref[pl.ds(0, LP), pl.ds(0, LP)]
    high = whole.astype(BF16)
    low = (whole - high.astype(F32)).astype(BF16)
    matrix = jnp.concatenate([high, high, low], 1)
    padding = jnp.zeros((LP - LEV, NX), F32)

    def finish(b, _):
        loaded = []
        for h in range(2):
            y = 2 * b + h
            at = pl.ds(pl.multiple_of(y * NX, NX), NX)
            parts = [acc[at, :] for acc in accs]
            while len(parts) > 1:
                parts = [p + q for p, q in zip(parts[::2], parts[1::2])]
            total = parts[0]
            column = total.T[:LEV] + forcing_ref[pl.ds(y, LEV, stride=NY), :]
            loaded.append(jnp.concatenate([column, padding], 0))
        values = jnp.concatenate(loaded, 1)
        top = values.astype(BF16)
        rest = (values - top.astype(F32)).astype(BF16)
        parts = jnp.concatenate([top, rest, top], 0)
        product = jnp.dot(matrix, parts, preferred_element_type=F32)
        out_ref[2 * b] = product[:, :NX]
        out_ref[2 * b + 1] = product[:, NX:]
        return 0

    lax.fori_loop(0, NY // 2, finish, 0, unroll=8)


def add_profiles(full, cells, forcing, matrix, sums):
    vm = pl.BlockSpec(memory_space=pltpu.VMEM)
    return pl.pallas_call(
        add_body,
        out_shape=(jax.ShapeDtypeStruct((NY, LP, NX), F32),)
        + (jax.ShapeDtypeStruct((SLOTS, NX), F32),) * EARLY,
        in_specs=[vm] * (4 + EARLY),
        out_specs=(vm,) * (1 + EARLY),
        input_output_aliases={4 + w: 1 + w for w in range(EARLY)},
        scratch_shapes=[pltpu.VMEM((SLOTS, NX), F32)] * (WAYS - EARLY)
        + [
            pltpu.SMEM((SLOTS,), jnp.int32),
            pltpu.SemaphoreType.DMA(()),
        ],
        compiler_params=pltpu.CompilerParams(vmem_limit_bytes=22 << 20),
        name="add_profiles",
    )(full, cells.reshape(SLOTS), forcing.reshape(LEV * NY, NX), matrix, *sums)[0]


def spread_body(
    field_ref, fac_ref, strip_ref,
    out_ref,
    wide_a, wide_b, tips, strip_a, strip_b, east_box, west_box, from_west, from_east, corner_box, corners,
    own_sem, send_sem, recv_sem,
):
    lon = lax.axis_index("lon")
    lat = lax.axis_index("lat")
    east, west = lax.rem(lon + 1, 32), lax.rem(lon + 31, 32)
    north, south = lax.rem(lat + 1, 4), lax.rem(lat + 3, 4)
    peers = [
        (lon, north), (lon, south), (east, lat), (west, lat),
        (east, north), (west, north), (east, south), (west, south),
    ]
    barrier = pltpu.get_barrier_semaphore()
    for peer in peers:
        pl.semaphore_signal(barrier, inc=1, device_id=peer, device_id_type=MESH)
    own = pltpu.make_async_copy(field_ref, wide_a.at[pl.ds(HALO, NY)], own_sem)
    own.start()
    own.wait()

    lane = iota((LP, NX), 1)
    group, place = lane // 32, lane % 32

    def tip(low, high, parts):
        def one(q, _):
            total = jnp.zeros((LP, NX), F32)
            for j in parts:
                piece = pltpu.roll(wide_a[q + Q * j], (32 * j + 8) % NX, 1)
                total = jnp.where((group == j) & (place < 16), piece, total)
            tips[q] = total
            return 0

        lax.fori_loop(low, high, one, 0, unroll=2)

    tip(0, HALO, (1, 2, 3))
    tip(HALO, Q - HALO, (0, 1, 2, 3))
    tip(Q - HALO, Q, (0, 1, 2))
    for b in range(3):
        e = jnp.zeros((LP, NX), F32)
        w = jnp.zeros((LP, NX), F32)
        for q in range(8 * b, min(8 * b + 8, Q)):
            here = place // 4 == q % 8
            row = tips[q]
            e = jnp.where(here, pltpu.roll(row, (4 * (q % 8) - 4) % NX, 1), e)
            w = jnp.where(here, pltpu.roll(row, (4 * (q % 8) - 8) % NX, 1), w)
        east_box[b] = e
        west_box[b] = w

    lane16 = iota((16, NX), 1)
    for number, (box, start) in enumerate(
        ((east_box.at[1], 104), (west_box.at[1], 104), (east_box.at[0], 16), (west_box.at[0], 16))
    ):
        total = jnp.zeros((16, NX), F32)
        for h in range(LP // 16):
            piece = pltpu.roll(box[pl.ds(16 * h, 16), :], (16 * h - start) % NX, 1)
            total = jnp.where(lane16 // 16 == h, piece, total)
        corner_box[number] = total

    pl.semaphore_wait(barrier, 8)
    moves = [
        (field_ref.at[pl.ds(NY - HALO, HALO)], wide_a.at[pl.ds(0, HALO)]),
        (field_ref.at[pl.ds(0, HALO)], wide_a.at[pl.ds(NY + HALO, HALO)]),
        (east_box, from_west),
        (west_box, from_east),
        (corner_box.at[0], corners.at[0]),
        (corner_box.at[1], corners.at[1]),
        (corner_box.at[2], corners.at[2]),
        (corner_box.at[3], corners.at[3]),
    ]
    copies = []
    for number, (src, dst) in enumerate(moves):
        copy = pltpu.make_async_remote_copy(
            src_ref=src, dst_ref=dst, send_sem=send_sem.at[number], recv_sem=recv_sem.at[number],
            device_id=peers[number], device_id_type=MESH,
        )
        copy.start()
        copies.append(copy)

    def stencil(facs, y, src, at):
        centre = src[at]

        def fac(i):
            return jnp.broadcast_to(facs[i, pl.ds(y, 1), :], (LP, NX))

        return (
            fac(0) * centre
            + fac(1) * pltpu.roll(centre, NX - 1, 1)
            + fac(2) * pltpu.roll(centre, 1, 1)
            + fac(3) * src[at + 1]
            + fac(4) * src[at - 1]
        )

    def rows(t, low, high, unroll):
        src, dst = (wide_a, wide_b) if t % 2 else (wide_b, wide_a)

        def row(y, _):
            dst[y] = stencil(fac_ref, y, src, y)
            return 0

        lax.fori_loop(low, high, row, 0, unroll=unroll)

    for t in range(1, 5):
        rows(t, HALO + t, NY + HALO - t, 8)

    for copy in copies:
        copy.wait()

    for near, from_side in ((0, from_west), (1, from_east)):
        below, above = corners[near], corners[near + 2]
        for h in range(LP // 16):
            at = pl.ds(16 * h, 16)

            def put(box, keep, corner, shift, at=at, from_side=from_side):
                box_rows = from_side[box, at, :]
                piece = pltpu.roll(corner, shift % NX, 1) if shift % NX else corner
                from_side[box, at, :] = jnp.where(keep, piece, box_rows)

            put(0, lane16 < 16, below, -16 * h)
            put(1, lane16 >= 120, above, 120 - 16 * h)
            put(2, (lane16 >= 96) & (lane16 < 104), above, 88 - 16 * h)
    for h in range(HALO):
        q = Q - HALO + h
        tips[h] = jnp.where((group == 0) & (place < 16), pltpu.roll(wide_a[h], 8, 1), tips[h])
        tips[q] = jnp.where((group == 3) & (place < 16), pltpu.roll(wide_a[q + 3 * Q], 104, 1), tips[q])
    for q in range(Q):
        row = tips[q]
        right = pltpu.roll(from_east[q // 8], (8 - 4 * (q % 8)) % NX, 1)
        left = pltpu.roll(from_west[q // 8], (16 - 4 * (q % 8)) % NX, 1)
        far = jnp.where((place >= 16) & (place < 20), left, pltpu.roll(row, 12, 1))
        strip_a[q + 1] = jnp.where(place < 8, row, jnp.where(place < 12, right, far))

    for t in range(1, 5):
        rows(t, t, HALO + t, 4)
        rows(t, NY + HALO - t, NY + 2 * HALO - t, 4)
    for t in range(4):
        src, dst = (strip_a, strip_b) if t % 2 == 0 else (strip_b, strip_a)
        src[0] = pltpu.roll(src[Q], 32, 1)
        src[Q + 1] = pltpu.roll(src[1], NX - 32, 1)

        def strip(q, _):
            dst[q + 1] = stencil(strip_ref, q, src, q + 1)
            return 0

        lax.fori_loop(0, Q, strip, 0, unroll=6)

    edge = (lane < HALO) | (lane >= NX - HALO)

    def write(low, high, parts):
        def one(q, _):
            row = strip_a[q + 1]
            row = jnp.where(place < 8, row, pltpu.roll(row, NX - 12, 1))
            for j in parts:
                y = q + Q * j
                whole = jnp.where(edge, pltpu.roll(row, (120 - 32 * j) % NX, 1), wide_a[y])
                out_ref[pl.ds(y - HALO, LEV, stride=NY), :] = whole[:LEV]
            return 0

        lax.fori_loop(low, high, one, 0, unroll=2)

    write(0, HALO, (1, 2, 3))
    write(HALO, Q - HALO, (0, 1, 2, 3))
    write(Q - HALO, Q, (0, 1, 2))


def spread(field, fac_main, fac_strip):
    vm = pl.BlockSpec(memory_space=pltpu.VMEM)
    wide = pltpu.VMEM((YE, LP, NX), F32)
    strip = pltpu.VMEM((Q + 2, LP, NX), F32)
    box = pltpu.VMEM((3, LP, NX), F32)
    return pl.pallas_call(
        spread_body,
        out_shape=jax.ShapeDtypeStruct((LEV * NY, NX), F32),
        in_specs=[pl.BlockSpec(memory_space=pl.ANY), vm, vm],
        out_specs=vm,
        scratch_shapes=[
            wide, wide, pltpu.VMEM((Q, LP, NX), F32), strip, strip, box, box, box, box,
            pltpu.VMEM((4, 16, NX), F32),
            pltpu.VMEM((4, 16, NX), F32),
            pltpu.SemaphoreType.DMA(()),
            pltpu.SemaphoreType.DMA((8,)),
            pltpu.SemaphoreType.DMA((8,)),
        ],
        compiler_params=pltpu.CompilerParams(
            collective_id=1, has_side_effects=True, vmem_limit_bytes=24 << 20
        ),
        name="spread",
    )(field, fac_main, fac_strip)


def local(
    forcing, obs_values, obs_owner, obs_cell, obs_count,
    coef_east, coef_north, area_inv, sea_mask, vert_coef, inv_thick,
):
    coefs = (coef_east, coef_north, area_inv, sea_mask)
    full, cells, fac_main, fac_strip, matrix, *sums = send_profiles(
        obs_count, vert_coef, inv_thick, obs_owner, obs_values, obs_cell, coefs
    )
    field = add_profiles(full, cells, forcing, matrix, sums)
    return spread(field, fac_main, fac_strip).reshape(LEV, NY, NX)


def solution(mesh):
    lead = P(("lon", "lat"))
    flat = P("lat", "lon")
    in_specs = (
        P(None, "lat", "lon"), P(None, ("lon", "lat")), lead, lead, lead,
        flat, flat, flat, flat, P(), P(),
    )
    return jax.shard_map(
        local, mesh=mesh, in_specs=in_specs, out_specs=P(None, "lat", "lon"), check_vma=False
    )
```

```python
import jax
import jax.numpy as jnp
from jax import lax
from jax.experimental import pallas as pl
from jax.experimental.pallas import tpu as pltpu
from jax.sharding import PartitionSpec as P

LEV = 75
LP = 80
NX = 128
NY = 64
DEV = 128
CAP = 64
SLOTS = 8192
ROWS = 40
HALO = 4
YE = NY + 2 * HALO
Q = 18
STRIDE = 27
F32 = jnp.float32
BF16 = jnp.bfloat16
HI = lax.Precision.HIGHEST
MESH = pl.DeviceIdType.MESH


def in_hbm(x):
    return pltpu.with_memory_space_constraint(x, pltpu.HBM)


def iota(shape, dim, dtype=jnp.int32):
    return lax.broadcasted_iota(dtype, shape, dim)


def vertical_fourth(vert_ref, thick_ref, out_ref, cp_ref, dp_ref):
    lane = iota((1, NX), 1)
    dp_ref[...] = jnp.zeros_like(dp_ref)

    def forward(i, carry):
        cp, dp = carry
        up = jnp.where(i < LEV - 1, vert_ref[jnp.minimum(i, LEV - 2)], 0.0)
        low = jnp.where(i > 0, vert_ref[jnp.maximum(i - 1, 0)], 0.0)
        middle = 1.0 + (low + up) * thick_ref[i]
        above = -thick_ref[jnp.minimum(i + 1, LEV - 1)] * up
        below = -thick_ref[jnp.maximum(i - 1, 0)] * low
        inv = 1.0 / (middle - below * cp)
        cp = above * inv
        dp = (jnp.where(lane == i, 1.0, 0.0) - below * dp) * inv
        cp_ref[pl.ds(i, 1), :] = cp
        dp_ref[pl.ds(i, 1), :] = dp
        return cp, dp

    zero = jnp.zeros((1, NX), F32)
    lax.fori_loop(0, LEV, forward, (zero, zero))

    def backward(j, x):
        i = LEV - 1 - j
        x = dp_ref[pl.ds(i, 1), :] - cp_ref[pl.ds(i, 1), :] * x
        dp_ref[pl.ds(i, 1), :] = x
        return x

    lax.fori_loop(0, LEV, backward, zero)
    single = dp_ref[...]
    double = jnp.dot(single, single, precision=HI, preferred_element_type=F32)
    out_ref[...] = jnp.dot(double, double, precision=HI, preferred_element_type=F32)


def places(count, own_ref, idx_ref):
    width = 256
    lane = iota((1, width), 1)
    owners = iota((DEV, width), 0)
    tri = (iota((width, width + NX), 0) <= iota((width, width + NX), 1)) | (
        iota((width, width + NX), 1) >= width
    )
    tri = tri.astype(F32).astype(BF16)
    kth = iota((CAP, width), 0).astype(F32)
    number = (iota((CAP, width), 1) + 1).astype(F32)
    acc_lane = iota((DEV, NX), 1)

    def step(b, carry):
        offset, acc = carry
        own = jnp.concatenate([own_ref[pl.ds(2 * b, 1), :], own_ref[pl.ds(2 * b + 1, 1), :]], 1)
        own = jnp.where(lane + b * width < count, own, -1)
        onehot = jnp.where(jnp.broadcast_to(own, (DEV, width)) == owners, 1.0, 0.0)
        ones = onehot.astype(BF16)
        prefix = jnp.dot(ones, tri, preferred_element_type=F32)
        rank = prefix[:, :width] + jnp.concatenate([offset, offset], 1)
        rank = jnp.sum(onehot * rank, axis=0, keepdims=True) - 1.0
        hit = jnp.where(jnp.broadcast_to(rank, (CAP, width)) == kth, 1.0, 0.0)
        both = jnp.concatenate([hit, hit * number], 0).astype(BF16)
        found = lax.dot_general(ones, both, (((1,), (1,)), ((), ())), preferred_element_type=F32)
        scale = jnp.where(acc_lane < CAP, (b * width).astype(F32), 1.0)
        return offset + prefix[:, width:], acc + found * scale

    zero = jnp.zeros((DEV, NX), F32)
    _, acc = lax.fori_loop(0, SLOTS // width, step, (zero, zero), unroll=16)
    total = (acc + pltpu.roll(acc, CAP, 1)).astype(jnp.int32)
    idx_ref[...] = jnp.clip(jnp.where(total > 0, total - 1, SLOTS + acc_lane % 8), 0, SLOTS + 7)


def factors(coef_refs, row_halo_ref, col_halo_ref, corner_ref, coef_main, coef_side, fac_main_ref, fac_strip_ref):
    lat = lax.axis_index("lat")
    lane64 = iota((NY, NX), 1)
    lane4 = iota((HALO, NX), 1)
    for i in range(4):
        coef_main[i, pl.ds(HALO, NY), :] = coef_refs[i][...].astype(F32)
        coef_main[i, pl.ds(0, HALO), :] = row_halo_ref[0, i, pl.ds(4, HALO), :]
        coef_main[i, pl.ds(NY + HALO, HALO), :] = row_halo_ref[1, i, pl.ds(0, HALO), :]

        def sides(lanes, left, right, i=i):
            return jnp.where(
                lanes < 64,
                pltpu.roll(right, (-8 * i) % NX, 1),
                pltpu.roll(left, (124 - 8 * i - 4) % NX, 1),
            )

        coef_side[i, pl.ds(HALO, NY), :] = sides(lane64, col_halo_ref[0], col_halo_ref[1])
        coef_side[i, pl.ds(0, HALO), :] = sides(
            lane4, corner_ref[0, pl.ds(4, HALO), :], corner_ref[1, pl.ds(4, HALO), :]
        )
        coef_side[i, pl.ds(NY + HALO, HALO), :] = sides(
            lane4, corner_ref[2, pl.ds(0, HALO), :], corner_ref[3, pl.ds(0, HALO), :]
        )
    row = iota((YE, NX), 0)
    first_row = jnp.where(lat == 0, HALO, 0)
    last_row = jnp.where(lat == 3, NY + HALO, YE)
    inside = (row >= first_row) & (row < last_row)
    lanes = iota((YE, NX), 1)

    def shifts(main, side):
        first, last = lanes == 0, lanes == NX - 1
        main_e = pltpu.roll(jnp.where(first, side, main), NX - 1, 1)
        side_e = pltpu.roll(jnp.where(first, main, side), NX - 1, 1)
        main_w = pltpu.roll(jnp.where(last, side, main), 1, 1)
        side_w = pltpu.roll(jnp.where(last, main, side), 1, 1)
        return main_e, side_e, main_w, side_w

    sea_m = jnp.where(inside, coef_main[3], 0.0)
    sea_s = jnp.where(inside, coef_side[3], 0.0)
    area_m, area_s = coef_main[2], coef_side[2]
    sea_me, sea_se, _, _ = shifts(sea_m, sea_s)
    east_m = coef_main[0] * sea_m * sea_me
    east_s = coef_side[0] * sea_s * sea_se
    _, _, west_m, west_s = shifts(east_m, east_s)
    area_me, area_se, area_mw, area_sw = shifts(area_m, area_s)

    def five(north_coef, ee, ww, sea, area, area_e, area_w):
        nn = north_coef * sea * pltpu.roll(sea, YE - 1, 0)
        ss = pltpu.roll(nn, 1, 0)
        return (
            1.0 - area * (ee + ww + nn + ss),
            ee * area_e,
            ww * area_w,
            nn * pltpu.roll(area, YE - 1, 0),
            ss * pltpu.roll(area, 1, 0),
        )

    mains = five(coef_main[1], east_m, west_m, sea_m, area_m, area_me, area_mw)
    sides = five(coef_side[1], east_s, west_s, sea_s, area_s, area_se, area_sw)
    laneq = iota((Q, NX), 1)
    group, place = laneq // 32, laneq % 32
    gap = ((place >= 12) & (place < 16)) | (place >= 28)
    for i in range(5):
        fac_main_ref[i] = mains[i]
        coef_main[0] = jnp.where(lanes < 64, sides[i], mains[i])
        coef_main[1] = jnp.where(lanes < 64, mains[i], sides[i])
        strip = jnp.zeros((Q, NX), F32)
        for j in range(4):
            own = pl.ds(Q * j, Q)
            near = pltpu.roll(coef_main[0, own, :], (32 * j + 8) % NX, 1)
            far = pltpu.roll(coef_main[1, own, :], (32 * j + 20) % NX, 1)
            strip = jnp.where(group == j, jnp.where(place < 14, near, far), strip)
        fac_strip_ref[i, pl.ds(0, Q), :] = jnp.where(gap, 0.0, strip)


def clear(refs):
    def some(i, _):
        at = pl.ds(pl.multiple_of(i * 64, 64), 64)
        for ref in refs:
            ref[at, :] = jnp.zeros((64, NX), F32)
        return 0

    lax.fori_loop(0, SLOTS // 64, some, 0, unroll=2)


def send_body(
    count_ref, vert_hbm, thick_hbm, own_hbm, obs_hbm, cell_hbm, east_hbm, north_hbm, area_hbm, sea_hbm,
    full_ref, cells_ref, fac_main_ref, fac_strip_ref, matrix_ref, sum0, sum1, sum2, sum3,
    vert_ref, thick_ref, own_ref, obs_ref, cell_ref, east_ref, north_ref, area_ref, sea_ref,
    recv, load_sem, table, rows, outbox, coef_box, colbox, row_halo, col_halo, corner, coef_main, coef_side,
    cp_ref, dp_ref, idx_v, idx_ref, idx_sem, send_sem, recv_sem, side_send, side_recv,
):
    lon = lax.axis_index("lon")
    lat = lax.axis_index("lat")
    z, y, c = lax.div(lon, 8), lax.rem(lax.div(lon, 2), 4), lax.rem(lon, 2)
    me = lon * 4 + lat

    def target(k):
        q = lax.rem(k * STRIDE, DEV)
        dx, dc = lax.rem(q, 4), lax.rem(lax.div(q, 4), 2)
        dy, dz = lax.rem(lax.div(q, 8), 4), lax.div(q, 32)
        there = (lax.rem(z + dz, 4) * 4 + lax.rem(y + dy, 4)) * 2 + lax.rem(c + dc, 2)
        return there, lax.rem(lat + dx, 4)

    loads = []
    for number, (src, dst) in enumerate((
        (own_hbm, own_ref), (obs_hbm, obs_ref), (cell_hbm, cell_ref), (east_hbm, east_ref),
        (north_hbm, north_ref), (area_hbm, area_ref), (sea_hbm, sea_ref),
        (vert_hbm, vert_ref), (thick_hbm, thick_ref),
    )):
        load = pltpu.make_async_copy(src, dst, load_sem.at[number])
        load.start()
        loads.append(load)

    barrier = pltpu.get_barrier_semaphore()

    deep = [lax.rem(z + d, 4) * 8 for d in range(4)]
    wide = [lax.rem(y + d, 4) * 2 for d in range(4)]
    core = [lax.rem(c + d, 2) for d in range(2)]
    flat = [lax.rem(lat + d, 4) for d in range(4)]
    for a in range(4):
        for b in range(4):
            for d in range(2):
                there = deep[a] + wide[b] + core[d]
                for e in range(4):
                    if a + b + d + e:
                        pl.semaphore_signal(
                            barrier, inc=1, device_id=(there, flat[e]), device_id_type=MESH
                        )

    loads[0].wait()
    places(count_ref[0], own_ref, idx_v)
    idx_copy = pltpu.make_async_copy(idx_v, idx_ref, idx_sem)
    idx_copy.start()
    for load in loads[1:]:
        load.wait()

    def turn(b, _):
        columns = pl.ds(pl.multiple_of(b * NX, NX), NX)
        block = jnp.concatenate(
            [
                obs_ref[:, columns],
                cell_ref[pl.ds(b, 1), :].astype(F32),
                jnp.zeros((NX - LEV - 1, NX), F32),
            ],
            0,
        )
        table[columns, :] = block.T
        return 0

    lax.fori_loop(0, SLOTS // NX, turn, 0, unroll=4)
    spare = (iota((8, NX), 0) * 1024).astype(F32)
    table[pl.ds(SLOTS, 8), :] = jnp.where(iota((8, NX), 1) == LEV, spare, 0.0)

    lane = iota((NY, NX), 1)
    cols = jnp.zeros((NY, NX), F32)
    coef_refs = (east_ref, north_ref, area_ref, sea_ref)
    for i in range(4):
        whole = coef_refs[i][...].astype(F32)
        coef_box[i, pl.ds(0, 8), :] = whole[:8]
        coef_box[i, pl.ds(8, 8), :] = whole[NY - 8:]
        cols = jnp.where((lane >= 8 * i) & (lane < 8 * i + 4), pltpu.roll(whole, 8 * i, 1), cols)
        cols = jnp.where(
            (lane >= 8 * i + 4) & (lane < 8 * i + 8),
            pltpu.roll(whole, (8 * i + 4 - 124) % NX, 1),
            cols,
        )
    colbox[...] = cols
    idx_copy.wait()
    pl.semaphore_wait(barrier, DEV - 1)

    east, west = lax.rem(lon + 1, 32), lax.rem(lon + 31, 32)
    north, south = lax.rem(lat + 1, 4), lax.rem(lat + 3, 4)
    side = []

    def beside(number, src, dst, where):
        copy = pltpu.make_async_remote_copy(
            src_ref=src, dst_ref=dst, send_sem=side_send.at[number], recv_sem=side_recv.at[number],
            device_id=where, device_id_type=MESH,
        )
        copy.start()
        side.append(copy)

    beside(0, coef_box.at[:, pl.ds(8, 8), :], row_halo.at[0], (lon, north))
    beside(1, coef_box.at[:, pl.ds(0, 8), :], row_halo.at[1], (lon, south))
    beside(2, colbox, col_halo.at[0], (east, lat))
    beside(3, colbox, col_halo.at[1], (west, lat))
    beside(4, colbox.at[pl.ds(NY - 8, 8), :], corner.at[0], (east, north))
    beside(5, colbox.at[pl.ds(NY - 8, 8), :], corner.at[1], (west, north))
    beside(6, colbox.at[pl.ds(0, 8), :], corner.at[2], (east, south))
    beside(7, colbox.at[pl.ds(0, 8), :], corner.at[3], (west, south))

    lane8 = iota((8, NX), 1)
    lane32 = iota((32, NX), 1)

    def gather(owner):
        for k in range(CAP):
            at = jnp.minimum(jnp.maximum(idx_ref[owner, k], 0), SLOTS + 7)
            rows[pl.ds(k, 1), :] = table[pl.ds(at, 1), :]

    def fold(box):
        box[pl.ds(0, 32), :] = jnp.where(
            lane32 < 64, rows[pl.ds(0, 32), :], pltpu.roll(rows[pl.ds(32, 32), :], 64, 1)
        )
        rest = jnp.zeros((8, NX), F32)
        for g in range(8):
            piece = rows[pl.ds(8 * g, 8), :]
            shift = (16 * g - 64) % NX
            piece = pltpu.roll(piece, shift, 1) if shift else piece
            rest = jnp.where(lane8 // 16 == g, piece, rest)
        box[pl.ds(32, 8), :] = rest

    def send(k, _):
        dlon, dlat = target(k)
        owner = dlon * 4 + dlat
        gather(owner)
        fold(outbox.at[owner])
        pltpu.make_async_remote_copy(
            src_ref=outbox.at[owner], dst_ref=recv.at[k], send_sem=send_sem, recv_sem=recv_sem.at[k],
            device_id=(dlon, dlat), device_id_type=MESH,
        ).start()
        return 0

    lax.fori_loop(1, DEV, send, 0)
    gather(me)
    fold(recv.at[0])
    vertical_fourth(vert_ref, thick_ref, matrix_ref, cp_ref, dp_ref)
    for copy in side:
        copy.wait()
    factors(coef_refs, row_halo, col_halo, corner, coef_main, coef_side, fac_main_ref, fac_strip_ref)
    clear((sum0, sum1, sum2, sum3))

    pick = jnp.where(
        iota((8, NX), 1) == 16 * iota((8, NX), 0) + (LEV - 64), 1.0, 0.0
    ).astype(F32)

    def unfold(k):
        rest = recv[k, pl.ds(32, 8), :]
        for g in range(8):
            tail = pltpu.roll(rest, (64 - 16 * g) % NX, 1) if g != 4 else rest
            head = recv[k, pl.ds(8 * (g % 4), 8), :]
            head = pltpu.roll(head, 64, 1) if g >= 4 else head
            full_ref[pl.ds(k * CAP + 8 * g, 8), :] = jnp.where(lane8 < 64, head, tail)

    def arrive(k, _):
        pltpu.make_async_copy(recv.at[k], recv.at[k], recv_sem.at[k]).wait()
        return 0

    def spread_out(k, _):
        unfold(k)
        return 0

    for b in range(8):
        lax.fori_loop(max(16 * b, 1), 16 * b + 16, arrive, 0)
        lax.fori_loop(16 * b, 16 * b + 16, spread_out, 0, unroll=4)
        part = recv[pl.ds(16 * b, 16), pl.ds(32, 8), :].reshape(NX, NX)
        found = lax.dot_general(
            pick, part, (((1,), (1,)), ((), ())), precision=HI, preferred_element_type=F32
        )
        cells_ref[pl.ds(8 * b, 8), :] = (found + 0.5).astype(jnp.int32)
    others = pl.ds(0, DEV - 1)
    pltpu.make_async_copy(outbox.at[others], outbox.at[others], send_sem).wait()


def send_profiles(count, vert_coef, inv_thick, owner, obs, cell, coefs):
    vm = pl.BlockSpec(memory_space=pltpu.VMEM)
    sm = pl.BlockSpec(memory_space=pltpu.SMEM)
    plane = pltpu.VMEM((4, YE, NX), F32)
    return pl.pallas_call(
        send_body,
        out_shape=(
            jax.ShapeDtypeStruct((SLOTS, NX), F32),
            jax.ShapeDtypeStruct((SLOTS // NX, NX), jnp.int32),
            jax.ShapeDtypeStruct((5, YE, NX), F32),
            jax.ShapeDtypeStruct((5, 24, NX), F32),
            jax.ShapeDtypeStruct((NX, NX), F32),
        ) + (jax.ShapeDtypeStruct((SLOTS, NX), F32),) * EARLY,
        in_specs=[sm] + [pl.BlockSpec(memory_space=pltpu.HBM)] * 9,
        out_specs=(vm,) * (5 + EARLY),
        scratch_shapes=[
            pltpu.SMEM((LEV - 1,), F32),
            pltpu.SMEM((LEV,), F32),
            pltpu.VMEM((SLOTS // NX, NX), jnp.int32),
            pltpu.VMEM((LEV, SLOTS), F32),
            pltpu.VMEM((SLOTS // NX, NX), jnp.int32),
            pltpu.VMEM((NY, NX), F32),
            pltpu.VMEM((NY, NX), F32),
            pltpu.VMEM((NY, NX), F32),
            pltpu.VMEM((NY, NX), jnp.int32),
            pltpu.VMEM((DEV, ROWS, NX), F32),
            pltpu.SemaphoreType.DMA((9,)),
            pltpu.VMEM((SLOTS + 8, NX), F32),
            pltpu.VMEM((CAP, NX), F32),
            pltpu.VMEM((DEV, ROWS, NX), F32),
            pltpu.VMEM((4, 16, NX), F32),
            pltpu.VMEM((NY, NX), F32),
            pltpu.VMEM((2, 4, 8, NX), F32),
            pltpu.VMEM((2, NY, NX), F32),
            pltpu.VMEM((4, 8, NX), F32),
            plane,
            plane,
            pltpu.VMEM((NX, NX), F32),
            pltpu.VMEM((NX, NX), F32),
            pltpu.VMEM((DEV, NX), jnp.int32),
            pltpu.SMEM((DEV, NX), jnp.int32),
            pltpu.SemaphoreType.DMA(()),
            pltpu.SemaphoreType.DMA(()),
            pltpu.SemaphoreType.DMA((DEV,)),
            pltpu.SemaphoreType.DMA((8,)),
            pltpu.SemaphoreType.DMA((8,)),
        ],
        compiler_params=pltpu.CompilerParams(
            collective_id=0, has_side_effects=True, vmem_limit_bytes=18 << 20
        ),
        name="send_profiles",
    )(count, *map(in_hbm, (
        vert_coef, inv_thick, owner.reshape(SLOTS // NX, NX), obs,
        cell.reshape(SLOTS // NX, NX), *coefs,
    )))


WAYS = 8
EARLY = 4


def add_body(
    full, cell_v, forcing_ref, matrix_ref, in0, in1, in2, in3, out_ref,
    acc0, acc1, acc2, acc3, acc4, acc5, acc6, acc7, cell_s, sem,
):
    accs = (acc0, acc1, acc2, acc3, acc4, acc5, acc6, acc7)
    copy = pltpu.make_async_copy(cell_v, cell_s, sem)
    copy.start()

    clear(accs[EARLY:])
    copy.wait()
    per = DEV // WAYS

    def add(s, _):
        starts = [pl.multiple_of((s + w * per) * CAP, CAP) for w in range(WAYS)]
        firsts = [(s + w * per) // 16 * 1024 + (s + w * per) % 16 * 8 for w in range(WAYS)]
        blocks = [full.at[pl.ds(start, CAP), :] for start in starts]
        for g in range(8):
            for e in range(8):
                places_of = [pl.ds(cell_s[first + (128 * g + e)], 1) for first in firsts]
                sums = [
                    acc[at, :] + block[pl.ds(8 * g + e, 1), :]
                    for acc, at, block in zip(accs, places_of, blocks)
                ]
                for acc, at, total in zip(accs, places_of, sums):
                    acc[at, :] = total
        return 0

    lax.fori_loop(0, per, add, 0)
    whole = matrix_ref[pl.ds(0, LP), pl.ds(0, LP)]
    high = whole.astype(BF16)
    low = (whole - high.astype(F32)).astype(BF16)
    matrix = jnp.concatenate([high, high, low], 1)
    padding = jnp.zeros((LP - LEV, NX), F32)

    def finish(b, _):
        loaded = []
        for h in range(2):
            y = 2 * b + h
            at = pl.ds(pl.multiple_of(y * NX, NX), NX)
            parts = [acc[at, :] for acc in accs]
            while len(parts) > 1:
                parts = [p + q for p, q in zip(parts[::2], parts[1::2])]
            total = parts[0]
            column = total.T[:LEV] + forcing_ref[pl.ds(y, LEV, stride=NY), :]
            loaded.append(jnp.concatenate([column, padding], 0))
        values = jnp.concatenate(loaded, 1)
        top = values.astype(BF16)
        rest = (values - top.astype(F32)).astype(BF16)
        parts = jnp.concatenate([top, rest, top], 0)
        product = jnp.dot(matrix, parts, preferred_element_type=F32)
        out_ref[2 * b] = product[:, :NX]
        out_ref[2 * b + 1] = product[:, NX:]
        return 0

    lax.fori_loop(0, NY // 2, finish, 0, unroll=8)


def add_profiles(full, cells, forcing, matrix, sums):
    vm = pl.BlockSpec(memory_space=pltpu.VMEM)
    return pl.pallas_call(
        add_body,
        out_shape=(jax.ShapeDtypeStruct((NY, LP, NX), F32),)
        + (jax.ShapeDtypeStruct((SLOTS, NX), F32),) * EARLY,
        in_specs=[vm] * (4 + EARLY),
        out_specs=(vm,) * (1 + EARLY),
        input_output_aliases={4 + w: 1 + w for w in range(EARLY)},
        scratch_shapes=[pltpu.VMEM((SLOTS, NX), F32)] * (WAYS - EARLY)
        + [
            pltpu.SMEM((SLOTS,), jnp.int32),
            pltpu.SemaphoreType.DMA(()),
        ],
        compiler_params=pltpu.CompilerParams(vmem_limit_bytes=22 << 20),
        name="add_profiles",
    )(full, cells.reshape(SLOTS), forcing.reshape(LEV * NY, NX), matrix, *sums)[0]


def spread_body(
    field_ref, fac_ref, strip_ref,
    out_ref,
    wide_a, wide_b, tips, strip_a, strip_b, east_box, west_box, from_west, from_east, corner_box, corners,
    own_sem, send_sem, recv_sem,
):
    lon = lax.axis_index("lon")
    lat = lax.axis_index("lat")
    east, west = lax.rem(lon + 1, 32), lax.rem(lon + 31, 32)
    north, south = lax.rem(lat + 1, 4), lax.rem(lat + 3, 4)
    peers = [
        (lon, north), (lon, south), (east, lat), (west, lat),
        (east, north), (west, north), (east, south), (west, south),
    ]
    barrier = pltpu.get_barrier_semaphore()
    for peer in peers:
        pl.semaphore_signal(barrier, inc=1, device_id=peer, device_id_type=MESH)
    own = pltpu.make_async_copy(field_ref, wide_a.at[pl.ds(HALO, NY)], own_sem)
    own.start()
    own.wait()

    lane = iota((LP, NX), 1)
    group, place = lane // 32, lane % 32

    def tip(low, high, parts):
        def one(q, _):
            total = jnp.zeros((LP, NX), F32)
            for j in parts:
                piece = pltpu.roll(wide_a[q + Q * j], (32 * j + 8) % NX, 1)
                total = jnp.where((group == j) & (place < 16), piece, total)
            tips[q] = total
            return 0

        lax.fori_loop(low, high, one, 0, unroll=2)

    tip(0, HALO, (1, 2, 3))
    tip(HALO, Q - HALO, (0, 1, 2, 3))
    tip(Q - HALO, Q, (0, 1, 2))
    for b in range(3):
        e = jnp.zeros((LP, NX), F32)
        w = jnp.zeros((LP, NX), F32)
        for q in range(8 * b, min(8 * b + 8, Q)):
            here = place // 4 == q % 8
            row = tips[q]
            e = jnp.where(here, pltpu.roll(row, (4 * (q % 8) - 4) % NX, 1), e)
            w = jnp.where(here, pltpu.roll(row, (4 * (q % 8) - 8) % NX, 1), w)
        east_box[b] = e
        west_box[b] = w

    lane16 = iota((16, NX), 1)
    for number, (box, start) in enumerate(
        ((east_box.at[1], 104), (west_box.at[1], 104), (east_box.at[0], 16), (west_box.at[0], 16))
    ):
        total = jnp.zeros((16, NX), F32)
        for h in range(LP // 16):
            piece = pltpu.roll(box[pl.ds(16 * h, 16), :], (16 * h - start) % NX, 1)
            total = jnp.where(lane16 // 16 == h, piece, total)
        corner_box[number] = total

    pl.semaphore_wait(barrier, 8)
    moves = [
        (field_ref.at[pl.ds(NY - HALO, HALO)], wide_a.at[pl.ds(0, HALO)]),
        (field_ref.at[pl.ds(0, HALO)], wide_a.at[pl.ds(NY + HALO, HALO)]),
        (east_box, from_west),
        (west_box, from_east),
        (corner_box.at[0], corners.at[0]),
        (corner_box.at[1], corners.at[1]),
        (corner_box.at[2], corners.at[2]),
        (corner_box.at[3], corners.at[3]),
    ]
    copies = []
    for number, (src, dst) in enumerate(moves):
        copy = pltpu.make_async_remote_copy(
            src_ref=src, dst_ref=dst, send_sem=send_sem.at[number], recv_sem=recv_sem.at[number],
            device_id=peers[number], device_id_type=MESH,
        )
        copy.start()
        copies.append(copy)

    def stencil(facs, y, src, at):
        centre = src[at]

        def fac(i):
            return jnp.broadcast_to(facs[i, pl.ds(y, 1), :], (LP, NX))

        return (
            fac(0) * centre
            + fac(1) * pltpu.roll(centre, NX - 1, 1)
            + fac(2) * pltpu.roll(centre, 1, 1)
            + fac(3) * src[at + 1]
            + fac(4) * src[at - 1]
        )

    def rows(t, low, high, unroll):
        src, dst = (wide_a, wide_b) if t % 2 else (wide_b, wide_a)

        def row(y, _):
            dst[y] = stencil(fac_ref, y, src, y)
            return 0

        lax.fori_loop(low, high, row, 0, unroll=unroll)

    for t in range(1, 5):
        rows(t, HALO + t, NY + HALO - t, 8)

    for copy in copies:
        copy.wait()

    for near, from_side in ((0, from_west), (1, from_east)):
        below, above = corners[near], corners[near + 2]
        for h in range(LP // 16):
            at = pl.ds(16 * h, 16)

            def put(box, keep, corner, shift, at=at, from_side=from_side):
                box_rows = from_side[box, at, :]
                piece = pltpu.roll(corner, shift % NX, 1) if shift % NX else corner
                from_side[box, at, :] = jnp.where(keep, piece, box_rows)

            put(0, lane16 < 16, below, -16 * h)
            put(1, lane16 >= 120, above, 120 - 16 * h)
            put(2, (lane16 >= 96) & (lane16 < 104), above, 88 - 16 * h)
    for h in range(HALO):
        q = Q - HALO + h
        tips[h] = jnp.where((group == 0) & (place < 16), pltpu.roll(wide_a[h], 8, 1), tips[h])
        tips[q] = jnp.where((group == 3) & (place < 16), pltpu.roll(wide_a[q + 3 * Q], 104, 1), tips[q])
    for q in range(Q):
        row = tips[q]
        right = pltpu.roll(from_east[q // 8], (8 - 4 * (q % 8)) % NX, 1)
        left = pltpu.roll(from_west[q // 8], (16 - 4 * (q % 8)) % NX, 1)
        far = jnp.where((place >= 16) & (place < 20), left, pltpu.roll(row, 12, 1))
        strip_a[q + 1] = jnp.where(place < 8, row, jnp.where(place < 12, right, far))

    for t in range(1, 5):
        rows(t, t, HALO + t, 4)
        rows(t, NY + HALO - t, NY + 2 * HALO - t, 4)
    for t in range(4):
        src, dst = (strip_a, strip_b) if t % 2 == 0 else (strip_b, strip_a)
        src[0] = pltpu.roll(src[Q], 32, 1)
        src[Q + 1] = pltpu.roll(src[1], NX - 32, 1)

        def strip(q, _):
            dst[q + 1] = stencil(strip_ref, q, src, q + 1)
            return 0

        lax.fori_loop(0, Q, strip, 0, unroll=6)

    edge = (lane < HALO) | (lane >= NX - HALO)

    def write(low, high, parts):
        def one(q, _):
            row = strip_a[q + 1]
            row = jnp.where(place < 8, row, pltpu.roll(row, NX - 12, 1))
            for j in parts:
                y = q + Q * j
                whole = jnp.where(edge, pltpu.roll(row, (120 - 32 * j) % NX, 1), wide_a[y])
                out_ref[pl.ds(y - HALO, LEV, stride=NY), :] = whole[:LEV]
            return 0

        lax.fori_loop(low, high, one, 0, unroll=2)

    write(0, HALO, (1, 2, 3))
    write(HALO, Q - HALO, (0, 1, 2, 3))
    write(Q - HALO, Q, (0, 1, 2))


def spread(field, fac_main, fac_strip):
    vm = pl.BlockSpec(memory_space=pltpu.VMEM)
    wide = pltpu.VMEM((YE, LP, NX), F32)
    strip = pltpu.VMEM((Q + 2, LP, NX), F32)
    box = pltpu.VMEM((3, LP, NX), F32)
    return pl.pallas_call(
        spread_body,
        out_shape=jax.ShapeDtypeStruct((LEV * NY, NX), F32),
        in_specs=[pl.BlockSpec(memory_space=pl.ANY), vm, vm],
        out_specs=vm,
        scratch_shapes=[
            wide, wide, pltpu.VMEM((Q, LP, NX), F32), strip, strip, box, box, box, box,
            pltpu.VMEM((4, 16, NX), F32),
            pltpu.VMEM((4, 16, NX), F32),
            pltpu.SemaphoreType.DMA(()),
            pltpu.SemaphoreType.DMA((8,)),
            pltpu.SemaphoreType.DMA((8,)),
        ],
        compiler_params=pltpu.CompilerParams(
            collective_id=1, has_side_effects=True, vmem_limit_bytes=24 << 20
        ),
        name="spread",
    )(field, fac_main, fac_strip)


def local(
    forcing, obs_values, obs_owner, obs_cell, obs_count,
    coef_east, coef_north, area_inv, sea_mask, vert_coef, inv_thick,
):
    coefs = (coef_east, coef_north, area_inv, sea_mask)
    full, cells, fac_main, fac_strip, matrix, *sums = send_profiles(
        obs_count, vert_coef, inv_thick, obs_owner, obs_values, obs_cell, coefs
    )
    field = add_profiles(full, cells, forcing, matrix, sums)
    return spread(field, fac_main, fac_strip).reshape(LEV, NY, NX)


def solution(mesh):
    lead = P(("lon", "lat"))
    flat = P("lat", "lon")
    in_specs = (
        P(None, "lat", "lon"), P(None, ("lon", "lat")), lead, lead, lead,
        flat, flat, flat, flat, P(), P(),
    )
    return jax.shard_map(
        local, mesh=mesh, in_specs=in_specs, out_specs=P(None, "lat", "lon"), check_vma=False
    )
```

```python
import jax
import jax.numpy as jnp
from jax import lax
from jax.experimental import pallas as pl
from jax.experimental.pallas import tpu as pltpu
from jax.sharding import PartitionSpec as P

LEV = 75
LP = 80
NX = 128
NY = 64
DEV = 128
CAP = 64
SLOTS = 8192
ROWS = 40
HALO = 4
YE = NY + 2 * HALO
Q = 18
STRIDE = 59
F32 = jnp.float32
BF16 = jnp.bfloat16
HI = lax.Precision.HIGHEST
MESH = pl.DeviceIdType.MESH


def in_hbm(x):
    return pltpu.with_memory_space_constraint(x, pltpu.HBM)


def iota(shape, dim, dtype=jnp.int32):
    return lax.broadcasted_iota(dtype, shape, dim)


def vertical_fourth(vert_ref, thick_ref, out_ref, cp_ref, dp_ref):
    lane = iota((1, NX), 1)
    dp_ref[...] = jnp.zeros_like(dp_ref)

    def forward(i, carry):
        cp, dp = carry
        up = jnp.where(i < LEV - 1, vert_ref[jnp.minimum(i, LEV - 2)], 0.0)
        low = jnp.where(i > 0, vert_ref[jnp.maximum(i - 1, 0)], 0.0)
        middle = 1.0 + (low + up) * thick_ref[i]
        above = -thick_ref[jnp.minimum(i + 1, LEV - 1)] * up
        below = -thick_ref[jnp.maximum(i - 1, 0)] * low
        inv = 1.0 / (middle - below * cp)
        cp = above * inv
        dp = (jnp.where(lane == i, 1.0, 0.0) - below * dp) * inv
        cp_ref[pl.ds(i, 1), :] = cp
        dp_ref[pl.ds(i, 1), :] = dp
        return cp, dp

    zero = jnp.zeros((1, NX), F32)
    lax.fori_loop(0, LEV, forward, (zero, zero))

    def backward(j, x):
        i = LEV - 1 - j
        x = dp_ref[pl.ds(i, 1), :] - cp_ref[pl.ds(i, 1), :] * x
        dp_ref[pl.ds(i, 1), :] = x
        return x

    lax.fori_loop(0, LEV, backward, zero)
    single = dp_ref[...]
    double = jnp.dot(single, single, precision=HI, preferred_element_type=F32)
    out_ref[...] = jnp.dot(double, double, precision=HI, preferred_element_type=F32)


def places(count, own_ref, idx_ref):
    width = 256
    lane = iota((1, width), 1)
    owners = iota((DEV, width), 0)
    tri = (iota((width, width + NX), 0) <= iota((width, width + NX), 1)) | (
        iota((width, width + NX), 1) >= width
    )
    tri = tri.astype(F32).astype(BF16)
    kth = iota((CAP, width), 0).astype(F32)
    number = (iota((CAP, width), 1) + 1).astype(F32)
    acc_lane = iota((DEV, NX), 1)

    def step(b, carry):
        offset, acc = carry
        own = jnp.concatenate([own_ref[pl.ds(2 * b, 1), :], own_ref[pl.ds(2 * b + 1, 1), :]], 1)
        own = jnp.where(lane + b * width < count, own, -1)
        onehot = jnp.where(jnp.broadcast_to(own, (DEV, width)) == owners, 1.0, 0.0)
        ones = onehot.astype(BF16)
        prefix = jnp.dot(ones, tri, preferred_element_type=F32)
        rank = prefix[:, :width] + jnp.concatenate([offset, offset], 1)
        rank = jnp.sum(onehot * rank, axis=0, keepdims=True) - 1.0
        hit = jnp.where(jnp.broadcast_to(rank, (CAP, width)) == kth, 1.0, 0.0)
        both = jnp.concatenate([hit, hit * number], 0).astype(BF16)
        found = lax.dot_general(ones, both, (((1,), (1,)), ((), ())), preferred_element_type=F32)
        scale = jnp.where(acc_lane < CAP, (b * width).astype(F32), 1.0)
        return offset + prefix[:, width:], acc + found * scale

    zero = jnp.zeros((DEV, NX), F32)
    _, acc = lax.fori_loop(0, SLOTS // width, step, (zero, zero), unroll=16)
    total = (acc + pltpu.roll(acc, CAP, 1)).astype(jnp.int32)
    idx_ref[...] = jnp.clip(jnp.where(total > 0, total - 1, SLOTS + acc_lane % 8), 0, SLOTS + 7)


def factors(coef_refs, row_halo_ref, col_halo_ref, corner_ref, coef_main, coef_side, fac_main_ref, fac_strip_ref):
    lat = lax.axis_index("lat")
    lane64 = iota((NY, NX), 1)
    lane4 = iota((HALO, NX), 1)
    for i in range(4):
        coef_main[i, pl.ds(HALO, NY), :] = coef_refs[i][...].astype(F32)
        coef_main[i, pl.ds(0, HALO), :] = row_halo_ref[0, i, pl.ds(4, HALO), :]
        coef_main[i, pl.ds(NY + HALO, HALO), :] = row_halo_ref[1, i, pl.ds(0, HALO), :]

        def sides(lanes, left, right, i=i):
            return jnp.where(
                lanes < 64,
                pltpu.roll(right, (-8 * i) % NX, 1),
                pltpu.roll(left, (124 - 8 * i - 4) % NX, 1),
            )

        coef_side[i, pl.ds(HALO, NY), :] = sides(lane64, col_halo_ref[0], col_halo_ref[1])
        coef_side[i, pl.ds(0, HALO), :] = sides(
            lane4, corner_ref[0, pl.ds(4, HALO), :], corner_ref[1, pl.ds(4, HALO), :]
        )
        coef_side[i, pl.ds(NY + HALO, HALO), :] = sides(
            lane4, corner_ref[2, pl.ds(0, HALO), :], corner_ref[3, pl.ds(0, HALO), :]
        )
    row = iota((YE, NX), 0)
    first_row = jnp.where(lat == 0, HALO, 0)
    last_row = jnp.where(lat == 3, NY + HALO, YE)
    inside = (row >= first_row) & (row < last_row)
    lanes = iota((YE, NX), 1)

    def shifts(main, side):
        first, last = lanes == 0, lanes == NX - 1
        main_e = pltpu.roll(jnp.where(first, side, main), NX - 1, 1)
        side_e = pltpu.roll(jnp.where(first, main, side), NX - 1, 1)
        main_w = pltpu.roll(jnp.where(last, side, main), 1, 1)
        side_w = pltpu.roll(jnp.where(last, main, side), 1, 1)
        return main_e, side_e, main_w, side_w

    sea_m = jnp.where(inside, coef_main[3], 0.0)
    sea_s = jnp.where(inside, coef_side[3], 0.0)
    area_m, area_s = coef_main[2], coef_side[2]
    sea_me, sea_se, _, _ = shifts(sea_m, sea_s)
    east_m = coef_main[0] * sea_m * sea_me
    east_s = coef_side[0] * sea_s * sea_se
    _, _, west_m, west_s = shifts(east_m, east_s)
    area_me, area_se, area_mw, area_sw = shifts(area_m, area_s)

    def five(north_coef, ee, ww, sea, area, area_e, area_w):
        nn = north_coef * sea * pltpu.roll(sea, YE - 1, 0)
        ss = pltpu.roll(nn, 1, 0)
        return (
            1.0 - area * (ee + ww + nn + ss),
            ee * area_e,
            ww * area_w,
            nn * pltpu.roll(area, YE - 1, 0),
            ss * pltpu.roll(area, 1, 0),
        )

    mains = five(coef_main[1], east_m, west_m, sea_m, area_m, area_me, area_mw)
    sides = five(coef_side[1], east_s, west_s, sea_s, area_s, area_se, area_sw)
    laneq = iota((Q, NX), 1)
    group, place = laneq // 32, laneq % 32
    gap = ((place >= 12) & (place < 16)) | (place >= 28)
    for i in range(5):
        fac_main_ref[i] = mains[i]
        coef_main[0] = jnp.where(lanes < 64, sides[i], mains[i])
        coef_main[1] = jnp.where(lanes < 64, mains[i], sides[i])
        strip = jnp.zeros((Q, NX), F32)
        for j in range(4):
            own = pl.ds(Q * j, Q)
            near = pltpu.roll(coef_main[0, own, :], (32 * j + 8) % NX, 1)
            far = pltpu.roll(coef_main[1, own, :], (32 * j + 20) % NX, 1)
            strip = jnp.where(group == j, jnp.where(place < 14, near, far), strip)
        fac_strip_ref[i, pl.ds(0, Q), :] = jnp.where(gap, 0.0, strip)


def clear(refs):
    def some(i, _):
        at = pl.ds(pl.multiple_of(i * 64, 64), 64)
        for ref in refs:
            ref[at, :] = jnp.zeros((64, NX), F32)
        return 0

    lax.fori_loop(0, SLOTS // 64, some, 0, unroll=2)


def send_body(
    count_ref, vert_hbm, thick_hbm, own_hbm, obs_hbm, cell_hbm, east_hbm, north_hbm, area_hbm, sea_hbm,
    full_ref, cells_ref, fac_main_ref, fac_strip_ref, matrix_ref, sum0, sum1, sum2, sum3,
    vert_ref, thick_ref, own_ref, obs_ref, cell_ref, east_ref, north_ref, area_ref, sea_ref,
    recv, load_sem, table, rows, outbox, coef_box, colbox, row_halo, col_halo, corner, coef_main, coef_side,
    cp_ref, dp_ref, idx_v, idx_ref, idx_sem, send_sem, recv_sem, side_send, side_recv,
):
    lon = lax.axis_index("lon")
    lat = lax.axis_index("lat")
    z, y, c = lax.div(lon, 8), lax.rem(lax.div(lon, 2), 4), lax.rem(lon, 2)
    me = lon * 4 + lat

    def target(k):
        q = lax.rem(k * STRIDE, DEV)
        dx, dc = lax.rem(q, 4), lax.rem(lax.div(q, 4), 2)
        dy, dz = lax.rem(lax.div(q, 8), 4), lax.div(q, 32)
        there = (lax.rem(z + dz, 4) * 4 + lax.rem(y + dy, 4)) * 2 + lax.rem(c + dc, 2)
        return there, lax.rem(lat + dx, 4)

    loads = []
    for number, (src, dst) in enumerate((
        (own_hbm, own_ref), (obs_hbm, obs_ref), (cell_hbm, cell_ref), (east_hbm, east_ref),
        (north_hbm, north_ref), (area_hbm, area_ref), (sea_hbm, sea_ref),
        (vert_hbm, vert_ref), (thick_hbm, thick_ref),
    )):
        load = pltpu.make_async_copy(src, dst, load_sem.at[number])
        load.start()
        loads.append(load)

    barrier = pltpu.get_barrier_semaphore()

    deep = [lax.rem(z + d, 4) * 8 for d in range(4)]
    wide = [lax.rem(y + d, 4) * 2 for d in range(4)]
    core = [lax.rem(c + d, 2) for d in range(2)]
    flat = [lax.rem(lat + d, 4) for d in range(4)]
    for a in range(4):
        for b in range(4):
            for d in range(2):
                there = deep[a] + wide[b] + core[d]
                for e in range(4):
                    if a + b + d + e:
                        pl.semaphore_signal(
                            barrier, inc=1, device_id=(there, flat[e]), device_id_type=MESH
                        )

    loads[0].wait()
    places(count_ref[0], own_ref, idx_v)
    idx_copy = pltpu.make_async_copy(idx_v, idx_ref, idx_sem)
    idx_copy.start()
    for load in loads[1:]:
        load.wait()

    def turn(b, _):
        columns = pl.ds(pl.multiple_of(b * NX, NX), NX)
        block = jnp.concatenate(
            [
                obs_ref[:, columns],
                cell_ref[pl.ds(b, 1), :].astype(F32),
                jnp.zeros((NX - LEV - 1, NX), F32),
            ],
            0,
        )
        table[columns, :] = block.T
        return 0

    lax.fori_loop(0, SLOTS // NX, turn, 0, unroll=4)
    spare = (iota((8, NX), 0) * 1024).astype(F32)
    table[pl.ds(SLOTS, 8), :] = jnp.where(iota((8, NX), 1) == LEV, spare, 0.0)

    lane = iota((NY, NX), 1)
    cols = jnp.zeros((NY, NX), F32)
    coef_refs = (east_ref, north_ref, area_ref, sea_ref)
    for i in range(4):
        whole = coef_refs[i][...].astype(F32)
        coef_box[i, pl.ds(0, 8), :] = whole[:8]
        coef_box[i, pl.ds(8, 8), :] = whole[NY - 8:]
        cols = jnp.where((lane >= 8 * i) & (lane < 8 * i + 4), pltpu.roll(whole, 8 * i, 1), cols)
        cols = jnp.where(
            (lane >= 8 * i + 4) & (lane < 8 * i + 8),
            pltpu.roll(whole, (8 * i + 4 - 124) % NX, 1),
            cols,
        )
    colbox[...] = cols
    idx_copy.wait()
    pl.semaphore_wait(barrier, DEV - 1)

    east, west = lax.rem(lon + 1, 32), lax.rem(lon + 31, 32)
    north, south = lax.rem(lat + 1, 4), lax.rem(lat + 3, 4)
    side = []

    def beside(number, src, dst, where):
        copy = pltpu.make_async_remote_copy(
            src_ref=src, dst_ref=dst, send_sem=side_send.at[number], recv_sem=side_recv.at[number],
            device_id=where, device_id_type=MESH,
        )
        copy.start()
        side.append(copy)

    beside(0, coef_box.at[:, pl.ds(8, 8), :], row_halo.at[0], (lon, north))
    beside(1, coef_box.at[:, pl.ds(0, 8), :], row_halo.at[1], (lon, south))
    beside(2, colbox, col_halo.at[0], (east, lat))
    beside(3, colbox, col_halo.at[1], (west, lat))
    beside(4, colbox.at[pl.ds(NY - 8, 8), :], corner.at[0], (east, north))
    beside(5, colbox.at[pl.ds(NY - 8, 8), :], corner.at[1], (west, north))
    beside(6, colbox.at[pl.ds(0, 8), :], corner.at[2], (east, south))
    beside(7, colbox.at[pl.ds(0, 8), :], corner.at[3], (west, south))

    lane8 = iota((8, NX), 1)
    lane32 = iota((32, NX), 1)

    def gather(owner):
        for k in range(CAP):
            at = jnp.minimum(jnp.maximum(idx_ref[owner, k], 0), SLOTS + 7)
            rows[pl.ds(k, 1), :] = table[pl.ds(at, 1), :]

    def fold(box):
        box[pl.ds(0, 32), :] = jnp.where(
            lane32 < 64, rows[pl.ds(0, 32), :], pltpu.roll(rows[pl.ds(32, 32), :], 64, 1)
        )
        rest = jnp.zeros((8, NX), F32)
        for g in range(8):
            piece = rows[pl.ds(8 * g, 8), :]
            shift = (16 * g - 64) % NX
            piece = pltpu.roll(piece, shift, 1) if shift else piece
            rest = jnp.where(lane8 // 16 == g, piece, rest)
        box[pl.ds(32, 8), :] = rest

    def send(k, _):
        dlon, dlat = target(k)
        owner = dlon * 4 + dlat
        gather(owner)
        fold(outbox.at[owner])
        pltpu.make_async_remote_copy(
            src_ref=outbox.at[owner], dst_ref=recv.at[k], send_sem=send_sem, recv_sem=recv_sem.at[k],
            device_id=(dlon, dlat), device_id_type=MESH,
        ).start()
        return 0

    lax.fori_loop(1, DEV, send, 0)
    gather(me)
    fold(recv.at[0])
    vertical_fourth(vert_ref, thick_ref, matrix_ref, cp_ref, dp_ref)
    for copy in side:
        copy.wait()
    factors(coef_refs, row_halo, col_halo, corner, coef_main, coef_side, fac_main_ref, fac_strip_ref)
    clear((sum0, sum1, sum2, sum3))

    pick = jnp.where(
        iota((8, NX), 1) == 16 * iota((8, NX), 0) + (LEV - 64), 1.0, 0.0
    ).astype(F32)

    def unfold(k):
        rest = recv[k, pl.ds(32, 8), :]
        for g in range(8):
            tail = pltpu.roll(rest, (64 - 16 * g) % NX, 1) if g != 4 else rest
            head = recv[k, pl.ds(8 * (g % 4), 8), :]
            head = pltpu.roll(head, 64, 1) if g >= 4 else head
            full_ref[pl.ds(k * CAP + 8 * g, 8), :] = jnp.where(lane8 < 64, head, tail)

    def arrive(k, _):
        pltpu.make_async_copy(recv.at[k], recv.at[k], recv_sem.at[k]).wait()
        return 0

    def spread_out(k, _):
        unfold(k)
        return 0

    for b in range(8):
        lax.fori_loop(max(16 * b, 1), 16 * b + 16, arrive, 0)
        lax.fori_loop(16 * b, 16 * b + 16, spread_out, 0, unroll=4)
        part = recv[pl.ds(16 * b, 16), pl.ds(32, 8), :].reshape(NX, NX)
        found = lax.dot_general(
            pick, part, (((1,), (1,)), ((), ())), precision=HI, preferred_element_type=F32
        )
        cells_ref[pl.ds(8 * b, 8), :] = (found + 0.5).astype(jnp.int32)
    others = pl.ds(0, DEV - 1)
    pltpu.make_async_copy(outbox.at[others], outbox.at[others], send_sem).wait()


def send_profiles(count, vert_coef, inv_thick, owner, obs, cell, coefs):
    vm = pl.BlockSpec(memory_space=pltpu.VMEM)
    sm = pl.BlockSpec(memory_space=pltpu.SMEM)
    plane = pltpu.VMEM((4, YE, NX), F32)
    return pl.pallas_call(
        send_body,
        out_shape=(
            jax.ShapeDtypeStruct((SLOTS, NX), F32),
            jax.ShapeDtypeStruct((SLOTS // NX, NX), jnp.int32),
            jax.ShapeDtypeStruct((5, YE, NX), F32),
            jax.ShapeDtypeStruct((5, 24, NX), F32),
            jax.ShapeDtypeStruct((NX, NX), F32),
        ) + (jax.ShapeDtypeStruct((SLOTS, NX), F32),) * EARLY,
        in_specs=[sm] + [pl.BlockSpec(memory_space=pltpu.HBM)] * 9,
        out_specs=(vm,) * (5 + EARLY),
        scratch_shapes=[
            pltpu.SMEM((LEV - 1,), F32),
            pltpu.SMEM((LEV,), F32),
            pltpu.VMEM((SLOTS // NX, NX), jnp.int32),
            pltpu.VMEM((LEV, SLOTS), F32),
            pltpu.VMEM((SLOTS // NX, NX), jnp.int32),
            pltpu.VMEM((NY, NX), F32),
            pltpu.VMEM((NY, NX), F32),
            pltpu.VMEM((NY, NX), F32),
            pltpu.VMEM((NY, NX), jnp.int32),
            pltpu.VMEM((DEV, ROWS, NX), F32),
            pltpu.SemaphoreType.DMA((9,)),
            pltpu.VMEM((SLOTS + 8, NX), F32),
            pltpu.VMEM((CAP, NX), F32),
            pltpu.VMEM((DEV, ROWS, NX), F32),
            pltpu.VMEM((4, 16, NX), F32),
            pltpu.VMEM((NY, NX), F32),
            pltpu.VMEM((2, 4, 8, NX), F32),
            pltpu.VMEM((2, NY, NX), F32),
            pltpu.VMEM((4, 8, NX), F32),
            plane,
            plane,
            pltpu.VMEM((NX, NX), F32),
            pltpu.VMEM((NX, NX), F32),
            pltpu.VMEM((DEV, NX), jnp.int32),
            pltpu.SMEM((DEV, NX), jnp.int32),
            pltpu.SemaphoreType.DMA(()),
            pltpu.SemaphoreType.DMA(()),
            pltpu.SemaphoreType.DMA((DEV,)),
            pltpu.SemaphoreType.DMA((8,)),
            pltpu.SemaphoreType.DMA((8,)),
        ],
        compiler_params=pltpu.CompilerParams(
            collective_id=0, has_side_effects=True, vmem_limit_bytes=18 << 20
        ),
        name="send_profiles",
    )(count, *map(in_hbm, (
        vert_coef, inv_thick, owner.reshape(SLOTS // NX, NX), obs,
        cell.reshape(SLOTS // NX, NX), *coefs,
    )))


WAYS = 8
EARLY = 4


def add_body(
    full, cell_v, forcing_ref, matrix_ref, in0, in1, in2, in3, out_ref,
    acc0, acc1, acc2, acc3, acc4, acc5, acc6, acc7, cell_s, sem,
):
    accs = (acc0, acc1, acc2, acc3, acc4, acc5, acc6, acc7)
    copy = pltpu.make_async_copy(cell_v, cell_s, sem)
    copy.start()

    clear(accs[EARLY:])
    copy.wait()
    per = DEV // WAYS

    def add(s, _):
        starts = [pl.multiple_of((s + w * per) * CAP, CAP) for w in range(WAYS)]
        firsts = [(s + w * per) // 16 * 1024 + (s + w * per) % 16 * 8 for w in range(WAYS)]
        blocks = [full.at[pl.ds(start, CAP), :] for start in starts]
        for g in range(8):
            for e in range(8):
                places_of = [pl.ds(cell_s[first + (128 * g + e)], 1) for first in firsts]
                sums = [
                    acc[at, :] + block[pl.ds(8 * g + e, 1), :]
                    for acc, at, block in zip(accs, places_of, blocks)
                ]
                for acc, at, total in zip(accs, places_of, sums):
                    acc[at, :] = total
        return 0

    lax.fori_loop(0, per, add, 0)
    whole = matrix_ref[pl.ds(0, LP), pl.ds(0, LP)]
    high = whole.astype(BF16)
    low = (whole - high.astype(F32)).astype(BF16)
    matrix = jnp.concatenate([high, high, low], 1)
    padding = jnp.zeros((LP - LEV, NX), F32)

    def finish(b, _):
        loaded = []
        for h in range(2):
            y = 2 * b + h
            at = pl.ds(pl.multiple_of(y * NX, NX), NX)
            parts = [acc[at, :] for acc in accs]
            while len(parts) > 1:
                parts = [p + q for p, q in zip(parts[::2], parts[1::2])]
            total = parts[0]
            column = total.T[:LEV] + forcing_ref[pl.ds(y, LEV, stride=NY), :]
            loaded.append(jnp.concatenate([column, padding], 0))
        values = jnp.concatenate(loaded, 1)
        top = values.astype(BF16)
        rest = (values - top.astype(F32)).astype(BF16)
        parts = jnp.concatenate([top, rest, top], 0)
        product = jnp.dot(matrix, parts, preferred_element_type=F32)
        out_ref[2 * b] = product[:, :NX]
        out_ref[2 * b + 1] = product[:, NX:]
        return 0

    lax.fori_loop(0, NY // 2, finish, 0, unroll=8)


def add_profiles(full, cells, forcing, matrix, sums):
    vm = pl.BlockSpec(memory_space=pltpu.VMEM)
    return pl.pallas_call(
        add_body,
        out_shape=(jax.ShapeDtypeStruct((NY, LP, NX), F32),)
        + (jax.ShapeDtypeStruct((SLOTS, NX), F32),) * EARLY,
        in_specs=[vm] * (4 + EARLY),
        out_specs=(vm,) * (1 + EARLY),
        input_output_aliases={4 + w: 1 + w for w in range(EARLY)},
        scratch_shapes=[pltpu.VMEM((SLOTS, NX), F32)] * (WAYS - EARLY)
        + [
            pltpu.SMEM((SLOTS,), jnp.int32),
            pltpu.SemaphoreType.DMA(()),
        ],
        compiler_params=pltpu.CompilerParams(vmem_limit_bytes=22 << 20),
        name="add_profiles",
    )(full, cells.reshape(SLOTS), forcing.reshape(LEV * NY, NX), matrix, *sums)[0]


def spread_body(
    field_ref, fac_ref, strip_ref,
    out_ref,
    wide_a, wide_b, tips, strip_a, strip_b, east_box, west_box, from_west, from_east, corner_box, corners,
    own_sem, send_sem, recv_sem,
):
    lon = lax.axis_index("lon")
    lat = lax.axis_index("lat")
    east, west = lax.rem(lon + 1, 32), lax.rem(lon + 31, 32)
    north, south = lax.rem(lat + 1, 4), lax.rem(lat + 3, 4)
    peers = [
        (lon, north), (lon, south), (east, lat), (west, lat),
        (east, north), (west, north), (east, south), (west, south),
    ]
    barrier = pltpu.get_barrier_semaphore()
    for peer in peers:
        pl.semaphore_signal(barrier, inc=1, device_id=peer, device_id_type=MESH)
    own = pltpu.make_async_copy(field_ref, wide_a.at[pl.ds(HALO, NY)], own_sem)
    own.start()
    own.wait()

    lane = iota((LP, NX), 1)
    group, place = lane // 32, lane % 32

    def tip(low, high, parts):
        def one(q, _):
            total = jnp.zeros((LP, NX), F32)
            for j in parts:
                piece = pltpu.roll(wide_a[q + Q * j], (32 * j + 8) % NX, 1)
                total = jnp.where((group == j) & (place < 16), piece, total)
            tips[q] = total
            return 0

        lax.fori_loop(low, high, one, 0, unroll=2)

    tip(0, HALO, (1, 2, 3))
    tip(HALO, Q - HALO, (0, 1, 2, 3))
    tip(Q - HALO, Q, (0, 1, 2))
    for b in range(3):
        e = jnp.zeros((LP, NX), F32)
        w = jnp.zeros((LP, NX), F32)
        for q in range(8 * b, min(8 * b + 8, Q)):
            here = place // 4 == q % 8
            row = tips[q]
            e = jnp.where(here, pltpu.roll(row, (4 * (q % 8) - 4) % NX, 1), e)
            w = jnp.where(here, pltpu.roll(row, (4 * (q % 8) - 8) % NX, 1), w)
        east_box[b] = e
        west_box[b] = w

    lane16 = iota((16, NX), 1)
    for number, (box, start) in enumerate(
        ((east_box.at[1], 104), (west_box.at[1], 104), (east_box.at[0], 16), (west_box.at[0], 16))
    ):
        total = jnp.zeros((16, NX), F32)
        for h in range(LP // 16):
            piece = pltpu.roll(box[pl.ds(16 * h, 16), :], (16 * h - start) % NX, 1)
            total = jnp.where(lane16 // 16 == h, piece, total)
        corner_box[number] = total

    pl.semaphore_wait(barrier, 8)
    moves = [
        (field_ref.at[pl.ds(NY - HALO, HALO)], wide_a.at[pl.ds(0, HALO)]),
        (field_ref.at[pl.ds(0, HALO)], wide_a.at[pl.ds(NY + HALO, HALO)]),
        (east_box, from_west),
        (west_box, from_east),
        (corner_box.at[0], corners.at[0]),
        (corner_box.at[1], corners.at[1]),
        (corner_box.at[2], corners.at[2]),
        (corner_box.at[3], corners.at[3]),
    ]
    copies = []
    for number, (src, dst) in enumerate(moves):
        copy = pltpu.make_async_remote_copy(
            src_ref=src, dst_ref=dst, send_sem=send_sem.at[number], recv_sem=recv_sem.at[number],
            device_id=peers[number], device_id_type=MESH,
        )
        copy.start()
        copies.append(copy)

    def stencil(facs, y, src, at):
        centre = src[at]

        def fac(i):
            return jnp.broadcast_to(facs[i, pl.ds(y, 1), :], (LP, NX))

        return (
            fac(0) * centre
            + fac(1) * pltpu.roll(centre, NX - 1, 1)
            + fac(2) * pltpu.roll(centre, 1, 1)
            + fac(3) * src[at + 1]
            + fac(4) * src[at - 1]
        )

    def rows(t, low, high, unroll):
        src, dst = (wide_a, wide_b) if t % 2 else (wide_b, wide_a)

        def row(y, _):
            dst[y] = stencil(fac_ref, y, src, y)
            return 0

        lax.fori_loop(low, high, row, 0, unroll=unroll)

    for t in range(1, 5):
        rows(t, HALO + t, NY + HALO - t, 8)

    for copy in copies:
        copy.wait()

    for near, from_side in ((0, from_west), (1, from_east)):
        below, above = corners[near], corners[near + 2]
        for h in range(LP // 16):
            at = pl.ds(16 * h, 16)

            def put(box, keep, corner, shift, at=at, from_side=from_side):
                box_rows = from_side[box, at, :]
                piece = pltpu.roll(corner, shift % NX, 1) if shift % NX else corner
                from_side[box, at, :] = jnp.where(keep, piece, box_rows)

            put(0, lane16 < 16, below, -16 * h)
            put(1, lane16 >= 120, above, 120 - 16 * h)
            put(2, (lane16 >= 96) & (lane16 < 104), above, 88 - 16 * h)
    for h in range(HALO):
        q = Q - HALO + h
        tips[h] = jnp.where((group == 0) & (place < 16), pltpu.roll(wide_a[h], 8, 1), tips[h])
        tips[q] = jnp.where((group == 3) & (place < 16), pltpu.roll(wide_a[q + 3 * Q], 104, 1), tips[q])
    for q in range(Q):
        row = tips[q]
        right = pltpu.roll(from_east[q // 8], (8 - 4 * (q % 8)) % NX, 1)
        left = pltpu.roll(from_west[q // 8], (16 - 4 * (q % 8)) % NX, 1)
        far = jnp.where((place >= 16) & (place < 20), left, pltpu.roll(row, 12, 1))
        strip_a[q + 1] = jnp.where(place < 8, row, jnp.where(place < 12, right, far))

    for t in range(1, 5):
        rows(t, t, HALO + t, 4)
        rows(t, NY + HALO - t, NY + 2 * HALO - t, 4)
    for t in range(4):
        src, dst = (strip_a, strip_b) if t % 2 == 0 else (strip_b, strip_a)
        src[0] = pltpu.roll(src[Q], 32, 1)
        src[Q + 1] = pltpu.roll(src[1], NX - 32, 1)

        def strip(q, _):
            dst[q + 1] = stencil(strip_ref, q, src, q + 1)
            return 0

        lax.fori_loop(0, Q, strip, 0, unroll=6)

    edge = (lane < HALO) | (lane >= NX - HALO)

    def write(low, high, parts):
        def one(q, _):
            row = strip_a[q + 1]
            row = jnp.where(place < 8, row, pltpu.roll(row, NX - 12, 1))
            for j in parts:
                y = q + Q * j
                whole = jnp.where(edge, pltpu.roll(row, (120 - 32 * j) % NX, 1), wide_a[y])
                out_ref[pl.ds(y - HALO, LEV, stride=NY), :] = whole[:LEV]
            return 0

        lax.fori_loop(low, high, one, 0, unroll=2)

    write(0, HALO, (1, 2, 3))
    write(HALO, Q - HALO, (0, 1, 2, 3))
    write(Q - HALO, Q, (0, 1, 2))


def spread(field, fac_main, fac_strip):
    vm = pl.BlockSpec(memory_space=pltpu.VMEM)
    wide = pltpu.VMEM((YE, LP, NX), F32)
    strip = pltpu.VMEM((Q + 2, LP, NX), F32)
    box = pltpu.VMEM((3, LP, NX), F32)
    return pl.pallas_call(
        spread_body,
        out_shape=jax.ShapeDtypeStruct((LEV * NY, NX), F32),
        in_specs=[pl.BlockSpec(memory_space=pl.ANY), vm, vm],
        out_specs=vm,
        scratch_shapes=[
            wide, wide, pltpu.VMEM((Q, LP, NX), F32), strip, strip, box, box, box, box,
            pltpu.VMEM((4, 16, NX), F32),
            pltpu.VMEM((4, 16, NX), F32),
            pltpu.SemaphoreType.DMA(()),
            pltpu.SemaphoreType.DMA((8,)),
            pltpu.SemaphoreType.DMA((8,)),
        ],
        compiler_params=pltpu.CompilerParams(
            collective_id=1, has_side_effects=True, vmem_limit_bytes=24 << 20
        ),
        name="spread",
    )(field, fac_main, fac_strip)


def local(
    forcing, obs_values, obs_owner, obs_cell, obs_count,
    coef_east, coef_north, area_inv, sea_mask, vert_coef, inv_thick,
):
    coefs = (coef_east, coef_north, area_inv, sea_mask)
    full, cells, fac_main, fac_strip, matrix, *sums = send_profiles(
        obs_count, vert_coef, inv_thick, obs_owner, obs_values, obs_cell, coefs
    )
    field = add_profiles(full, cells, forcing, matrix, sums)
    return spread(field, fac_main, fac_strip).reshape(LEV, NY, NX)


def solution(mesh):
    lead = P(("lon", "lat"))
    flat = P("lat", "lon")
    in_specs = (
        P(None, "lat", "lon"), P(None, ("lon", "lat")), lead, lead, lead,
        flat, flat, flat, flat, P(), P(),
    )
    return jax.shard_map(
        local, mesh=mesh, in_specs=in_specs, out_specs=P(None, "lat", "lon"), check_vma=False
    )
```

```python
import jax
import jax.numpy as jnp
from jax import lax
from jax.experimental import pallas as pl
from jax.experimental.pallas import tpu as pltpu
from jax.sharding import PartitionSpec as P

LEV = 75
LP = 80
NX = 128
NY = 64
DEV = 128
CAP = 64
SLOTS = 8192
ROWS = 40
HALO = 4
YE = NY + 2 * HALO
Q = 18
STRIDE = 59
F32 = jnp.float32
BF16 = jnp.bfloat16
HI = lax.Precision.HIGHEST
MESH = pl.DeviceIdType.MESH


def in_hbm(x):
    return pltpu.with_memory_space_constraint(x, pltpu.HBM)


def iota(shape, dim, dtype=jnp.int32):
    return lax.broadcasted_iota(dtype, shape, dim)


def vertical_fourth(vert_ref, thick_ref, out_ref, cp_ref, dp_ref):
    lane = iota((1, NX), 1)
    dp_ref[...] = jnp.zeros_like(dp_ref)

    def forward(i, carry):
        cp, dp = carry
        up = jnp.where(i < LEV - 1, vert_ref[jnp.minimum(i, LEV - 2)], 0.0)
        low = jnp.where(i > 0, vert_ref[jnp.maximum(i - 1, 0)], 0.0)
        middle = 1.0 + (low + up) * thick_ref[i]
        above = -thick_ref[jnp.minimum(i + 1, LEV - 1)] * up
        below = -thick_ref[jnp.maximum(i - 1, 0)] * low
        inv = 1.0 / (middle - below * cp)
        cp = above * inv
        dp = (jnp.where(lane == i, 1.0, 0.0) - below * dp) * inv
        cp_ref[pl.ds(i, 1), :] = cp
        dp_ref[pl.ds(i, 1), :] = dp
        return cp, dp

    zero = jnp.zeros((1, NX), F32)
    lax.fori_loop(0, LEV, forward, (zero, zero))

    def backward(j, x):
        i = LEV - 1 - j
        x = dp_ref[pl.ds(i, 1), :] - cp_ref[pl.ds(i, 1), :] * x
        dp_ref[pl.ds(i, 1), :] = x
        return x

    lax.fori_loop(0, LEV, backward, zero)
    single = dp_ref[...]
    double = jnp.dot(single, single, precision=HI, preferred_element_type=F32)
    out_ref[...] = jnp.dot(double, double, precision=HI, preferred_element_type=F32)


def places(count, own_ref, idx_ref):
    width = 256
    lane = iota((1, width), 1)
    owners = iota((DEV, width), 0)
    tri = (iota((width, width + NX), 0) <= iota((width, width + NX), 1)) | (
        iota((width, width + NX), 1) >= width
    )
    tri = tri.astype(F32).astype(BF16)
    kth = iota((CAP, width), 0).astype(F32)
    number = (iota((CAP, width), 1) + 1).astype(F32)
    acc_lane = iota((DEV, NX), 1)

    def step(b, carry):
        offset, acc = carry
        own = jnp.concatenate([own_ref[pl.ds(2 * b, 1), :], own_ref[pl.ds(2 * b + 1, 1), :]], 1)
        own = jnp.where(lane + b * width < count, own, -1)
        onehot = jnp.where(jnp.broadcast_to(own, (DEV, width)) == owners, 1.0, 0.0)
        ones = onehot.astype(BF16)
        prefix = jnp.dot(ones, tri, preferred_element_type=F32)
        rank = prefix[:, :width] + jnp.concatenate([offset, offset], 1)
        rank = jnp.sum(onehot * rank, axis=0, keepdims=True) - 1.0
        hit = jnp.where(jnp.broadcast_to(rank, (CAP, width)) == kth, 1.0, 0.0)
        both = jnp.concatenate([hit, hit * number], 0).astype(BF16)
        found = lax.dot_general(ones, both, (((1,), (1,)), ((), ())), preferred_element_type=F32)
        scale = jnp.where(acc_lane < CAP, (b * width).astype(F32), 1.0)
        return offset + prefix[:, width:], acc + found * scale

    zero = jnp.zeros((DEV, NX), F32)
    _, acc = lax.fori_loop(0, SLOTS // width, step, (zero, zero), unroll=16)
    total = (acc + pltpu.roll(acc, CAP, 1)).astype(jnp.int32)
    idx_ref[...] = jnp.clip(jnp.where(total > 0, total - 1, SLOTS + acc_lane % 8), 0, SLOTS + 7)


def factors(coef_refs, row_halo_ref, col_halo_ref, corner_ref, coef_main, coef_side, fac_main_ref, fac_strip_ref):
    lat = lax.axis_index("lat")
    lane64 = iota((NY, NX), 1)
    lane4 = iota((HALO, NX), 1)
    for i in range(4):
        coef_main[i, pl.ds(HALO, NY), :] = coef_refs[i][...].astype(F32)
        coef_main[i, pl.ds(0, HALO), :] = row_halo_ref[0, i, pl.ds(4, HALO), :]
        coef_main[i, pl.ds(NY + HALO, HALO), :] = row_halo_ref[1, i, pl.ds(0, HALO), :]

        def sides(lanes, left, right, i=i):
            return jnp.where(
                lanes < 64,
                pltpu.roll(right, (-8 * i) % NX, 1),
                pltpu.roll(left, (124 - 8 * i - 4) % NX, 1),
            )

        coef_side[i, pl.ds(HALO, NY), :] = sides(lane64, col_halo_ref[0], col_halo_ref[1])
        coef_side[i, pl.ds(0, HALO), :] = sides(
            lane4, corner_ref[0, pl.ds(4, HALO), :], corner_ref[1, pl.ds(4, HALO), :]
        )
        coef_side[i, pl.ds(NY + HALO, HALO), :] = sides(
            lane4, corner_ref[2, pl.ds(0, HALO), :], corner_ref[3, pl.ds(0, HALO), :]
        )
    row = iota((YE, NX), 0)
    first_row = jnp.where(lat == 0, HALO, 0)
    last_row = jnp.where(lat == 3, NY + HALO, YE)
    inside = (row >= first_row) & (row < last_row)
    lanes = iota((YE, NX), 1)

    def shifts(main, side):
        first, last = lanes == 0, lanes == NX - 1
        main_e = pltpu.roll(jnp.where(first, side, main), NX - 1, 1)
        side_e = pltpu.roll(jnp.where(first, main, side), NX - 1, 1)
        main_w = pltpu.roll(jnp.where(last, side, main), 1, 1)
        side_w = pltpu.roll(jnp.where(last, main, side), 1, 1)
        return main_e, side_e, main_w, side_w

    sea_m = jnp.where(inside, coef_main[3], 0.0)
    sea_s = jnp.where(inside, coef_side[3], 0.0)
    area_m, area_s = coef_main[2], coef_side[2]
    sea_me, sea_se, _, _ = shifts(sea_m, sea_s)
    east_m = coef_main[0] * sea_m * sea_me
    east_s = coef_side[0] * sea_s * sea_se
    _, _, west_m, west_s = shifts(east_m, east_s)
    area_me, area_se, area_mw, area_sw = shifts(area_m, area_s)

    def five(north_coef, ee, ww, sea, area, area_e, area_w):
        nn = north_coef * sea * pltpu.roll(sea, YE - 1, 0)
        ss = pltpu.roll(nn, 1, 0)
        return (
            1.0 - area * (ee + ww + nn + ss),
            ee * area_e,
            ww * area_w,
            nn * pltpu.roll(area, YE - 1, 0),
            ss * pltpu.roll(area, 1, 0),
        )

    mains = five(coef_main[1], east_m, west_m, sea_m, area_m, area_me, area_mw)
    sides = five(coef_side[1], east_s, west_s, sea_s, area_s, area_se, area_sw)
    laneq = iota((Q, NX), 1)
    group, place = laneq // 32, laneq % 32
    gap = ((place >= 12) & (place < 16)) | (place >= 28)
    for i in range(5):
        fac_main_ref[i] = mains[i]
        coef_main[0] = jnp.where(lanes < 64, sides[i], mains[i])
        coef_main[1] = jnp.where(lanes < 64, mains[i], sides[i])
        strip = jnp.zeros((Q, NX), F32)
        for j in range(4):
            own = pl.ds(Q * j, Q)
            near = pltpu.roll(coef_main[0, own, :], (32 * j + 8) % NX, 1)
            far = pltpu.roll(coef_main[1, own, :], (32 * j + 20) % NX, 1)
            strip = jnp.where(group == j, jnp.where(place < 14, near, far), strip)
        fac_strip_ref[i, pl.ds(0, Q), :] = jnp.where(gap, 0.0, strip)


def clear(refs):
    def some(i, _):
        at = pl.ds(pl.multiple_of(i * 64, 64), 64)
        for ref in refs:
            ref[at, :] = jnp.zeros((64, NX), F32)
        return 0

    lax.fori_loop(0, SLOTS // 64, some, 0, unroll=2)


def send_body(
    count_ref, vert_hbm, thick_hbm, own_hbm, obs_hbm, cell_hbm, east_hbm, north_hbm, area_hbm, sea_hbm,
    full_ref, cells_ref, fac_main_ref, fac_strip_ref, matrix_ref, sum0, sum1, sum2, sum3,
    vert_ref, thick_ref, own_ref, obs_ref, cell_ref, east_ref, north_ref, area_ref, sea_ref,
    recv, load_sem, table, rows, outbox, coef_box, colbox, row_halo, col_halo, corner, coef_main, coef_side,
    cp_ref, dp_ref, idx_v, idx_ref, idx_sem, send_sem, recv_sem, side_send, side_recv,
):
    lon = lax.axis_index("lon")
    lat = lax.axis_index("lat")
    z, y, c = lax.div(lon, 8), lax.rem(lax.div(lon, 2), 4), lax.rem(lon, 2)
    me = lon * 4 + lat

    def target(k):
        q = lax.rem(k * STRIDE, DEV)
        dx, dc = lax.rem(q, 4), lax.rem(lax.div(q, 4), 2)
        dy, dz = lax.rem(lax.div(q, 8), 4), lax.div(q, 32)
        there = (lax.rem(z + dz, 4) * 4 + lax.rem(y + dy, 4)) * 2 + lax.rem(c + dc, 2)
        return there, lax.rem(lat + dx, 4)

    loads = []
    for number, (src, dst) in enumerate((
        (own_hbm, own_ref), (obs_hbm, obs_ref), (cell_hbm, cell_ref), (east_hbm, east_ref),
        (north_hbm, north_ref), (area_hbm, area_ref), (sea_hbm, sea_ref),
        (vert_hbm, vert_ref), (thick_hbm, thick_ref),
    )):
        load = pltpu.make_async_copy(src, dst, load_sem.at[number])
        load.start()
        loads.append(load)

    barrier = pltpu.get_barrier_semaphore()

    deep = [lax.rem(z + d, 4) * 8 for d in range(4)]
    wide = [lax.rem(y + d, 4) * 2 for d in range(4)]
    core = [lax.rem(c + d, 2) for d in range(2)]
    flat = [lax.rem(lat + d, 4) for d in range(4)]
    for a in range(4):
        for b in range(4):
            for d in range(2):
                there = deep[a] + wide[b] + core[d]
                for e in range(4):
                    if a + b + d + e:
                        pl.semaphore_signal(
                            barrier, inc=1, device_id=(there, flat[e]), device_id_type=MESH
                        )

    loads[0].wait()
    places(count_ref[0], own_ref, idx_v)
    idx_copy = pltpu.make_async_copy(idx_v, idx_ref, idx_sem)
    idx_copy.start()
    for load in loads[1:]:
        load.wait()

    def turn(b, _):
        columns = pl.ds(pl.multiple_of(b * NX, NX), NX)
        block = jnp.concatenate(
            [
                obs_ref[:, columns],
                cell_ref[pl.ds(b, 1), :].astype(F32),
                jnp.zeros((NX - LEV - 1, NX), F32),
            ],
            0,
        )
        table[columns, :] = block.T
        return 0

    lax.fori_loop(0, SLOTS // NX, turn, 0, unroll=4)
    spare = (iota((8, NX), 0) * 1024).astype(F32)
    table[pl.ds(SLOTS, 8), :] = jnp.where(iota((8, NX), 1) == LEV, spare, 0.0)

    lane = iota((NY, NX), 1)
    cols = jnp.zeros((NY, NX), F32)
    coef_refs = (east_ref, north_ref, area_ref, sea_ref)
    for i in range(4):
        whole = coef_refs[i][...].astype(F32)
        coef_box[i, pl.ds(0, 8), :] = whole[:8]
        coef_box[i, pl.ds(8, 8), :] = whole[NY - 8:]
        cols = jnp.where((lane >= 8 * i) & (lane < 8 * i + 4), pltpu.roll(whole, 8 * i, 1), cols)
        cols = jnp.where(
            (lane >= 8 * i + 4) & (lane < 8 * i + 8),
            pltpu.roll(whole, (8 * i + 4 - 124) % NX, 1),
            cols,
        )
    colbox[...] = cols
    idx_copy.wait()
    pl.semaphore_wait(barrier, DEV - 1)

    east, west = lax.rem(lon + 1, 32), lax.rem(lon + 31, 32)
    north, south = lax.rem(lat + 1, 4), lax.rem(lat + 3, 4)
    side = []

    def beside(number, src, dst, where):
        copy = pltpu.make_async_remote_copy(
            src_ref=src, dst_ref=dst, send_sem=side_send.at[number], recv_sem=side_recv.at[number],
            device_id=where, device_id_type=MESH,
        )
        copy.start()
        side.append(copy)

    beside(0, coef_box.at[:, pl.ds(8, 8), :], row_halo.at[0], (lon, north))
    beside(1, coef_box.at[:, pl.ds(0, 8), :], row_halo.at[1], (lon, south))
    beside(2, colbox, col_halo.at[0], (east, lat))
    beside(3, colbox, col_halo.at[1], (west, lat))
    beside(4, colbox.at[pl.ds(NY - 8, 8), :], corner.at[0], (east, north))
    beside(5, colbox.at[pl.ds(NY - 8, 8), :], corner.at[1], (west, north))
    beside(6, colbox.at[pl.ds(0, 8), :], corner.at[2], (east, south))
    beside(7, colbox.at[pl.ds(0, 8), :], corner.at[3], (west, south))

    lane8 = iota((8, NX), 1)
    lane32 = iota((32, NX), 1)

    def gather(owner):
        for k in range(CAP):
            at = jnp.minimum(jnp.maximum(idx_ref[owner, k], 0), SLOTS + 7)
            rows[pl.ds(k, 1), :] = table[pl.ds(at, 1), :]

    def fold(box):
        box[pl.ds(0, 32), :] = jnp.where(
            lane32 < 64, rows[pl.ds(0, 32), :], pltpu.roll(rows[pl.ds(32, 32), :], 64, 1)
        )
        rest = jnp.zeros((8, NX), F32)
        for g in range(8):
            piece = rows[pl.ds(8 * g, 8), :]
            shift = (16 * g - 64) % NX
            piece = pltpu.roll(piece, shift, 1) if shift else piece
            rest = jnp.where(lane8 // 16 == g, piece, rest)
        box[pl.ds(32, 8), :] = rest

    def send(k, _):
        dlon, dlat = target(k)
        owner = dlon * 4 + dlat
        gather(owner)
        fold(outbox.at[owner])
        pltpu.make_async_remote_copy(
            src_ref=outbox.at[owner], dst_ref=recv.at[k], send_sem=send_sem, recv_sem=recv_sem.at[k],
            device_id=(dlon, dlat), device_id_type=MESH,
        ).start()
        return 0

    lax.fori_loop(1, DEV, send, 0)
    gather(me)
    fold(recv.at[0])
    vertical_fourth(vert_ref, thick_ref, matrix_ref, cp_ref, dp_ref)
    for copy in side:
        copy.wait()
    factors(coef_refs, row_halo, col_halo, corner, coef_main, coef_side, fac_main_ref, fac_strip_ref)
    clear((sum0, sum1, sum2, sum3))

    pick = jnp.where(
        iota((8, NX), 1) == 16 * iota((8, NX), 0) + (LEV - 64), 1.0, 0.0
    ).astype(F32)

    def unfold(k):
        rest = recv[k, pl.ds(32, 8), :]
        for g in range(8):
            tail = pltpu.roll(rest, (64 - 16 * g) % NX, 1) if g != 4 else rest
            head = recv[k, pl.ds(8 * (g % 4), 8), :]
            head = pltpu.roll(head, 64, 1) if g >= 4 else head
            full_ref[pl.ds(k * CAP + 8 * g, 8), :] = jnp.where(lane8 < 64, head, tail)

    def arrive(k, _):
        pltpu.make_async_copy(recv.at[k], recv.at[k], recv_sem.at[k]).wait()
        return 0

    def spread_out(k, _):
        unfold(k)
        return 0

    for b in range(8):
        lax.fori_loop(max(16 * b, 1), 16 * b + 16, arrive, 0)
        lax.fori_loop(16 * b, 16 * b + 16, spread_out, 0, unroll=4)
        part = recv[pl.ds(16 * b, 16), pl.ds(32, 8), :].reshape(NX, NX)
        found = lax.dot_general(
            pick, part, (((1,), (1,)), ((), ())), precision=HI, preferred_element_type=F32
        )
        cells_ref[pl.ds(8 * b, 8), :] = (found + 0.5).astype(jnp.int32)
    others = pl.ds(0, DEV - 1)
    pltpu.make_async_copy(outbox.at[others], outbox.at[others], send_sem).wait()


def send_profiles(count, vert_coef, inv_thick, owner, obs, cell, coefs):
    vm = pl.BlockSpec(memory_space=pltpu.VMEM)
    sm = pl.BlockSpec(memory_space=pltpu.SMEM)
    plane = pltpu.VMEM((4, YE, NX), F32)
    return pl.pallas_call(
        send_body,
        out_shape=(
            jax.ShapeDtypeStruct((SLOTS, NX), F32),
            jax.ShapeDtypeStruct((SLOTS // NX, NX), jnp.int32),
            jax.ShapeDtypeStruct((5, YE, NX), F32),
            jax.ShapeDtypeStruct((5, 24, NX), F32),
            jax.ShapeDtypeStruct((NX, NX), F32),
        ) + (jax.ShapeDtypeStruct((SLOTS, NX), F32),) * EARLY,
        in_specs=[sm] + [pl.BlockSpec(memory_space=pltpu.HBM)] * 9,
        out_specs=(vm,) * (5 + EARLY),
        scratch_shapes=[
            pltpu.SMEM((LEV - 1,), F32),
            pltpu.SMEM((LEV,), F32),
            pltpu.VMEM((SLOTS // NX, NX), jnp.int32),
            pltpu.VMEM((LEV, SLOTS), F32),
            pltpu.VMEM((SLOTS // NX, NX), jnp.int32),
            pltpu.VMEM((NY, NX), F32),
            pltpu.VMEM((NY, NX), F32),
            pltpu.VMEM((NY, NX), F32),
            pltpu.VMEM((NY, NX), jnp.int32),
            pltpu.VMEM((DEV, ROWS, NX), F32),
            pltpu.SemaphoreType.DMA((9,)),
            pltpu.VMEM((SLOTS + 8, NX), F32),
            pltpu.VMEM((CAP, NX), F32),
            pltpu.VMEM((DEV, ROWS, NX), F32),
            pltpu.VMEM((4, 16, NX), F32),
            pltpu.VMEM((NY, NX), F32),
            pltpu.VMEM((2, 4, 8, NX), F32),
            pltpu.VMEM((2, NY, NX), F32),
            pltpu.VMEM((4, 8, NX), F32),
            plane,
            plane,
            pltpu.VMEM((NX, NX), F32),
            pltpu.VMEM((NX, NX), F32),
            pltpu.VMEM((DEV, NX), jnp.int32),
            pltpu.SMEM((DEV, NX), jnp.int32),
            pltpu.SemaphoreType.DMA(()),
            pltpu.SemaphoreType.DMA(()),
            pltpu.SemaphoreType.DMA((DEV,)),
            pltpu.SemaphoreType.DMA((8,)),
            pltpu.SemaphoreType.DMA((8,)),
        ],
        compiler_params=pltpu.CompilerParams(
            collective_id=0, has_side_effects=True, vmem_limit_bytes=18 << 20
        ),
        name="send_profiles",
    )(count, *map(in_hbm, (
        vert_coef, inv_thick, owner.reshape(SLOTS // NX, NX), obs,
        cell.reshape(SLOTS // NX, NX), *coefs,
    )))


WAYS = 8
EARLY = 4


def add_body(
    full, cell_v, forcing_ref, matrix_ref, in0, in1, in2, in3, out_ref,
    acc0, acc1, acc2, acc3, acc4, acc5, acc6, acc7, cell_s, sem,
):
    accs = (acc0, acc1, acc2, acc3, acc4, acc5, acc6, acc7)
    copy = pltpu.make_async_copy(cell_v, cell_s, sem)
    copy.start()

    clear(accs[EARLY:])
    copy.wait()
    per = DEV // WAYS

    def add(s, _):
        starts = [pl.multiple_of((s + w * per) * CAP, CAP) for w in range(WAYS)]
        firsts = [(s + w * per) // 16 * 1024 + (s + w * per) % 16 * 8 for w in range(WAYS)]
        blocks = [full.at[pl.ds(start, CAP), :] for start in starts]
        for g in range(8):
            for e in range(8):
                places_of = [pl.ds(cell_s[first + (128 * g + e)], 1) for first in firsts]
                sums = [
                    acc[at, :] + block[pl.ds(8 * g + e, 1), :]
                    for acc, at, block in zip(accs, places_of, blocks)
                ]
                for acc, at, total in zip(accs, places_of, sums):
                    acc[at, :] = total
        return 0

    lax.fori_loop(0, per, add, 0)
    whole = matrix_ref[pl.ds(0, LP), pl.ds(0, LP)]
    high = whole.astype(BF16)
    low = (whole - high.astype(F32)).astype(BF16)
    matrix = jnp.concatenate([high, high, low], 1)
    padding = jnp.zeros((LP - LEV, NX), F32)

    def finish(b, _):
        loaded = []
        for h in range(2):
            y = 2 * b + h
            at = pl.ds(pl.multiple_of(y * NX, NX), NX)
            parts = [acc[at, :] for acc in accs]
            while len(parts) > 1:
                parts = [p + q for p, q in zip(parts[::2], parts[1::2])]
            total = parts[0]
            column = total.T[:LEV] + forcing_ref[pl.ds(y, LEV, stride=NY), :]
            loaded.append(jnp.concatenate([column, padding], 0))
        values = jnp.concatenate(loaded, 1)
        top = values.astype(BF16)
        rest = (values - top.astype(F32)).astype(BF16)
        parts = jnp.concatenate([top, rest, top], 0)
        product = jnp.dot(matrix, parts, preferred_element_type=F32)
        out_ref[2 * b] = product[:, :NX]
        out_ref[2 * b + 1] = product[:, NX:]
        return 0

    lax.fori_loop(0, NY // 2, finish, 0, unroll=8)


def add_profiles(full, cells, forcing, matrix, sums):
    vm = pl.BlockSpec(memory_space=pltpu.VMEM)
    return pl.pallas_call(
        add_body,
        out_shape=(jax.ShapeDtypeStruct((NY, LP, NX), F32),)
        + (jax.ShapeDtypeStruct((SLOTS, NX), F32),) * EARLY,
        in_specs=[vm] * (4 + EARLY),
        out_specs=(vm,) * (1 + EARLY),
        input_output_aliases={4 + w: 1 + w for w in range(EARLY)},
        scratch_shapes=[pltpu.VMEM((SLOTS, NX), F32)] * (WAYS - EARLY)
        + [
            pltpu.SMEM((SLOTS,), jnp.int32),
            pltpu.SemaphoreType.DMA(()),
        ],
        compiler_params=pltpu.CompilerParams(vmem_limit_bytes=22 << 20),
        name="add_profiles",
    )(full, cells.reshape(SLOTS), forcing.reshape(LEV * NY, NX), matrix, *sums)[0]


def spread_body(
    field_ref, fac_ref, strip_ref,
    out_ref,
    wide_a, wide_b, tips, strip_a, strip_b, east_box, west_box, from_west, from_east, corner_box, corners,
    own_sem, send_sem, recv_sem,
):
    lon = lax.axis_index("lon")
    lat = lax.axis_index("lat")
    east, west = lax.rem(lon + 1, 32), lax.rem(lon + 31, 32)
    north, south = lax.rem(lat + 1, 4), lax.rem(lat + 3, 4)
    peers = [
        (lon, north), (lon, south), (east, lat), (west, lat),
        (east, north), (west, north), (east, south), (west, south),
    ]
    barrier = pltpu.get_barrier_semaphore()
    for peer in peers:
        pl.semaphore_signal(barrier, inc=1, device_id=peer, device_id_type=MESH)
    own = pltpu.make_async_copy(field_ref, wide_a.at[pl.ds(HALO, NY)], own_sem)
    own.start()
    own.wait()

    lane = iota((LP, NX), 1)
    group, place = lane // 32, lane % 32

    def tip(low, high, parts):
        def one(q, _):
            total = jnp.zeros((LP, NX), F32)
            for j in parts:
                piece = pltpu.roll(wide_a[q + Q * j], (32 * j + 8) % NX, 1)
                total = jnp.where((group == j) & (place < 16), piece, total)
            tips[q] = total
            return 0

        lax.fori_loop(low, high, one, 0, unroll=2)

    tip(0, HALO, (1, 2, 3))
    tip(HALO, Q - HALO, (0, 1, 2, 3))
    tip(Q - HALO, Q, (0, 1, 2))
    for b in range(3):
        e = jnp.zeros((LP, NX), F32)
        w = jnp.zeros((LP, NX), F32)
        for q in range(8 * b, min(8 * b + 8, Q)):
            here = place // 4 == q % 8
            row = tips[q]
            e = jnp.where(here, pltpu.roll(row, (4 * (q % 8) - 4) % NX, 1), e)
            w = jnp.where(here, pltpu.roll(row, (4 * (q % 8) - 8) % NX, 1), w)
        east_box[b] = e
        west_box[b] = w

    lane16 = iota((16, NX), 1)
    for number, (box, start) in enumerate(
        ((east_box.at[1], 104), (west_box.at[1], 104), (east_box.at[0], 16), (west_box.at[0], 16))
    ):
        total = jnp.zeros((16, NX), F32)
        for h in range(LP // 16):
            piece = pltpu.roll(box[pl.ds(16 * h, 16), :], (16 * h - start) % NX, 1)
            total = jnp.where(lane16 // 16 == h, piece, total)
        corner_box[number] = total

    pl.semaphore_wait(barrier, 8)
    moves = [
        (field_ref.at[pl.ds(NY - HALO, HALO)], wide_a.at[pl.ds(0, HALO)]),
        (field_ref.at[pl.ds(0, HALO)], wide_a.at[pl.ds(NY + HALO, HALO)]),
        (east_box, from_west),
        (west_box, from_east),
        (corner_box.at[0], corners.at[0]),
        (corner_box.at[1], corners.at[1]),
        (corner_box.at[2], corners.at[2]),
        (corner_box.at[3], corners.at[3]),
    ]
    copies = []
    for number, (src, dst) in enumerate(moves):
        copy = pltpu.make_async_remote_copy(
            src_ref=src, dst_ref=dst, send_sem=send_sem.at[number], recv_sem=recv_sem.at[number],
            device_id=peers[number], device_id_type=MESH,
        )
        copy.start()
        copies.append(copy)

    def stencil(facs, y, src, at):
        centre = src[at]

        def fac(i):
            return jnp.broadcast_to(facs[i, pl.ds(y, 1), :], (LP, NX))

        return (
            fac(0) * centre
            + fac(1) * pltpu.roll(centre, NX - 1, 1)
            + fac(2) * pltpu.roll(centre, 1, 1)
            + fac(3) * src[at + 1]
            + fac(4) * src[at - 1]
        )

    def rows(t, low, high, unroll):
        src, dst = (wide_a, wide_b) if t % 2 else (wide_b, wide_a)

        def row(y, _):
            dst[y] = stencil(fac_ref, y, src, y)
            return 0

        lax.fori_loop(low, high, row, 0, unroll=unroll)

    for t in range(1, 5):
        rows(t, HALO + t, NY + HALO - t, 8)

    for copy in copies:
        copy.wait()

    for near, from_side in ((0, from_west), (1, from_east)):
        below, above = corners[near], corners[near + 2]
        for h in range(LP // 16):
            at = pl.ds(16 * h, 16)

            def put(box, keep, corner, shift, at=at, from_side=from_side):
                box_rows = from_side[box, at, :]
                piece = pltpu.roll(corner, shift % NX, 1) if shift % NX else corner
                from_side[box, at, :] = jnp.where(keep, piece, box_rows)

            put(0, lane16 < 16, below, -16 * h)
            put(1, lane16 >= 120, above, 120 - 16 * h)
            put(2, (lane16 >= 96) & (lane16 < 104), above, 88 - 16 * h)
    for h in range(HALO):
        q = Q - HALO + h
        tips[h] = jnp.where((group == 0) & (place < 16), pltpu.roll(wide_a[h], 8, 1), tips[h])
        tips[q] = jnp.where((group == 3) & (place < 16), pltpu.roll(wide_a[q + 3 * Q], 104, 1), tips[q])
    for q in range(Q):
        row = tips[q]
        right = pltpu.roll(from_east[q // 8], (8 - 4 * (q % 8)) % NX, 1)
        left = pltpu.roll(from_west[q // 8], (16 - 4 * (q % 8)) % NX, 1)
        far = jnp.where((place >= 16) & (place < 20), left, pltpu.roll(row, 12, 1))
        strip_a[q + 1] = jnp.where(place < 8, row, jnp.where(place < 12, right, far))

    for t in range(1, 5):
        rows(t, t, HALO + t, 4)
        rows(t, NY + HALO - t, NY + 2 * HALO - t, 4)
    for t in range(4):
        src, dst = (strip_a, strip_b) if t % 2 == 0 else (strip_b, strip_a)
        src[0] = pltpu.roll(src[Q], 32, 1)
        src[Q + 1] = pltpu.roll(src[1], NX - 32, 1)

        def strip(q, _):
            dst[q + 1] = stencil(strip_ref, q, src, q + 1)
            return 0

        lax.fori_loop(0, Q, strip, 0, unroll=9)

    edge = (lane < HALO) | (lane >= NX - HALO)

    def write(low, high, parts):
        def one(q, _):
            row = strip_a[q + 1]
            row = jnp.where(place < 8, row, pltpu.roll(row, NX - 12, 1))
            for j in parts:
                y = q + Q * j
                whole = jnp.where(edge, pltpu.roll(row, (120 - 32 * j) % NX, 1), wide_a[y])
                out_ref[pl.ds(y - HALO, LEV, stride=NY), :] = whole[:LEV]
            return 0

        lax.fori_loop(low, high, one, 0, unroll=4)

    write(0, HALO, (1, 2, 3))
    write(HALO, Q - HALO, (0, 1, 2, 3))
    write(Q - HALO, Q, (0, 1, 2))


def spread(field, fac_main, fac_strip):
    vm = pl.BlockSpec(memory_space=pltpu.VMEM)
    wide = pltpu.VMEM((YE, LP, NX), F32)
    strip = pltpu.VMEM((Q + 2, LP, NX), F32)
    box = pltpu.VMEM((3, LP, NX), F32)
    return pl.pallas_call(
        spread_body,
        out_shape=jax.ShapeDtypeStruct((LEV * NY, NX), F32),
        in_specs=[pl.BlockSpec(memory_space=pl.ANY), vm, vm],
        out_specs=vm,
        scratch_shapes=[
            wide, wide, pltpu.VMEM((Q, LP, NX), F32), strip, strip, box, box, box, box,
            pltpu.VMEM((4, 16, NX), F32),
            pltpu.VMEM((4, 16, NX), F32),
            pltpu.SemaphoreType.DMA(()),
            pltpu.SemaphoreType.DMA((8,)),
            pltpu.SemaphoreType.DMA((8,)),
        ],
        compiler_params=pltpu.CompilerParams(
            collective_id=1, has_side_effects=True, vmem_limit_bytes=24 << 20
        ),
        name="spread",
    )(field, fac_main, fac_strip)


def local(
    forcing, obs_values, obs_owner, obs_cell, obs_count,
    coef_east, coef_north, area_inv, sea_mask, vert_coef, inv_thick,
):
    coefs = (coef_east, coef_north, area_inv, sea_mask)
    full, cells, fac_main, fac_strip, matrix, *sums = send_profiles(
        obs_count, vert_coef, inv_thick, obs_owner, obs_values, obs_cell, coefs
    )
    field = add_profiles(full, cells, forcing, matrix, sums)
    return spread(field, fac_main, fac_strip).reshape(LEV, NY, NX)


def solution(mesh):
    lead = P(("lon", "lat"))
    flat = P("lat", "lon")
    in_specs = (
        P(None, "lat", "lon"), P(None, ("lon", "lat")), lead, lead, lead,
        flat, flat, flat, flat, P(), P(),
    )
    return jax.shard_map(
        local, mesh=mesh, in_specs=in_specs, out_specs=P(None, "lat", "lon"), check_vma=False
    )
```
